128 devices in a mesh: wide: 8 (over y, z_hi), narrow: 16 (over z_lo, x, core).
Axes of the slice: x: 4, y: 4, z: 4 (z_hi: 2, z_lo: 2; z = z_hi * 2 + z_lo), core: 2. Of those that a mesh axis runs over, the one named last changes fastest.
Arguments:
- hidden_pre: bfloat16 [32, 256, 256, 256], P(None, 'wide', 'narrow'), may hold values from -6 to 6
- cotangent: bfloat16 [32, 256, 256, 256], P(None, 'wide', 'narrow'), may hold values from -6 to 6
- mode_weight: bfloat16 [32, 32, 32, 1024], P('narrow', 'wide'), may hold values from -6 to 6
- skip_weight: bfloat16 [32, 32], replicated, may hold values from -1 to 1
Outputs:
- grad_hidden: bfloat16 [32, 256, 256, 256], P(None, 'wide', 'narrow')
- grad_modes: float32 [32, 32, 32, 1024], P('narrow', 'wide')
- grad_skip: float32 [32, 32], replicated
The draws below stay inside these ranges and needn't reach their ends.
All inputs are finite; a program needn't handle non-finite values.
Results may differ from the reference program's by a relative error of at most 0.0087.
Values may be sent and summed in bfloat16 or wider, within the bound.
A program may use at most 128 MiB of HBM per device.

```python
import math
import jax
import jax.numpy as jnp
from jax import lax

C = 32
M = 32
NX = 256
NY = 256
NZ = 256


def block_scale(rng, dims, shards, low, largest):
    gain, own = 1.0, jax.random.fold_in(rng, 6)
    for axis_at, parts in shards:
        heights = jnp.exp(jax.random.uniform(jax.random.fold_in(own, axis_at), (parts,), jnp.float32, low / len(shards), largest / len(shards)))
        gain = gain * jnp.repeat(heights, dims[axis_at] // parts).reshape([-1 if axis == axis_at else 1 for axis in range(len(dims))])
    return gain


def bell_draw(rng, extent, deviation, reach, pieces=(), kind=jnp.bfloat16):
    drawn = jax.random.normal(rng, extent, jnp.float32) * deviation
    if len(pieces) > 0:
        drawn = block_scale(rng, extent, pieces, -0.22, 0.18) * drawn
    return jnp.clip(drawn, min=-reach, max=reach).astype(kind)


def setup_inputs(seed: int = 0) -> dict:
    streams_of = jax.random.split(jax.random.key(seed), 5)
    return {
        "hidden_pre": bell_draw(streams_of[0], (C, NX, NY, NZ), 1.0, 6.0, ((1, 8), (2, 16))),
        "cotangent": bell_draw(streams_of[1], (C, NX, NY, NZ), 1.0, 6.0, ((1, 8), (2, 16))),
        "mode_weight": bell_draw(streams_of[2], (M, M, M, C * C), 1.0, 6.0, ((0, 16), (1, 8))),
        "skip_weight": bell_draw(streams_of[3], (C, C), C ** -0.5, 1.0),
    }


def basis_table(mode_count, length):
    mode_index = jnp.arange(mode_count, dtype=jnp.int32)
    halfway = mode_count // 2
    frequency = jnp.where(mode_index < halfway, mode_index, mode_index - halfway + 1)
    points = jnp.arange(length, dtype=jnp.int32)
    phases = frequency[:, None] * points[None, :] % length
    angles = phases.astype(jnp.float32) * (2.0 * math.pi / length)
    values_table = jnp.where((mode_index < halfway)[:, None], jnp.cos(angles), jnp.sin(angles))
    return (values_table * (1.0 / math.sqrt(length))).astype(jnp.bfloat16)

def reference(hidden_pre, cotangent, mode_weight, skip_weight):
    highest = lax.Precision.HIGHEST
    table_x = basis_table(M, NX)
    table_y = basis_table(M, NY)
    table_z = basis_table(M, NZ)

    def analyse(channel_grid):
        zcoeffs = jnp.dot(channel_grid.reshape(NX * NY, NZ), table_z.T, preferred_element_type=jnp.float32)
        zcoeffs = zcoeffs.astype(jnp.bfloat16).reshape(NX, NY, M)
        ycoeffs = jnp.einsum('xym,ny->xnm', zcoeffs.astype(jnp.float32), table_y.astype(jnp.float32), precision=highest)
        ycoeffs = ycoeffs.astype(jnp.bfloat16)
        return jnp.einsum('xnm,kx->knm', ycoeffs.astype(jnp.float32), table_x.astype(jnp.float32), precision=highest)

    def synthesize(channel_spec):
        xsynth = jnp.einsum('knm,kx->xnm', channel_spec.astype(jnp.float32), table_x.astype(jnp.float32), precision=highest)
        xsynth = xsynth.astype(jnp.bfloat16)
        ysynth = jnp.einsum('xnm,ny->xym', xsynth.astype(jnp.float32), table_y.astype(jnp.float32), precision=highest)
        ysynth = ysynth.astype(jnp.bfloat16)
        spectral = jnp.dot(ysynth.reshape(NX * NY, M), table_z, preferred_element_type=jnp.float32)
        return spectral.astype(jnp.bfloat16).reshape(NX, NY, NZ)
    layer_in = lax.map(lambda grid: jnp.tanh(grid.astype(jnp.float32)).astype(jnp.bfloat16), hidden_pre)
    forward_s = lax.map(analyse, layer_in)
    adjoint_q = lax.map(analyse, cotangent)
    s_modes = jnp.transpose(forward_s, (3, 2, 1, 0))
    q_modes = jnp.transpose(adjoint_q, (3, 2, 1, 0))
    grad_modes = (s_modes[..., :, None] * q_modes[..., None, :]).reshape(M, M, M, C * C)
    weights_five = mode_weight.reshape(M, M, M, C, C).astype(jnp.float32)
    back_modes = jnp.einsum('zykco,zyko->zykc', weights_five, q_modes, precision=highest)
    back_spec = jnp.transpose(back_modes, (3, 2, 1, 0)).astype(jnp.bfloat16)
    spectral = lax.map(synthesize, back_spec)
    skip_f = skip_weight.astype(jnp.float32)

    def slab_step(total, position):
        hidden_slab = lax.dynamic_slice_in_dim(hidden_pre, position, 1, 1)[:, 0]
        cot_slab = lax.dynamic_slice_in_dim(cotangent, position, 1, 1)[:, 0].astype(jnp.float32)
        spec_slab = lax.dynamic_slice_in_dim(spectral, position, 1, 1)[:, 0].astype(jnp.float32)
        activ = jnp.tanh(hidden_slab.astype(jnp.float32))
        input_slab = activ.astype(jnp.bfloat16).astype(jnp.float32)
        grad_in = spec_slab + jnp.einsum('co,oyz->cyz', skip_f, cot_slab, precision=highest)
        grad_slab = (grad_in * (1.0 - activ * activ)).astype(jnp.bfloat16)
        total = total + jnp.einsum('cyz,oyz->co', input_slab, cot_slab, precision=highest)
        return (total, grad_slab)
    start = jnp.zeros((C, C), jnp.float32)
    total, slabs = lax.scan(slab_step, start, jnp.arange(NX, dtype=jnp.int32))
    grad_hidden = jnp.transpose(slabs, (1, 0, 2, 3))
    grad_skip = total * (1.0 / math.sqrt(NX * NY * NZ))
    return (grad_hidden, grad_modes, grad_skip)
```

```python
import math

import jax
import jax.numpy as jnp
from jax import lax
from jax.experimental import pallas as pl
from jax.experimental.pallas import tpu as pltpu
from jax.sharding import PartitionSpec as P

NX = 256
NY = 256
NZ = 256
XB = 8


def basis_table(mode_count, length):
    mode_index = jnp.arange(mode_count, dtype=jnp.int32)
    halfway = mode_count // 2
    frequency = jnp.where(mode_index < halfway, mode_index, mode_index - halfway + 1)
    points = jnp.arange(length, dtype=jnp.int32)
    phases = frequency[:, None] * points[None, :] % length
    angles = phases.astype(jnp.float32) * (2.0 * math.pi / length)
    values_table = jnp.where((mode_index < halfway)[:, None], jnp.cos(angles), jnp.sin(angles))
    return (values_table * (1.0 / math.sqrt(length))).astype(jnp.bfloat16)


def _nt(a, b):
    return lax.dot_general(a, b, (((1,), (1,)), ((), ())), preferred_element_type=jnp.float32)


def analysis_kernel(h_ref, g_ref, tz_ref, zc_ref, gram_ref, acc_ref):
    step = pl.program_id(0)
    channels, xb, ny, nz = h_ref.shape

    @pl.when(step == 0)
    def _():
        acc_ref[...] = jnp.zeros_like(acc_ref)

    tz = tz_ref[...]
    li = jnp.tanh(h_ref[...].astype(jnp.float32)).astype(jnp.bfloat16)
    g = g_ref[...]
    width = xb * ny
    zl = _nt(tz, li.reshape(channels * width, nz))
    zg = _nt(tz, g.reshape(channels * width, nz))
    for c in range(channels):
        zc_ref[c] = zl[:, c * width:(c + 1) * width].astype(jnp.bfloat16)
        zc_ref[channels + c] = zg[:, c * width:(c + 1) * width].astype(jnp.bfloat16)
    for x in range(xb):
        acc_ref[...] += _nt(li[:, x].reshape(channels * ny, nz), g[:, x].reshape(channels * ny, nz))

    @pl.when(step == pl.num_programs(0) - 1)
    def _():
        gram_ref[...] = acc_ref[...]


def analysis(hidden_pre, cotangent, table_z):
    channels, nx, ny, nz = hidden_pre.shape
    modes = table_z.shape[0]
    steps = nx // XB
    field_spec = pl.BlockSpec((channels, XB, ny, nz), lambda i: (0, i, 0, 0))
    return pl.pallas_call(
        analysis_kernel,
        grid=(steps,),
        in_specs=[field_spec, field_spec, pl.BlockSpec((modes, nz), lambda i: (0, 0))],
        out_specs=[
            pl.BlockSpec((2 * channels, modes, XB * ny), lambda i: (0, 0, i)),
            pl.BlockSpec((channels * ny, channels * ny), lambda i: (0, 0)),
        ],
        out_shape=[
            jax.ShapeDtypeStruct((2 * channels, modes, nx * ny), jnp.bfloat16),
            jax.ShapeDtypeStruct((channels * ny, channels * ny), jnp.float32),
        ],
        scratch_shapes=[pltpu.VMEM((channels * ny, channels * ny), jnp.float32)],
        compiler_params=pltpu.CompilerParams(
            dimension_semantics=("arbitrary",), vmem_limit_bytes=60 * 1024 * 1024
        ),
    )(hidden_pre, cotangent, table_z)


def synthesis_kernel(h_ref, g_ref, ys_ref, tz_ref, ks_ref, out_ref):
    channels, xb, ny, nz = h_ref.shape
    tz = tz_ref[...]
    ks = ks_ref[...]
    for x in range(xb):
        spec = jnp.dot(ys_ref[x], tz, preferred_element_type=jnp.float32)
        spec = spec.astype(jnp.bfloat16).astype(jnp.float32)
        skip = jnp.dot(ks, g_ref[:, x].reshape(channels * ny, nz), preferred_element_type=jnp.float32)
        activ = jnp.tanh(h_ref[:, x].astype(jnp.float32)).reshape(channels * ny, nz)
        grad = (spec + skip) * (1.0 - activ * activ)
        out_ref[:, x] = grad.astype(jnp.bfloat16).reshape(channels, ny, nz)


def synthesis(hidden_pre, cotangent, ysynth, table_z, kron_skip):
    channels, nx, ny, nz = hidden_pre.shape
    modes = table_z.shape[0]
    steps = nx // XB
    field_spec = pl.BlockSpec((channels, XB, ny, nz), lambda i: (0, i, 0, 0))
    return pl.pallas_call(
        synthesis_kernel,
        grid=(steps,),
        in_specs=[
            field_spec,
            field_spec,
            pl.BlockSpec((XB, channels * ny, modes), lambda i: (i, 0, 0)),
            pl.BlockSpec((modes, nz), lambda i: (0, 0)),
            pl.BlockSpec((channels * ny, channels * ny), lambda i: (0, 0)),
        ],
        out_specs=field_spec,
        out_shape=jax.ShapeDtypeStruct(hidden_pre.shape, jnp.bfloat16),
        compiler_params=pltpu.CompilerParams(
            dimension_semantics=("arbitrary",), vmem_limit_bytes=60 * 1024 * 1024
        ),
    )(hidden_pre, cotangent, ysynth, table_z, kron_skip)


def per_device(hidden_pre, cotangent, mode_weight, skip_weight):
    highest = lax.Precision.HIGHEST
    channels, nx, ny, nz = hidden_pre.shape
    mode_count = mode_weight.shape[2]
    n_narrow = lax.axis_size("narrow")
    n_wide = lax.axis_size("wide")
    table_x = basis_table(mode_count, NX)
    table_y = basis_table(mode_count, NY)
    table_z = basis_table(mode_count, NZ)

    zc, gram = analysis(hidden_pre, cotangent, table_z)
    zc = zc.reshape(2 * channels, mode_count, nx, ny)
    zc = lax.all_to_all(zc, "narrow", split_axis=1, concat_axis=3, tiled=True)
    ycoeffs = jnp.einsum(
        "cmxy,ny->mcnx", zc, table_y, preferred_element_type=jnp.float32
    ).astype(jnp.bfloat16)
    ycoeffs = lax.all_to_all(ycoeffs, "wide", split_axis=2, concat_axis=3, tiled=True)
    spectra = jnp.einsum("zcyx,kx->zcyk", ycoeffs, table_x, preferred_element_type=jnp.float32)
    s_modes = jnp.transpose(spectra[:, :channels], (0, 2, 3, 1))
    q_modes = jnp.transpose(spectra[:, channels:], (0, 2, 3, 1))
    z_local, y_local = (s_modes.shape[0], s_modes.shape[1])
    grad_modes = (s_modes[..., :, None] * q_modes[..., None, :]).reshape(
        z_local, y_local, mode_count, channels * channels
    )
    weights_five = mode_weight.reshape(z_local, y_local, mode_count, channels, channels).astype(
        jnp.float32
    )
    back_spec = jnp.einsum("zykco,zyko->zcyk", weights_five, q_modes, precision=highest).astype(
        jnp.bfloat16
    )
    xsynth = jnp.einsum(
        "zcyk,kx->zcyx", back_spec, table_x, preferred_element_type=jnp.float32
    ).astype(jnp.bfloat16)
    xsynth = lax.all_to_all(xsynth, "wide", split_axis=3, concat_axis=2, tiled=True)
    ysynth = jnp.einsum(
        "zcnx,ny->xcyz", xsynth, table_y, preferred_element_type=jnp.float32
    ).astype(jnp.bfloat16)
    ysynth = lax.all_to_all(ysynth, "narrow", split_axis=2, concat_axis=3, tiled=True)
    ysynth = ysynth.reshape(nx, channels * ny, mode_count)
    kron_skip = jnp.kron(skip_weight, jnp.eye(ny, dtype=skip_weight.dtype))
    grad_hidden = synthesis(hidden_pre, cotangent, ysynth, table_z, kron_skip)

    diag = jnp.eye(ny, dtype=jnp.float32)
    local_terms = (gram.reshape(channels, ny, channels, ny) * diag[None, :, None, :]).sum((1, 3))
    grad_skip = lax.psum(local_terms, ("wide", "narrow")) * (1.0 / math.sqrt(NX * NY * NZ))
    del n_narrow, n_wide
    return (grad_hidden, grad_modes, grad_skip)


def solution(mesh):
    in_specs = (
        P(None, "wide", "narrow", None),
        P(None, "wide", "narrow", None),
        P("narrow", "wide", None, None),
        P(),
    )
    out_specs = (P(None, "wide", "narrow", None), P("narrow", "wide", None, None), P())
    return jax.shard_map(
        per_device, mesh=mesh, in_specs=in_specs, out_specs=out_specs, check_vma=False
    )
```

```python
import math

import jax
import jax.numpy as jnp
from jax import lax
from jax.experimental import pallas as pl
from jax.experimental.pallas import tpu as pltpu
from jax.sharding import PartitionSpec as P

NX = 256
NY = 256
NZ = 256
XB = 8


def basis_table(mode_count, length):
    mode_index = jnp.arange(mode_count, dtype=jnp.int32)
    halfway = mode_count // 2
    frequency = jnp.where(mode_index < halfway, mode_index, mode_index - halfway + 1)
    points = jnp.arange(length, dtype=jnp.int32)
    phases = frequency[:, None] * points[None, :] % length
    angles = phases.astype(jnp.float32) * (2.0 * math.pi / length)
    values_table = jnp.where((mode_index < halfway)[:, None], jnp.cos(angles), jnp.sin(angles))
    return (values_table * (1.0 / math.sqrt(length))).astype(jnp.bfloat16)


def _nt(a, b):
    return lax.dot_general(a, b, (((1,), (1,)), ((), ())), preferred_element_type=jnp.float32)


def analysis_kernel(h_ref, g_ref, tz_ref, zc_ref, gram_ref, acc_ref):
    step = pl.program_id(0)
    channels, xb, ny, nz = h_ref.shape

    @pl.when(step == 0)
    def _():
        acc_ref[...] = jnp.zeros_like(acc_ref)

    tz = tz_ref[...]
    li = jnp.tanh(h_ref[...].astype(jnp.float32)).astype(jnp.bfloat16)
    g = g_ref[...]
    width = xb * ny
    zl = _nt(tz, li.reshape(channels * width, nz))
    zg = _nt(tz, g.reshape(channels * width, nz))
    for c in range(channels):
        zc_ref[c] = zl[:, c * width:(c + 1) * width].astype(jnp.bfloat16)
        zc_ref[channels + c] = zg[:, c * width:(c + 1) * width].astype(jnp.bfloat16)
    for x in range(xb):
        acc_ref[...] += _nt(li[:, x].reshape(channels * ny, nz), g[:, x].reshape(channels * ny, nz))

    @pl.when(step == pl.num_programs(0) - 1)
    def _():
        gram_ref[...] = acc_ref[...]


def analysis(hidden_pre, cotangent, table_z):
    channels, nx, ny, nz = hidden_pre.shape
    modes = table_z.shape[0]
    steps = nx // XB
    field_spec = pl.BlockSpec((channels, XB, ny, nz), lambda i: (0, i, 0, 0))
    return pl.pallas_call(
        analysis_kernel,
        grid=(steps,),
        in_specs=[field_spec, field_spec, pl.BlockSpec((modes, nz), lambda i: (0, 0))],
        out_specs=[
            pl.BlockSpec((2 * channels, modes, XB * ny), lambda i: (0, 0, i)),
            pl.BlockSpec((channels * ny, channels * ny), lambda i: (0, 0)),
        ],
        out_shape=[
            jax.ShapeDtypeStruct((2 * channels, modes, nx * ny), jnp.bfloat16),
            jax.ShapeDtypeStruct((channels * ny, channels * ny), jnp.float32),
        ],
        scratch_shapes=[pltpu.VMEM((channels * ny, channels * ny), jnp.float32)],
        compiler_params=pltpu.CompilerParams(
            dimension_semantics=("arbitrary",), vmem_limit_bytes=60 * 1024 * 1024
        ),
    )(hidden_pre, cotangent, table_z)


def synthesis_kernel(h_ref, g_ref, ys_ref, tz_ref, sw_ref, out_ref, ks_ref):
    channels, xb, ny, nz = h_ref.shape
    rows = channels * ny

    @pl.when(pl.program_id(0) == 0)
    def _():
        r = lax.broadcasted_iota(jnp.int32, (rows, channels), 0)
        k = lax.broadcasted_iota(jnp.int32, (rows, channels), 1)
        expand = (r // ny == k).astype(jnp.float32)
        spread = jnp.dot(expand, sw_ref[...].astype(jnp.float32), preferred_element_type=jnp.float32)
        kr = lax.broadcasted_iota(jnp.int32, (channels, rows), 0)
        kc = lax.broadcasted_iota(jnp.int32, (channels, rows), 1)
        expand_t = (kc // ny == kr).astype(jnp.float32)
        full = jnp.dot(spread, expand_t, preferred_element_type=jnp.float32)
        ri = lax.broadcasted_iota(jnp.int32, (rows, rows), 0)
        ci = lax.broadcasted_iota(jnp.int32, (rows, rows), 1)
        ks_ref[...] = jnp.where(ri % ny == ci % ny, full, 0.0).astype(ks_ref.dtype)

    tz = tz_ref[...]
    ks = ks_ref[...]
    for x in range(xb):
        spec = jnp.dot(ys_ref[x], tz, preferred_element_type=jnp.float32)
        spec = spec.astype(jnp.bfloat16).astype(jnp.float32)
        skip = jnp.dot(ks, g_ref[:, x].reshape(channels * ny, nz), preferred_element_type=jnp.float32)
        activ = jnp.tanh(h_ref[:, x].astype(jnp.float32)).reshape(channels * ny, nz)
        grad = (spec + skip) * (1.0 - activ * activ)
        out_ref[:, x] = grad.astype(jnp.bfloat16).reshape(channels, ny, nz)


def synthesis(hidden_pre, cotangent, ysynth, table_z, skip_weight):
    channels, nx, ny, nz = hidden_pre.shape
    modes = table_z.shape[0]
    steps = nx // XB
    field_spec = pl.BlockSpec((channels, XB, ny, nz), lambda i: (0, i, 0, 0))
    return pl.pallas_call(
        synthesis_kernel,
        grid=(steps,),
        in_specs=[
            field_spec,
            field_spec,
            pl.BlockSpec((XB, channels * ny, modes), lambda i: (i, 0, 0)),
            pl.BlockSpec((modes, nz), lambda i: (0, 0)),
            pl.BlockSpec((channels, channels), lambda i: (0, 0)),
        ],
        out_specs=field_spec,
        out_shape=jax.ShapeDtypeStruct(hidden_pre.shape, jnp.bfloat16),
        scratch_shapes=[pltpu.VMEM((channels * ny, channels * ny), jnp.bfloat16)],
        compiler_params=pltpu.CompilerParams(
            dimension_semantics=("arbitrary",), vmem_limit_bytes=60 * 1024 * 1024
        ),
    )(hidden_pre, cotangent, ysynth, table_z, skip_weight)


def per_device(hidden_pre, cotangent, mode_weight, skip_weight):
    highest = lax.Precision.HIGHEST
    channels, nx, ny, nz = hidden_pre.shape
    mode_count = mode_weight.shape[2]
    n_narrow = lax.axis_size("narrow")
    n_wide = lax.axis_size("wide")
    table_x = basis_table(mode_count, NX)
    table_y = basis_table(mode_count, NY)
    table_z = basis_table(mode_count, NZ)

    zc, gram = analysis(hidden_pre, cotangent, table_z)
    zc = zc.reshape(2 * channels, mode_count, nx, ny)
    zc = lax.all_to_all(zc, "narrow", split_axis=1, concat_axis=3, tiled=True)
    ycoeffs = jnp.einsum(
        "cmxy,ny->mcnx", zc, table_y, preferred_element_type=jnp.float32
    ).astype(jnp.bfloat16)
    ycoeffs = lax.all_to_all(ycoeffs, "wide", split_axis=2, concat_axis=3, tiled=True)
    spectra = jnp.einsum("zcyx,kx->zcyk", ycoeffs, table_x, preferred_element_type=jnp.float32)
    s_modes = jnp.transpose(spectra[:, :channels], (0, 2, 3, 1))
    q_modes = jnp.transpose(spectra[:, channels:], (0, 2, 3, 1))
    z_local, y_local = (s_modes.shape[0], s_modes.shape[1])
    grad_modes = (s_modes[..., :, None] * q_modes[..., None, :]).reshape(
        z_local, y_local, mode_count, channels * channels
    )
    weights_five = mode_weight.reshape(z_local, y_local, mode_count, channels, channels).astype(
        jnp.float32
    )
    back_spec = jnp.einsum("zykco,zyko->zcyk", weights_five, q_modes, precision=highest).astype(
        jnp.bfloat16
    )
    xsynth = jnp.einsum(
        "zcyk,kx->zcyx", back_spec, table_x, preferred_element_type=jnp.float32
    ).astype(jnp.bfloat16)
    xsynth = lax.all_to_all(xsynth, "wide", split_axis=3, concat_axis=2, tiled=True)
    ysynth = jnp.einsum(
        "zcnx,ny->xcyz", xsynth, table_y, preferred_element_type=jnp.float32
    ).astype(jnp.bfloat16)
    ysynth = lax.all_to_all(ysynth, "narrow", split_axis=2, concat_axis=3, tiled=True)
    ysynth = ysynth.reshape(nx, channels * ny, mode_count)
    grad_hidden = synthesis(hidden_pre, cotangent, ysynth, table_z, skip_weight)

    diag = jnp.eye(ny, dtype=jnp.float32)
    local_terms = (gram.reshape(channels, ny, channels, ny) * diag[None, :, None, :]).sum((1, 3))
    total = local_terms.reshape(1, channels * channels)
    for axis, count in (("narrow", n_narrow), ("wide", n_wide)):
        spread = jnp.broadcast_to(total, (count, channels * channels))
        total = lax.all_to_all(spread, axis, 0, 0, tiled=True).sum(0, keepdims=True)
    grad_skip = total.reshape(channels, channels) * (1.0 / math.sqrt(NX * NY * NZ))
    return (grad_hidden, grad_modes, grad_skip)


def solution(mesh):
    in_specs = (
        P(None, "wide", "narrow", None),
        P(None, "wide", "narrow", None),
        P("narrow", "wide", None, None),
        P(),
    )
    out_specs = (P(None, "wide", "narrow", None), P("narrow", "wide", None, None), P())
    return jax.shard_map(
        per_device, mesh=mesh, in_specs=in_specs, out_specs=out_specs, check_vma=False
    )
```

```python
import math

import jax
import jax.numpy as jnp
from jax import lax
from jax.experimental import pallas as pl
from jax.experimental.pallas import tpu as pltpu
from jax.sharding import PartitionSpec as P

NX = 256
NY = 256
NZ = 256
XB = 8


def basis_table(mode_count, length):
    mode_index = jnp.arange(mode_count, dtype=jnp.int32)
    halfway = mode_count // 2
    frequency = jnp.where(mode_index < halfway, mode_index, mode_index - halfway + 1)
    points = jnp.arange(length, dtype=jnp.int32)
    phases = frequency[:, None] * points[None, :] % length
    angles = phases.astype(jnp.float32) * (2.0 * math.pi / length)
    values_table = jnp.where((mode_index < halfway)[:, None], jnp.cos(angles), jnp.sin(angles))
    return (values_table * (1.0 / math.sqrt(length))).astype(jnp.bfloat16)


def _nt(a, b):
    return lax.dot_general(a, b, (((1,), (1,)), ((), ())), preferred_element_type=jnp.float32)


def analysis_kernel(h_ref, g_ref, tz_ref, zc_ref, gram_ref, acc_ref):
    step = pl.program_id(0)
    channels, xb, ny, nz = h_ref.shape

    @pl.when(step == 0)
    def _():
        acc_ref[...] = jnp.zeros_like(acc_ref)

    tz = tz_ref[...]
    li = jnp.tanh(h_ref[...].astype(jnp.float32)).astype(jnp.bfloat16)
    g = g_ref[...]
    width = xb * ny
    zl = _nt(tz, li.reshape(channels * width, nz))
    zg = _nt(tz, g.reshape(channels * width, nz))
    for c in range(channels):
        zc_ref[c] = zl[:, c * width:(c + 1) * width].astype(jnp.bfloat16)
        zc_ref[channels + c] = zg[:, c * width:(c + 1) * width].astype(jnp.bfloat16)
    for x in range(xb):
        acc_ref[...] += _nt(li[:, x].reshape(channels * ny, nz), g[:, x].reshape(channels * ny, nz))

    @pl.when(step == pl.num_programs(0) - 1)
    def _():
        rows = channels * ny
        ri = lax.broadcasted_iota(jnp.int32, (rows, rows), 0)
        ci = lax.broadcasted_iota(jnp.int32, (rows, rows), 1)
        diag = jnp.where(ri % ny == ci % ny, acc_ref[...], 0.0)
        er = lax.broadcasted_iota(jnp.int32, (channels, rows), 0)
        ec = lax.broadcasted_iota(jnp.int32, (channels, rows), 1)
        gather = (ec // ny == er).astype(jnp.float32)
        part = jnp.dot(gather, diag, precision=lax.Precision.HIGHEST, preferred_element_type=jnp.float32)
        gram_ref[...] = lax.dot_general(
            part, gather, (((1,), (1,)), ((), ())), precision=lax.Precision.HIGHEST,
            preferred_element_type=jnp.float32)


def analysis(hidden_pre, cotangent, table_z):
    channels, nx, ny, nz = hidden_pre.shape
    modes = table_z.shape[0]
    steps = nx // XB
    field_spec = pl.BlockSpec((channels, XB, ny, nz), lambda i: (0, i, 0, 0))
    return pl.pallas_call(
        analysis_kernel,
        grid=(steps,),
        in_specs=[field_spec, field_spec, pl.BlockSpec((modes, nz), lambda i: (0, 0))],
        out_specs=[
            pl.BlockSpec((2 * channels, modes, XB * ny), lambda i: (0, 0, i)),
            pl.BlockSpec((channels, channels), lambda i: (0, 0)),
        ],
        out_shape=[
            jax.ShapeDtypeStruct((2 * channels, modes, nx * ny), jnp.bfloat16),
            jax.ShapeDtypeStruct((channels, channels), jnp.float32),
        ],
        scratch_shapes=[pltpu.VMEM((channels * ny, channels * ny), jnp.float32)],
        compiler_params=pltpu.CompilerParams(
            dimension_semantics=("arbitrary",), vmem_limit_bytes=60 * 1024 * 1024
        ),
    )(hidden_pre, cotangent, table_z)


def synthesis_kernel(h_ref, g_ref, ys_ref, tz_ref, sw_ref, out_ref, ks_ref):
    channels, xb, ny, nz = h_ref.shape
    rows = channels * ny

    @pl.when(pl.program_id(0) == 0)
    def _():
        r = lax.broadcasted_iota(jnp.int32, (rows, channels), 0)
        k = lax.broadcasted_iota(jnp.int32, (rows, channels), 1)
        expand = (r // ny == k).astype(jnp.float32)
        spread = jnp.dot(expand, sw_ref[...].astype(jnp.float32), preferred_element_type=jnp.float32)
        kr = lax.broadcasted_iota(jnp.int32, (channels, rows), 0)
        kc = lax.broadcasted_iota(jnp.int32, (channels, rows), 1)
        expand_t = (kc // ny == kr).astype(jnp.float32)
        full = jnp.dot(spread, expand_t, preferred_element_type=jnp.float32)
        ri = lax.broadcasted_iota(jnp.int32, (rows, rows), 0)
        ci = lax.broadcasted_iota(jnp.int32, (rows, rows), 1)
        ks_ref[...] = jnp.where(ri % ny == ci % ny, full, 0.0).astype(ks_ref.dtype)

    tz = tz_ref[...]
    ks = ks_ref[...]
    for x in range(xb):
        spec = jnp.dot(ys_ref[x], tz, preferred_element_type=jnp.float32)
        spec = spec.astype(jnp.bfloat16).astype(jnp.float32)
        skip = jnp.dot(ks, g_ref[:, x].reshape(channels * ny, nz), preferred_element_type=jnp.float32)
        activ = jnp.tanh(h_ref[:, x].astype(jnp.float32)).reshape(channels * ny, nz)
        grad = (spec + skip) * (1.0 - activ * activ)
        out_ref[:, x] = grad.astype(jnp.bfloat16).reshape(channels, ny, nz)


def synthesis(hidden_pre, cotangent, ysynth, table_z, skip_weight):
    channels, nx, ny, nz = hidden_pre.shape
    modes = table_z.shape[0]
    steps = nx // XB
    field_spec = pl.BlockSpec((channels, XB, ny, nz), lambda i: (0, i, 0, 0))
    return pl.pallas_call(
        synthesis_kernel,
        grid=(steps,),
        in_specs=[
            field_spec,
            field_spec,
            pl.BlockSpec((XB, channels * ny, modes), lambda i: (i, 0, 0)),
            pl.BlockSpec((modes, nz), lambda i: (0, 0)),
            pl.BlockSpec((channels, channels), lambda i: (0, 0)),
        ],
        out_specs=field_spec,
        out_shape=jax.ShapeDtypeStruct(hidden_pre.shape, jnp.bfloat16),
        scratch_shapes=[pltpu.VMEM((channels * ny, channels * ny), jnp.bfloat16)],
        compiler_params=pltpu.CompilerParams(
            dimension_semantics=("arbitrary",), vmem_limit_bytes=60 * 1024 * 1024
        ),
    )(hidden_pre, cotangent, ysynth, table_z, skip_weight)


def modes_kernel(sp_ref, w_ref, gm_ref, bs_ref):
    highest = lax.Precision.HIGHEST
    channels = sp_ref.shape[1] // 2
    width = channels * channels
    sp = sp_ref[...]
    er = lax.broadcasted_iota(jnp.int32, (channels, width), 0)
    ec = lax.broadcasted_iota(jnp.int32, (channels, width), 1)
    spread = (ec // channels == er).astype(jnp.float32)
    tile = (ec % channels == er).astype(jnp.float32)
    s_rep = jnp.dot(sp[:, :channels], spread, precision=highest, preferred_element_type=jnp.float32)
    q_rep = jnp.dot(sp[:, channels:], tile, precision=highest, preferred_element_type=jnp.float32)
    gm_ref[...] = s_rep * q_rep
    weighted = w_ref[...].astype(jnp.float32) * q_rep
    back = lax.dot_general(
        weighted, spread, (((1,), (1,)), ((), ())), precision=highest,
        preferred_element_type=jnp.float32)
    bs_ref[...] = back.astype(bs_ref.dtype)


def modes_step(spectra, weights):
    rows, both = spectra.shape
    channels = both // 2
    vmem = pl.BlockSpec(memory_space=pltpu.VMEM)
    return pl.pallas_call(
        modes_kernel,
        in_specs=[vmem, vmem],
        out_specs=[vmem, vmem],
        out_shape=[
            jax.ShapeDtypeStruct((rows, channels * channels), jnp.float32),
            jax.ShapeDtypeStruct((rows, channels), jnp.bfloat16),
        ],
    )(spectra, weights)


def per_device(hidden_pre, cotangent, mode_weight, skip_weight):
    highest = lax.Precision.HIGHEST
    channels, nx, ny, nz = hidden_pre.shape
    mode_count = mode_weight.shape[2]
    n_narrow = lax.axis_size("narrow")
    n_wide = lax.axis_size("wide")
    table_x = basis_table(mode_count, NX)
    table_y = basis_table(mode_count, NY)
    table_z = basis_table(mode_count, NZ)

    zc, gram = analysis(hidden_pre, cotangent, table_z)
    zc = zc.reshape(2 * channels, mode_count, nx, ny)
    zc = lax.all_to_all(zc, "narrow", split_axis=1, concat_axis=3, tiled=True)
    ycoeffs = jnp.einsum(
        "cmxy,ny->mcnx", zc, table_y, preferred_element_type=jnp.float32
    ).astype(jnp.bfloat16)
    ycoeffs = lax.all_to_all(ycoeffs, "wide", split_axis=2, concat_axis=3, tiled=True)
    spectra = jnp.einsum("zcyx,kx->zykc", ycoeffs, table_x, preferred_element_type=jnp.float32)
    z_local, y_local = (spectra.shape[0], spectra.shape[1])
    grad_modes, back_spec = modes_step(
        spectra.reshape(z_local * y_local * mode_count, 2 * channels),
        mode_weight.reshape(z_local * y_local * mode_count, channels * channels),
    )
    grad_modes = grad_modes.reshape(z_local, y_local, mode_count, channels * channels)
    back_spec = jnp.transpose(
        back_spec.reshape(z_local, y_local, mode_count, channels), (0, 3, 1, 2)
    )
    xsynth = jnp.einsum(
        "zcyk,kx->zcyx", back_spec, table_x, preferred_element_type=jnp.float32
    ).astype(jnp.bfloat16)
    xsynth = lax.all_to_all(xsynth, "wide", split_axis=3, concat_axis=2, tiled=True)
    ysynth = jnp.einsum(
        "zcnx,ny->xcyz", xsynth, table_y, preferred_element_type=jnp.float32
    ).astype(jnp.bfloat16)
    ysynth = lax.all_to_all(ysynth, "narrow", split_axis=2, concat_axis=3, tiled=True)
    ysynth = ysynth.reshape(nx, channels * ny, mode_count)
    grad_hidden = synthesis(hidden_pre, cotangent, ysynth, table_z, skip_weight)

    total = gram.reshape(1, channels * channels)
    for axis, count in (("narrow", n_narrow), ("wide", n_wide)):
        spread = jnp.broadcast_to(total, (count, channels * channels))
        total = lax.all_to_all(spread, axis, 0, 0, tiled=True).sum(0, keepdims=True)
    grad_skip = total.reshape(channels, channels) * (1.0 / math.sqrt(NX * NY * NZ))
    return (grad_hidden, grad_modes, grad_skip)


def solution(mesh):
    in_specs = (
        P(None, "wide", "narrow", None),
        P(None, "wide", "narrow", None),
        P("narrow", "wide", None, None),
        P(),
    )
    out_specs = (P(None, "wide", "narrow", None), P("narrow", "wide", None, None), P())
    return jax.shard_map(
        per_device, mesh=mesh, in_specs=in_specs, out_specs=out_specs, check_vma=False
    )
```

```python
import math

import jax
import jax.numpy as jnp
from jax import lax
from jax.experimental import pallas as pl
from jax.experimental.pallas import tpu as pltpu
from jax.sharding import PartitionSpec as P

NX = 256
NY = 256
NZ = 256
XB = 8


def basis_table(mode_count, length):
    mode_index = jnp.arange(mode_count, dtype=jnp.int32)
    halfway = mode_count // 2
    frequency = jnp.where(mode_index < halfway, mode_index, mode_index - halfway + 1)
    points = jnp.arange(length, dtype=jnp.int32)
    phases = frequency[:, None] * points[None, :] % length
    angles = phases.astype(jnp.float32) * (2.0 * math.pi / length)
    values_table = jnp.where((mode_index < halfway)[:, None], jnp.cos(angles), jnp.sin(angles))
    return (values_table * (1.0 / math.sqrt(length))).astype(jnp.bfloat16)


def _nt(a, b):
    return lax.dot_general(a, b, (((1,), (1,)), ((), ())), preferred_element_type=jnp.float32)


def analysis_kernel(h_ref, g_ref, tz_ref, zc_ref, gram_ref, acc_ref):
    step = pl.program_id(0)
    channels, xb, ny, nz = h_ref.shape

    @pl.when(step == 0)
    def _():
        acc_ref[...] = jnp.zeros_like(acc_ref)

    tz = tz_ref[...]
    li = jnp.tanh(h_ref[...].astype(jnp.float32)).astype(jnp.bfloat16)
    g = g_ref[...]
    width = xb * ny
    zl = _nt(tz, li.reshape(channels * width, nz))
    zg = _nt(tz, g.reshape(channels * width, nz))
    for c in range(channels):
        zc_ref[c] = zl[:, c * width:(c + 1) * width].astype(jnp.bfloat16)
        zc_ref[channels + c] = zg[:, c * width:(c + 1) * width].astype(jnp.bfloat16)
    for x in range(xb):
        acc_ref[...] += _nt(li[:, x].reshape(channels * ny, nz), g[:, x].reshape(channels * ny, nz))

    @pl.when(step == pl.num_programs(0) - 1)
    def _():
        rows = channels * ny
        ri = lax.broadcasted_iota(jnp.int32, (rows, rows), 0)
        ci = lax.broadcasted_iota(jnp.int32, (rows, rows), 1)
        diag = jnp.where(ri % ny == ci % ny, acc_ref[...], 0.0)
        er = lax.broadcasted_iota(jnp.int32, (channels, rows), 0)
        ec = lax.broadcasted_iota(jnp.int32, (channels, rows), 1)
        gather = (ec // ny == er).astype(jnp.float32)
        part = jnp.dot(gather, diag, precision=lax.Precision.HIGHEST, preferred_element_type=jnp.float32)
        gram_ref[...] = lax.dot_general(
            part, gather, (((1,), (1,)), ((), ())), precision=lax.Precision.HIGHEST,
            preferred_element_type=jnp.float32)


def analysis(hidden_pre, cotangent, table_z):
    channels, nx, ny, nz = hidden_pre.shape
    modes = table_z.shape[0]
    steps = nx // XB
    field_spec = pl.BlockSpec((channels, XB, ny, nz), lambda i: (0, i, 0, 0))
    return pl.pallas_call(
        analysis_kernel,
        grid=(steps,),
        in_specs=[field_spec, field_spec, pl.BlockSpec((modes, nz), lambda i: (0, 0))],
        out_specs=[
            pl.BlockSpec((2 * channels, modes, XB * ny), lambda i: (0, 0, i)),
            pl.BlockSpec((channels, channels), lambda i: (0, 0)),
        ],
        out_shape=[
            jax.ShapeDtypeStruct((2 * channels, modes, nx * ny), jnp.bfloat16),
            jax.ShapeDtypeStruct((channels, channels), jnp.float32),
        ],
        scratch_shapes=[pltpu.VMEM((channels * ny, channels * ny), jnp.float32)],
        compiler_params=pltpu.CompilerParams(
            dimension_semantics=("arbitrary",), vmem_limit_bytes=60 * 1024 * 1024
        ),
    )(hidden_pre, cotangent, table_z)


def synthesis_kernel(h_ref, g_ref, ys_ref, tz_ref, sw_ref, out_ref, ks_ref):
    channels, xb, ny, nz = h_ref.shape
    rows = channels * ny

    @pl.when(pl.program_id(0) == 0)
    def _():
        r = lax.broadcasted_iota(jnp.int32, (rows, channels), 0)
        k = lax.broadcasted_iota(jnp.int32, (rows, channels), 1)
        expand = (r // ny == k).astype(jnp.float32)
        spread = jnp.dot(expand, sw_ref[...].astype(jnp.float32), preferred_element_type=jnp.float32)
        kr = lax.broadcasted_iota(jnp.int32, (channels, rows), 0)
        kc = lax.broadcasted_iota(jnp.int32, (channels, rows), 1)
        expand_t = (kc // ny == kr).astype(jnp.float32)
        full = jnp.dot(spread, expand_t, preferred_element_type=jnp.float32)
        ri = lax.broadcasted_iota(jnp.int32, (rows, rows), 0)
        ci = lax.broadcasted_iota(jnp.int32, (rows, rows), 1)
        ks_ref[...] = jnp.where(ri % ny == ci % ny, full, 0.0).astype(ks_ref.dtype)

    tz = tz_ref[...]
    ks = ks_ref[...]
    for x in range(xb):
        spec = jnp.dot(ys_ref[x], tz, preferred_element_type=jnp.float32)
        spec = spec.astype(jnp.bfloat16).astype(jnp.float32)
        skip = jnp.dot(ks, g_ref[:, x].reshape(channels * ny, nz), preferred_element_type=jnp.float32)
        activ = jnp.tanh(h_ref[:, x].astype(jnp.float32)).reshape(channels * ny, nz)
        grad = (spec + skip) * (1.0 - activ * activ)
        out_ref[:, x] = grad.astype(jnp.bfloat16).reshape(channels, ny, nz)


def synthesis(hidden_pre, cotangent, ysynth, table_z, skip_weight):
    channels, nx, ny, nz = hidden_pre.shape
    modes = table_z.shape[0]
    steps = nx // XB
    field_spec = pl.BlockSpec((channels, XB, ny, nz), lambda i: (0, i, 0, 0))
    return pl.pallas_call(
        synthesis_kernel,
        grid=(steps,),
        in_specs=[
            field_spec,
            field_spec,
            pl.BlockSpec((XB, channels * ny, modes), lambda i: (i, 0, 0)),
            pl.BlockSpec((modes, nz), lambda i: (0, 0)),
            pl.BlockSpec((channels, channels), lambda i: (0, 0)),
        ],
        out_specs=field_spec,
        out_shape=jax.ShapeDtypeStruct(hidden_pre.shape, jnp.bfloat16),
        scratch_shapes=[pltpu.VMEM((channels * ny, channels * ny), jnp.bfloat16)],
        compiler_params=pltpu.CompilerParams(
            dimension_semantics=("arbitrary",), vmem_limit_bytes=60 * 1024 * 1024
        ),
    )(hidden_pre, cotangent, ysynth, table_z, skip_weight)


def modes_kernel(sp_ref, w_ref, gm_ref, bs_ref):
    highest = lax.Precision.HIGHEST
    channels = sp_ref.shape[1] // 2
    width = channels * channels
    sp = sp_ref[...]
    er = lax.broadcasted_iota(jnp.int32, (channels, width), 0)
    ec = lax.broadcasted_iota(jnp.int32, (channels, width), 1)
    spread = (ec // channels == er).astype(jnp.float32)
    tile = (ec % channels == er).astype(jnp.float32)
    s_rep = jnp.dot(sp[:, :channels], spread, precision=highest, preferred_element_type=jnp.float32)
    q_rep = jnp.dot(sp[:, channels:], tile, precision=highest, preferred_element_type=jnp.float32)
    gm_ref[...] = s_rep * q_rep
    weighted = w_ref[...].astype(jnp.float32) * q_rep
    back = lax.dot_general(
        weighted, spread, (((1,), (1,)), ((), ())), precision=highest,
        preferred_element_type=jnp.float32)
    bs_ref[...] = back.astype(bs_ref.dtype)


def modes_step(spectra, weights):
    rows, both = spectra.shape
    channels = both // 2
    vmem = pl.BlockSpec(memory_space=pltpu.VMEM)
    return pl.pallas_call(
        modes_kernel,
        in_specs=[vmem, vmem],
        out_specs=[vmem, vmem],
        out_shape=[
            jax.ShapeDtypeStruct((rows, channels * channels), jnp.float32),
            jax.ShapeDtypeStruct((rows, channels), jnp.bfloat16),
        ],
    )(spectra, weights)


def per_device(hidden_pre, cotangent, mode_weight, skip_weight):
    highest = lax.Precision.HIGHEST
    channels, nx, ny, nz = hidden_pre.shape
    mode_count = mode_weight.shape[2]
    n_narrow = lax.axis_size("narrow")
    n_wide = lax.axis_size("wide")
    table_x = basis_table(mode_count, NX)
    table_y = basis_table(mode_count, NY)
    table_z = basis_table(mode_count, NZ)

    zc, gram = analysis(hidden_pre, cotangent, table_z)
    zc = zc.reshape(2 * channels, mode_count, nx, ny)
    zc = lax.all_to_all(zc, "narrow", split_axis=1, concat_axis=3, tiled=True)
    ycoeffs = jnp.einsum(
        "cmxy,ny->mcnx", zc, table_y, preferred_element_type=jnp.float32
    ).astype(jnp.bfloat16)
    ycoeffs = lax.all_to_all(ycoeffs, "wide", split_axis=2, concat_axis=3, tiled=True)
    spectra = jnp.einsum("zcyx,kx->zykc", ycoeffs, table_x, preferred_element_type=jnp.float32)
    z_local, y_local = (spectra.shape[0], spectra.shape[1])
    grad_modes, back_spec = modes_step(
        spectra.reshape(z_local * y_local * mode_count, 2 * channels),
        mode_weight.reshape(z_local * y_local * mode_count, channels * channels),
    )
    grad_modes = grad_modes.reshape(z_local, y_local, mode_count, channels * channels)
    back_spec = jnp.transpose(
        back_spec.reshape(z_local, y_local, mode_count, channels), (0, 3, 1, 2)
    )
    xsynth = jnp.einsum(
        "zcyk,kx->zcyx", back_spec, table_x, preferred_element_type=jnp.float32
    ).astype(jnp.bfloat16)
    xsynth = lax.all_to_all(xsynth, "wide", split_axis=3, concat_axis=2, tiled=True)
    xsynth = lax.all_gather(xsynth, "narrow", axis=0, tiled=True)
    me = lax.axis_index("narrow")
    table_y_local = lax.dynamic_slice_in_dim(table_y, me * ny, ny, axis=1)
    ysynth = jnp.einsum(
        "zcnx,ny->xcyz", xsynth, table_y_local, preferred_element_type=jnp.float32
    ).astype(jnp.bfloat16)
    ysynth = ysynth.reshape(nx, channels * ny, mode_count)
    grad_hidden = synthesis(hidden_pre, cotangent, ysynth, table_z, skip_weight)

    total = gram.reshape(1, channels * channels)
    for axis, count in (("narrow", n_narrow), ("wide", n_wide)):
        spread = jnp.broadcast_to(total, (count, channels * channels))
        total = lax.all_to_all(spread, axis, 0, 0, tiled=True).sum(0, keepdims=True)
    grad_skip = total.reshape(channels, channels) * (1.0 / math.sqrt(NX * NY * NZ))
    return (grad_hidden, grad_modes, grad_skip)


def solution(mesh):
    in_specs = (
        P(None, "wide", "narrow", None),
        P(None, "wide", "narrow", None),
        P("narrow", "wide", None, None),
        P(),
    )
    out_specs = (P(None, "wide", "narrow", None), P("narrow", "wide", None, None), P())
    return jax.shard_map(
        per_device, mesh=mesh, in_specs=in_specs, out_specs=out_specs, check_vma=False
    )
```

```python
import functools
import math

import jax
import jax.numpy as jnp
from jax import lax
from jax.experimental import pallas as pl
from jax.experimental.pallas import tpu as pltpu
from jax.sharding import PartitionSpec as P

NX = 256
NY = 256
NZ = 256
XB = 8


def basis_table(mode_count, length):
    mode_index = jnp.arange(mode_count, dtype=jnp.int32)
    halfway = mode_count // 2
    frequency = jnp.where(mode_index < halfway, mode_index, mode_index - halfway + 1)
    points = jnp.arange(length, dtype=jnp.int32)
    phases = frequency[:, None] * points[None, :] % length
    angles = phases.astype(jnp.float32) * (2.0 * math.pi / length)
    values_table = jnp.where((mode_index < halfway)[:, None], jnp.cos(angles), jnp.sin(angles))
    return (values_table * (1.0 / math.sqrt(length))).astype(jnp.bfloat16)


def _nt(a, b):
    return lax.dot_general(a, b, (((1,), (1,)), ((), ())), preferred_element_type=jnp.float32)


def analysis_kernel(h_ref, g_ref, tz_ref, zc_ref, gram_ref, acc_ref, stage_ref):
    step = pl.program_id(0)
    channels, xb, ny, nz = h_ref.shape

    @pl.when(step == 0)
    def _():
        acc_ref[...] = jnp.zeros_like(acc_ref)

    tz = tz_ref[...]
    li = jnp.tanh(h_ref[...].astype(jnp.float32)).astype(jnp.bfloat16)
    g = g_ref[...]
    width = xb * ny
    zl = _nt(tz, li.reshape(channels * width, nz))
    zg = _nt(tz, g.reshape(channels * width, nz))
    for c in range(channels):
        stage_ref[:, c, :] = zl[:, c * width:(c + 1) * width]
        stage_ref[:, channels + c, :] = zg[:, c * width:(c + 1) * width]
    zc_ref[...] = stage_ref[...].astype(jnp.bfloat16)
    for x in range(xb):
        acc_ref[...] += _nt(li[:, x].reshape(channels * ny, nz), g[:, x].reshape(channels * ny, nz))

    @pl.when(step == pl.num_programs(0) - 1)
    def _():
        rows = channels * ny
        ri = lax.broadcasted_iota(jnp.int32, (rows, rows), 0)
        ci = lax.broadcasted_iota(jnp.int32, (rows, rows), 1)
        diag = jnp.where(ri % ny == ci % ny, acc_ref[...], 0.0)
        er = lax.broadcasted_iota(jnp.int32, (channels, rows), 0)
        ec = lax.broadcasted_iota(jnp.int32, (channels, rows), 1)
        gather = (ec // ny == er).astype(jnp.float32)
        part = jnp.dot(gather, diag, precision=lax.Precision.HIGHEST, preferred_element_type=jnp.float32)
        gram_ref[...] = lax.dot_general(
            part, gather, (((1,), (1,)), ((), ())), precision=lax.Precision.HIGHEST,
            preferred_element_type=jnp.float32)


def analysis(hidden_pre, cotangent, table_z):
    channels, nx, ny, nz = hidden_pre.shape
    modes = table_z.shape[0]
    steps = nx // XB
    field_spec = pl.BlockSpec((channels, XB, ny, nz), lambda i: (0, i, 0, 0))
    return pl.pallas_call(
        analysis_kernel,
        grid=(steps,),
        in_specs=[field_spec, field_spec, pl.BlockSpec((modes, nz), lambda i: (0, 0))],
        out_specs=[
            pl.BlockSpec((modes, 2 * channels, XB * ny), lambda i: (0, 0, i)),
            pl.BlockSpec((channels, channels), lambda i: (0, 0)),
        ],
        out_shape=[
            jax.ShapeDtypeStruct((modes, 2 * channels, nx * ny), jnp.bfloat16),
            jax.ShapeDtypeStruct((channels, channels), jnp.float32),
        ],
        scratch_shapes=[
            pltpu.VMEM((channels * ny, channels * ny), jnp.float32),
            pltpu.VMEM((modes, 2 * channels, XB * ny), jnp.float32),
        ],
        compiler_params=pltpu.CompilerParams(
            dimension_semantics=("arbitrary",), vmem_limit_bytes=60 * 1024 * 1024
        ),
    )(hidden_pre, cotangent, table_z)


def exchange_kernel(axis, count, src_ref, dst_ref, local_sem, send_sems, recv_sems):
    mesh_ids = pl.DeviceIdType.MESH
    me = lax.axis_index(axis)
    barrier = pltpu.get_barrier_semaphore()
    for k in range(1, count):
        peer = lax.rem(me + k, count)
        pl.semaphore_signal(barrier, inc=1, device_id={axis: peer}, device_id_type=mesh_ids)
    pl.semaphore_wait(barrier, count - 1)
    local = pltpu.make_async_copy(src_ref.at[me], dst_ref.at[me], local_sem)
    local.start()
    sends = []
    for k in range(1, count):
        peer = lax.rem(me + k, count)
        copy = pltpu.make_async_remote_copy(
            src_ref=src_ref.at[peer],
            dst_ref=dst_ref.at[me],
            send_sem=send_sems.at[k],
            recv_sem=recv_sems.at[k],
            device_id={axis: peer},
            device_id_type=mesh_ids,
        )
        copy.start()
        sends.append(copy)
    local.wait()
    for k in range(1, count):
        sends[k - 1].wait_send()
        origin = lax.rem(me + count - k, count)
        incoming = pltpu.make_async_remote_copy(
            src_ref=src_ref.at[me],
            dst_ref=dst_ref.at[origin],
            send_sem=send_sems.at[k],
            recv_sem=recv_sems.at[k],
            device_id={axis: origin},
            device_id_type=mesh_ids,
        )
        incoming.wait_recv()


def exchange(chunks, axis, count, collective_id):
    return pl.pallas_call(
        functools.partial(exchange_kernel, axis, count),
        in_specs=[pl.BlockSpec(memory_space=pl.ANY)],
        out_specs=pl.BlockSpec(memory_space=pl.ANY),
        out_shape=jax.ShapeDtypeStruct(chunks.shape, chunks.dtype),
        scratch_shapes=[
            pltpu.SemaphoreType.DMA,
            pltpu.SemaphoreType.DMA((count,)),
            pltpu.SemaphoreType.DMA((count,)),
        ],
        compiler_params=pltpu.CompilerParams(collective_id=collective_id, has_side_effects=True),
    )(chunks)


def synthesis_kernel(h_ref, g_ref, ys_ref, tz_ref, sw_ref, out_ref, ks_ref):
    channels, xb, ny, nz = h_ref.shape
    rows = channels * ny

    @pl.when(pl.program_id(0) == 0)
    def _():
        r = lax.broadcasted_iota(jnp.int32, (rows, channels), 0)
        k = lax.broadcasted_iota(jnp.int32, (rows, channels), 1)
        expand = (r // ny == k).astype(jnp.float32)
        spread = jnp.dot(expand, sw_ref[...].astype(jnp.float32), preferred_element_type=jnp.float32)
        kr = lax.broadcasted_iota(jnp.int32, (channels, rows), 0)
        kc = lax.broadcasted_iota(jnp.int32, (channels, rows), 1)
        expand_t = (kc // ny == kr).astype(jnp.float32)
        full = jnp.dot(spread, expand_t, preferred_element_type=jnp.float32)
        ri = lax.broadcasted_iota(jnp.int32, (rows, rows), 0)
        ci = lax.broadcasted_iota(jnp.int32, (rows, rows), 1)
        ks_ref[...] = jnp.where(ri % ny == ci % ny, full, 0.0).astype(ks_ref.dtype)

    tz = tz_ref[...]
    ks = ks_ref[...]
    for x in range(xb):
        spec = jnp.dot(ys_ref[x], tz, preferred_element_type=jnp.float32)
        spec = spec.astype(jnp.bfloat16).astype(jnp.float32)
        skip = jnp.dot(ks, g_ref[:, x].reshape(channels * ny, nz), preferred_element_type=jnp.float32)
        activ = jnp.tanh(h_ref[:, x].astype(jnp.float32)).reshape(channels * ny, nz)
        grad = (spec + skip) * (1.0 - activ * activ)
        out_ref[:, x] = grad.astype(jnp.bfloat16).reshape(channels, ny, nz)


def synthesis(hidden_pre, cotangent, ysynth, table_z, skip_weight):
    channels, nx, ny, nz = hidden_pre.shape
    modes = table_z.shape[0]
    steps = nx // XB
    field_spec = pl.BlockSpec((channels, XB, ny, nz), lambda i: (0, i, 0, 0))
    return pl.pallas_call(
        synthesis_kernel,
        grid=(steps,),
        in_specs=[
            field_spec,
            field_spec,
            pl.BlockSpec((XB, channels * ny, modes), lambda i: (i, 0, 0)),
            pl.BlockSpec((modes, nz), lambda i: (0, 0)),
            pl.BlockSpec((channels, channels), lambda i: (0, 0)),
        ],
        out_specs=field_spec,
        out_shape=jax.ShapeDtypeStruct(hidden_pre.shape, jnp.bfloat16),
        scratch_shapes=[pltpu.VMEM((channels * ny, channels * ny), jnp.bfloat16)],
        compiler_params=pltpu.CompilerParams(
            dimension_semantics=("arbitrary",), vmem_limit_bytes=60 * 1024 * 1024
        ),
    )(hidden_pre, cotangent, ysynth, table_z, skip_weight)


def modes_kernel(sp_ref, w_ref, gm_ref, bs_ref):
    highest = lax.Precision.HIGHEST
    channels = sp_ref.shape[1] // 2
    width = channels * channels
    sp = sp_ref[...]
    er = lax.broadcasted_iota(jnp.int32, (channels, width), 0)
    ec = lax.broadcasted_iota(jnp.int32, (channels, width), 1)
    spread = (ec // channels == er).astype(jnp.float32)
    tile = (ec % channels == er).astype(jnp.float32)
    s_rep = jnp.dot(sp[:, :channels], spread, precision=highest, preferred_element_type=jnp.float32)
    q_rep = jnp.dot(sp[:, channels:], tile, precision=highest, preferred_element_type=jnp.float32)
    gm_ref[...] = s_rep * q_rep
    weighted = w_ref[...].astype(jnp.float32) * q_rep
    back = lax.dot_general(
        weighted, spread, (((1,), (1,)), ((), ())), precision=highest,
        preferred_element_type=jnp.float32)
    bs_ref[...] = back.astype(bs_ref.dtype)


def modes_step(spectra, weights):
    rows, both = spectra.shape
    channels = both // 2
    vmem = pl.BlockSpec(memory_space=pltpu.VMEM)
    return pl.pallas_call(
        modes_kernel,
        in_specs=[vmem, vmem],
        out_specs=[vmem, vmem],
        out_shape=[
            jax.ShapeDtypeStruct((rows, channels * channels), jnp.float32),
            jax.ShapeDtypeStruct((rows, channels), jnp.bfloat16),
        ],
    )(spectra, weights)


def per_device(hidden_pre, cotangent, mode_weight, skip_weight):
    highest = lax.Precision.HIGHEST
    channels, nx, ny, nz = hidden_pre.shape
    mode_count = mode_weight.shape[2]
    n_narrow = lax.axis_size("narrow")
    n_wide = lax.axis_size("wide")
    table_x = basis_table(mode_count, NX)
    table_y = basis_table(mode_count, NY)
    table_z = basis_table(mode_count, NZ)

    zc, gram = analysis(hidden_pre, cotangent, table_z)
    mz_local = mode_count // n_narrow
    zc = zc.reshape(n_narrow, mz_local, 2 * channels, nx * ny)
    zc = exchange(zc, "narrow", n_narrow, 0)
    zc = zc.reshape(n_narrow, mz_local, 2 * channels, nx, ny)
    ycoeffs = jnp.einsum(
        "smcxl,nsl->mcnx", zc, table_y.reshape(mode_count, n_narrow, ny),
        preferred_element_type=jnp.float32,
    ).astype(jnp.bfloat16)
    ycoeffs = lax.all_to_all(ycoeffs, "wide", split_axis=2, concat_axis=3, tiled=True)
    spectra = jnp.einsum("zcyx,kx->zykc", ycoeffs, table_x, preferred_element_type=jnp.float32)
    z_local, y_local = (spectra.shape[0], spectra.shape[1])
    grad_modes, back_spec = modes_step(
        spectra.reshape(z_local * y_local * mode_count, 2 * channels),
        mode_weight.reshape(z_local * y_local * mode_count, channels * channels),
    )
    grad_modes = grad_modes.reshape(z_local, y_local, mode_count, channels * channels)
    back_spec = jnp.transpose(
        back_spec.reshape(z_local, y_local, mode_count, channels), (0, 3, 1, 2)
    )
    xsynth = jnp.einsum(
        "zcyk,kx->zcyx", back_spec, table_x, preferred_element_type=jnp.float32
    ).astype(jnp.bfloat16)
    xsynth = lax.all_to_all(xsynth, "wide", split_axis=3, concat_axis=2, tiled=True)
    ysynth = jnp.einsum(
        "zcnx,ny->xcyz", xsynth, table_y, preferred_element_type=jnp.float32
    ).astype(jnp.bfloat16)
    ysynth = lax.all_to_all(ysynth, "narrow", split_axis=2, concat_axis=3, tiled=True)
    ysynth = ysynth.reshape(nx, channels * ny, mode_count)
    grad_hidden = synthesis(hidden_pre, cotangent, ysynth, table_z, skip_weight)

    total = gram.reshape(1, channels * channels)
    for axis, count in (("narrow", n_narrow), ("wide", n_wide)):
        spread = jnp.broadcast_to(total, (count, channels * channels))
        total = lax.all_to_all(spread, axis, 0, 0, tiled=True).sum(0, keepdims=True)
    grad_skip = total.reshape(channels, channels) * (1.0 / math.sqrt(NX * NY * NZ))
    return (grad_hidden, grad_modes, grad_skip)


def solution(mesh):
    in_specs = (
        P(None, "wide", "narrow", None),
        P(None, "wide", "narrow", None),
        P("narrow", "wide", None, None),
        P(),
    )
    out_specs = (P(None, "wide", "narrow", None), P("narrow", "wide", None, None), P())
    return jax.shard_map(
        per_device, mesh=mesh, in_specs=in_specs, out_specs=out_specs, check_vma=False
    )
```

```python
import functools
import math

import jax
import jax.numpy as jnp
from jax import lax
from jax.experimental import pallas as pl
from jax.experimental.pallas import tpu as pltpu
from jax.sharding import PartitionSpec as P

NX = 256
NY = 256
NZ = 256
XB = 8


def basis_table(mode_count, length):
    mode_index = jnp.arange(mode_count, dtype=jnp.int32)
    halfway = mode_count // 2
    frequency = jnp.where(mode_index < halfway, mode_index, mode_index - halfway + 1)
    points = jnp.arange(length, dtype=jnp.int32)
    phases = frequency[:, None] * points[None, :] % length
    angles = phases.astype(jnp.float32) * (2.0 * math.pi / length)
    values_table = jnp.where((mode_index < halfway)[:, None], jnp.cos(angles), jnp.sin(angles))
    return (values_table * (1.0 / math.sqrt(length))).astype(jnp.bfloat16)


def _nt(a, b):
    return lax.dot_general(a, b, (((1,), (1,)), ((), ())), preferred_element_type=jnp.float32)


def analysis_kernel(h_ref, g_ref, tz_ref, zc_ref, gram_ref, acc_ref, stage_ref):
    step = pl.program_id(0)
    channels, xb, ny, nz = h_ref.shape

    @pl.when(step == 0)
    def _():
        acc_ref[...] = jnp.zeros_like(acc_ref)

    tz = tz_ref[...]
    li = jnp.tanh(h_ref[...].astype(jnp.float32)).astype(jnp.bfloat16)
    g = g_ref[...]
    width = xb * ny
    zl = _nt(tz, li.reshape(channels * width, nz))
    zg = _nt(tz, g.reshape(channels * width, nz))
    for c in range(channels):
        stage_ref[:, c, :] = zl[:, c * width:(c + 1) * width]
        stage_ref[:, channels + c, :] = zg[:, c * width:(c + 1) * width]
    zc_ref[...] = stage_ref[...].astype(jnp.bfloat16)
    for x in range(xb):
        acc_ref[...] += _nt(li[:, x].reshape(channels * ny, nz), g[:, x].reshape(channels * ny, nz))

    @pl.when(step == pl.num_programs(0) - 1)
    def _():
        rows = channels * ny
        ri = lax.broadcasted_iota(jnp.int32, (rows, rows), 0)
        ci = lax.broadcasted_iota(jnp.int32, (rows, rows), 1)
        diag = jnp.where(ri % ny == ci % ny, acc_ref[...], 0.0)
        er = lax.broadcasted_iota(jnp.int32, (channels, rows), 0)
        ec = lax.broadcasted_iota(jnp.int32, (channels, rows), 1)
        gather = (ec // ny == er).astype(jnp.float32)
        part = jnp.dot(gather, diag, precision=lax.Precision.HIGHEST, preferred_element_type=jnp.float32)
        gram_ref[...] = lax.dot_general(
            part, gather, (((1,), (1,)), ((), ())), precision=lax.Precision.HIGHEST,
            preferred_element_type=jnp.float32)


def analysis(hidden_pre, cotangent, table_z):
    channels, nx, ny, nz = hidden_pre.shape
    modes = table_z.shape[0]
    steps = nx // XB
    field_spec = pl.BlockSpec((channels, XB, ny, nz), lambda i: (0, i, 0, 0))
    return pl.pallas_call(
        analysis_kernel,
        grid=(steps,),
        in_specs=[field_spec, field_spec, pl.BlockSpec((modes, nz), lambda i: (0, 0))],
        out_specs=[
            pl.BlockSpec((modes, 2 * channels, XB * ny), lambda i: (0, 0, i)),
            pl.BlockSpec((channels, channels), lambda i: (0, 0)),
        ],
        out_shape=[
            jax.ShapeDtypeStruct((modes, 2 * channels, nx * ny), jnp.bfloat16),
            jax.ShapeDtypeStruct((channels, channels), jnp.float32),
        ],
        scratch_shapes=[
            pltpu.VMEM((channels * ny, channels * ny), jnp.float32),
            pltpu.VMEM((modes, 2 * channels, XB * ny), jnp.float32),
        ],
        compiler_params=pltpu.CompilerParams(
            dimension_semantics=("arbitrary",), vmem_limit_bytes=60 * 1024 * 1024
        ),
    )(hidden_pre, cotangent, table_z)


def exchange_kernel(axis, count, src_ref, dst_ref, local_sem, send_sems, recv_sems):
    mesh_ids = pl.DeviceIdType.MESH
    me = lax.axis_index(axis)
    barrier = pltpu.get_barrier_semaphore()
    for k in range(1, count):
        peer = lax.rem(me + k, count)
        pl.semaphore_signal(barrier, inc=1, device_id={axis: peer}, device_id_type=mesh_ids)
    pl.semaphore_wait(barrier, count - 1)
    local = pltpu.make_async_copy(src_ref.at[me], dst_ref.at[me], local_sem)
    local.start()
    sends = []
    for k in range(1, count):
        peer = lax.rem(me + k, count)
        copy = pltpu.make_async_remote_copy(
            src_ref=src_ref.at[peer],
            dst_ref=dst_ref.at[me],
            send_sem=send_sems.at[k],
            recv_sem=recv_sems.at[k],
            device_id={axis: peer},
            device_id_type=mesh_ids,
        )
        copy.start()
        sends.append(copy)
    local.wait()
    for k in range(1, count):
        sends[k - 1].wait_send()
        origin = lax.rem(me + count - k, count)
        incoming = pltpu.make_async_remote_copy(
            src_ref=src_ref.at[me],
            dst_ref=dst_ref.at[origin],
            send_sem=send_sems.at[k],
            recv_sem=recv_sems.at[k],
            device_id={axis: origin},
            device_id_type=mesh_ids,
        )
        incoming.wait_recv()


def exchange(chunks, axis, count, collective_id):
    return pl.pallas_call(
        functools.partial(exchange_kernel, axis, count),
        in_specs=[pl.BlockSpec(memory_space=pl.ANY)],
        out_specs=pl.BlockSpec(memory_space=pl.ANY),
        out_shape=jax.ShapeDtypeStruct(chunks.shape, chunks.dtype),
        scratch_shapes=[
            pltpu.SemaphoreType.DMA,
            pltpu.SemaphoreType.DMA((count,)),
            pltpu.SemaphoreType.DMA((count,)),
        ],
        compiler_params=pltpu.CompilerParams(collective_id=collective_id, has_side_effects=True),
    )(chunks)


def synthesis_kernel(h_ref, g_ref, ys_ref, tz_ref, sw_ref, out_ref, ks_ref):
    channels, xb, ny, nz = h_ref.shape
    rows = channels * ny

    @pl.when(pl.program_id(0) == 0)
    def _():
        r = lax.broadcasted_iota(jnp.int32, (rows, channels), 0)
        k = lax.broadcasted_iota(jnp.int32, (rows, channels), 1)
        expand = (r // ny == k).astype(jnp.float32)
        spread = jnp.dot(expand, sw_ref[...].astype(jnp.float32), preferred_element_type=jnp.float32)
        kr = lax.broadcasted_iota(jnp.int32, (channels, rows), 0)
        kc = lax.broadcasted_iota(jnp.int32, (channels, rows), 1)
        expand_t = (kc // ny == kr).astype(jnp.float32)
        full = jnp.dot(spread, expand_t, preferred_element_type=jnp.float32)
        ri = lax.broadcasted_iota(jnp.int32, (rows, rows), 0)
        ci = lax.broadcasted_iota(jnp.int32, (rows, rows), 1)
        ks_ref[...] = jnp.where(ri % ny == ci % ny, full, 0.0).astype(ks_ref.dtype)

    tz = tz_ref[...]
    ks = ks_ref[...]
    ys = ys_ref[...].astype(jnp.float32)
    for x in range(xb):
        lo = ys[:, 2 * x, :]
        hi = ys[:, 2 * x + 1, :]
        lhs = jnp.concatenate([lo, hi], axis=0).T.astype(jnp.bfloat16)
        spec = jnp.dot(lhs, tz, preferred_element_type=jnp.float32)
        spec = spec.astype(jnp.bfloat16).astype(jnp.float32)
        skip = jnp.dot(ks, g_ref[:, x].reshape(channels * ny, nz), preferred_element_type=jnp.float32)
        activ = jnp.tanh(h_ref[:, x].astype(jnp.float32)).reshape(channels * ny, nz)
        grad = (spec + skip) * (1.0 - activ * activ)
        out_ref[:, x] = grad.astype(jnp.bfloat16).reshape(channels, ny, nz)


def synthesis(hidden_pre, cotangent, ysynth, table_z, skip_weight):
    channels, nx, ny, nz = hidden_pre.shape
    modes = table_z.shape[0]
    steps = nx // XB
    field_spec = pl.BlockSpec((channels, XB, ny, nz), lambda i: (0, i, 0, 0))
    return pl.pallas_call(
        synthesis_kernel,
        grid=(steps,),
        in_specs=[
            field_spec,
            field_spec,
            pl.BlockSpec((ysynth.shape[0], 2 * XB, channels * ny), lambda i: (0, i, 0)),
            pl.BlockSpec((modes, nz), lambda i: (0, 0)),
            pl.BlockSpec((channels, channels), lambda i: (0, 0)),
        ],
        out_specs=field_spec,
        out_shape=jax.ShapeDtypeStruct(hidden_pre.shape, jnp.bfloat16),
        scratch_shapes=[pltpu.VMEM((channels * ny, channels * ny), jnp.bfloat16)],
        compiler_params=pltpu.CompilerParams(
            dimension_semantics=("arbitrary",), vmem_limit_bytes=60 * 1024 * 1024
        ),
    )(hidden_pre, cotangent, ysynth, table_z, skip_weight)


def modes_kernel(sp_ref, w_ref, gm_ref, bs_ref):
    highest = lax.Precision.HIGHEST
    channels = sp_ref.shape[1] // 2
    width = channels * channels
    sp = sp_ref[...]
    er = lax.broadcasted_iota(jnp.int32, (channels, width), 0)
    ec = lax.broadcasted_iota(jnp.int32, (channels, width), 1)
    spread = (ec // channels == er).astype(jnp.float32)
    tile = (ec % channels == er).astype(jnp.float32)
    s_rep = jnp.dot(sp[:, :channels], spread, precision=highest, preferred_element_type=jnp.float32)
    q_rep = jnp.dot(sp[:, channels:], tile, precision=highest, preferred_element_type=jnp.float32)
    gm_ref[...] = s_rep * q_rep
    weighted = w_ref[...].astype(jnp.float32) * q_rep
    back = lax.dot_general(
        weighted, spread, (((1,), (1,)), ((), ())), precision=highest,
        preferred_element_type=jnp.float32)
    bs_ref[...] = back.astype(bs_ref.dtype)


def modes_step(spectra, weights):
    rows, both = spectra.shape
    channels = both // 2
    vmem = pl.BlockSpec(memory_space=pltpu.VMEM)
    return pl.pallas_call(
        modes_kernel,
        in_specs=[vmem, vmem],
        out_specs=[vmem, vmem],
        out_shape=[
            jax.ShapeDtypeStruct((rows, channels * channels), jnp.float32),
            jax.ShapeDtypeStruct((rows, channels), jnp.bfloat16),
        ],
    )(spectra, weights)


def per_device(hidden_pre, cotangent, mode_weight, skip_weight):
    highest = lax.Precision.HIGHEST
    channels, nx, ny, nz = hidden_pre.shape
    mode_count = mode_weight.shape[2]
    n_narrow = lax.axis_size("narrow")
    n_wide = lax.axis_size("wide")
    table_x = basis_table(mode_count, NX)
    table_y = basis_table(mode_count, NY)
    table_z = basis_table(mode_count, NZ)

    zc, gram = analysis(hidden_pre, cotangent, table_z)
    mz_local = mode_count // n_narrow
    zc = zc.reshape(n_narrow, mz_local, 2 * channels, nx * ny)
    zc = exchange(zc, "narrow", n_narrow, 0)
    zc = zc.reshape(n_narrow, mz_local, 2 * channels, nx, ny)
    ycoeffs = jnp.einsum(
        "smcxl,nsl->mcnx", zc, table_y.reshape(mode_count, n_narrow, ny),
        preferred_element_type=jnp.float32,
    ).astype(jnp.bfloat16)
    ycoeffs = lax.all_to_all(ycoeffs, "wide", split_axis=2, concat_axis=3, tiled=True)
    spectra = jnp.einsum("zcyx,kx->zykc", ycoeffs, table_x, preferred_element_type=jnp.float32)
    z_local, y_local = (spectra.shape[0], spectra.shape[1])
    grad_modes, back_spec = modes_step(
        spectra.reshape(z_local * y_local * mode_count, 2 * channels),
        mode_weight.reshape(z_local * y_local * mode_count, channels * channels),
    )
    grad_modes = grad_modes.reshape(z_local, y_local, mode_count, channels * channels)
    back_spec = jnp.transpose(
        back_spec.reshape(z_local, y_local, mode_count, channels), (0, 3, 1, 2)
    )
    xsynth = jnp.einsum(
        "zcyk,kx->zcyx", back_spec, table_x, preferred_element_type=jnp.float32
    ).astype(jnp.bfloat16)
    xsynth = lax.all_to_all(xsynth, "wide", split_axis=3, concat_axis=2, tiled=True)
    ysynth = jnp.einsum(
        "zcnx,ndy->dxzcy", xsynth, table_y.reshape(mode_count, n_narrow, ny),
        preferred_element_type=jnp.float32,
    ).astype(jnp.bfloat16)
    ysynth = ysynth.reshape(n_narrow, nx * mz_local, channels * ny)
    ysynth = exchange(ysynth, "narrow", n_narrow, 1)
    table_zp = jnp.transpose(table_z.reshape(n_narrow, mz_local, nz), (1, 0, 2)).reshape(mode_count, nz)
    grad_hidden = synthesis(hidden_pre, cotangent, ysynth, table_zp, skip_weight)

    total = gram.reshape(1, channels * channels)
    for axis, count in (("narrow", n_narrow), ("wide", n_wide)):
        spread = jnp.broadcast_to(total, (count, channels * channels))
        total = lax.all_to_all(spread, axis, 0, 0, tiled=True).sum(0, keepdims=True)
    grad_skip = total.reshape(channels, channels) * (1.0 / math.sqrt(NX * NY * NZ))
    return (grad_hidden, grad_modes, grad_skip)


def solution(mesh):
    in_specs = (
        P(None, "wide", "narrow", None),
        P(None, "wide", "narrow", None),
        P("narrow", "wide", None, None),
        P(),
    )
    out_specs = (P(None, "wide", "narrow", None), P("narrow", "wide", None, None), P())
    return jax.shard_map(
        per_device, mesh=mesh, in_specs=in_specs, out_specs=out_specs, check_vma=False
    )
```

```python
import functools
import math

import jax
import jax.numpy as jnp
from jax import lax
from jax.experimental import pallas as pl
from jax.experimental.pallas import tpu as pltpu
from jax.sharding import PartitionSpec as P

NX = 256
NY = 256
NZ = 256
XB = 8


def basis_table(mode_count, length):
    mode_index = jnp.arange(mode_count, dtype=jnp.int32)
    halfway = mode_count // 2
    frequency = jnp.where(mode_index < halfway, mode_index, mode_index - halfway + 1)
    points = jnp.arange(length, dtype=jnp.int32)
    phases = frequency[:, None] * points[None, :] % length
    angles = phases.astype(jnp.float32) * (2.0 * math.pi / length)
    values_table = jnp.where((mode_index < halfway)[:, None], jnp.cos(angles), jnp.sin(angles))
    return (values_table * (1.0 / math.sqrt(length))).astype(jnp.bfloat16)


def _nt(a, b):
    return lax.dot_general(a, b, (((1,), (1,)), ((), ())), preferred_element_type=jnp.float32)


def analysis_kernel(h_ref, g_ref, tz_ref, zc_ref, gram_ref, acc_ref, stage_ref):
    step = pl.program_id(0)
    channels, xb, ny, nz = h_ref.shape

    @pl.when(step == 0)
    def _():
        acc_ref[...] = jnp.zeros_like(acc_ref)

    tz = tz_ref[...]
    li = jnp.tanh(h_ref[...].astype(jnp.float32)).astype(jnp.bfloat16)
    g = g_ref[...]
    width = xb * ny
    zl = _nt(tz, li.reshape(channels * width, nz))
    zg = _nt(tz, g.reshape(channels * width, nz))
    for c in range(channels):
        stage_ref[:, c, :] = zl[:, c * width:(c + 1) * width]
        stage_ref[:, channels + c, :] = zg[:, c * width:(c + 1) * width]
    zc_ref[...] = stage_ref[...].astype(jnp.bfloat16)
    for x in range(xb):
        acc_ref[...] += _nt(li[:, x].reshape(channels * ny, nz), g[:, x].reshape(channels * ny, nz))

    @pl.when(step == pl.num_programs(0) - 1)
    def _():
        rows = channels * ny
        ri = lax.broadcasted_iota(jnp.int32, (rows, rows), 0)
        ci = lax.broadcasted_iota(jnp.int32, (rows, rows), 1)
        diag = jnp.where(ri % ny == ci % ny, acc_ref[...], 0.0)
        er = lax.broadcasted_iota(jnp.int32, (channels, rows), 0)
        ec = lax.broadcasted_iota(jnp.int32, (channels, rows), 1)
        gather = (ec // ny == er).astype(jnp.float32)
        part = jnp.dot(gather, diag, precision=lax.Precision.HIGHEST, preferred_element_type=jnp.float32)
        gram_ref[...] = lax.dot_general(
            part, gather, (((1,), (1,)), ((), ())), precision=lax.Precision.HIGHEST,
            preferred_element_type=jnp.float32)


def analysis(hidden_pre, cotangent, table_z):
    channels, nx, ny, nz = hidden_pre.shape
    modes = table_z.shape[0]
    steps = nx // XB
    field_spec = pl.BlockSpec((channels, XB, ny, nz), lambda i: (0, i, 0, 0))
    return pl.pallas_call(
        analysis_kernel,
        grid=(steps,),
        in_specs=[field_spec, field_spec, pl.BlockSpec((modes, nz), lambda i: (0, 0))],
        out_specs=[
            pl.BlockSpec((modes, 2 * channels, XB * ny), lambda i: (0, 0, i)),
            pl.BlockSpec((channels, channels), lambda i: (0, 0)),
        ],
        out_shape=[
            jax.ShapeDtypeStruct((modes, 2 * channels, nx * ny), jnp.bfloat16),
            jax.ShapeDtypeStruct((channels, channels), jnp.float32),
        ],
        scratch_shapes=[
            pltpu.VMEM((channels * ny, channels * ny), jnp.float32),
            pltpu.VMEM((modes, 2 * channels, XB * ny), jnp.float32),
        ],
        compiler_params=pltpu.CompilerParams(
            dimension_semantics=("arbitrary",), vmem_limit_bytes=60 * 1024 * 1024
        ),
    )(hidden_pre, cotangent, table_z)


def exchange_kernel(axis, count, src_ref, dst_ref, local_sem, send_sems, recv_sems):
    mesh_ids = pl.DeviceIdType.MESH
    me = lax.axis_index(axis)
    barrier = pltpu.get_barrier_semaphore()
    for k in range(1, count):
        peer = lax.rem(me + k, count)
        pl.semaphore_signal(barrier, inc=1, device_id={axis: peer}, device_id_type=mesh_ids)
    pl.semaphore_wait(barrier, count - 1)
    local = pltpu.make_async_copy(src_ref.at[me], dst_ref.at[me], local_sem)
    local.start()
    sends = []
    for k in range(1, count):
        peer = lax.rem(me + k, count)
        copy = pltpu.make_async_remote_copy(
            src_ref=src_ref.at[peer],
            dst_ref=dst_ref.at[me],
            send_sem=send_sems.at[k],
            recv_sem=recv_sems.at[k],
            device_id={axis: peer},
            device_id_type=mesh_ids,
        )
        copy.start()
        sends.append(copy)
    local.wait()
    for k in range(1, count):
        sends[k - 1].wait_send()
        origin = lax.rem(me + count - k, count)
        incoming = pltpu.make_async_remote_copy(
            src_ref=src_ref.at[me],
            dst_ref=dst_ref.at[origin],
            send_sem=send_sems.at[k],
            recv_sem=recv_sems.at[k],
            device_id={axis: origin},
            device_id_type=mesh_ids,
        )
        incoming.wait_recv()


def exchange(chunks, axis, count, collective_id):
    return pl.pallas_call(
        functools.partial(exchange_kernel, axis, count),
        in_specs=[pl.BlockSpec(memory_space=pl.ANY)],
        out_specs=pl.BlockSpec(memory_space=pl.ANY),
        out_shape=jax.ShapeDtypeStruct(chunks.shape, chunks.dtype),
        scratch_shapes=[
            pltpu.SemaphoreType.DMA,
            pltpu.SemaphoreType.DMA((count,)),
            pltpu.SemaphoreType.DMA((count,)),
        ],
        compiler_params=pltpu.CompilerParams(collective_id=collective_id, has_side_effects=True),
    )(chunks)


def synthesis_kernel(h_ref, g_ref, ys_ref, tz_ref, sw_ref, out_ref, ks_ref):
    channels, xb, ny, nz = h_ref.shape
    rows = channels * ny

    @pl.when(pl.program_id(0) == 0)
    def _():
        r = lax.broadcasted_iota(jnp.int32, (rows, channels), 0)
        k = lax.broadcasted_iota(jnp.int32, (rows, channels), 1)
        expand = (r // ny == k).astype(jnp.float32)
        spread = jnp.dot(expand, sw_ref[...].astype(jnp.float32), preferred_element_type=jnp.float32)
        kr = lax.broadcasted_iota(jnp.int32, (channels, rows), 0)
        kc = lax.broadcasted_iota(jnp.int32, (channels, rows), 1)
        expand_t = (kc // ny == kr).astype(jnp.float32)
        full = jnp.dot(spread, expand_t, preferred_element_type=jnp.float32)
        ri = lax.broadcasted_iota(jnp.int32, (rows, rows), 0)
        ci = lax.broadcasted_iota(jnp.int32, (rows, rows), 1)
        ks_ref[...] = jnp.where(ri % ny == ci % ny, full, 0.0).astype(ks_ref.dtype)

    tz = tz_ref[...]
    ks = ks_ref[...]
    ys = ys_ref[...].astype(jnp.float32)
    for x in range(xb):
        lo = ys[:, 2 * x, :]
        hi = ys[:, 2 * x + 1, :]
        lhs = jnp.concatenate([lo, hi], axis=0).T.astype(jnp.bfloat16)
        spec = jnp.dot(lhs, tz, preferred_element_type=jnp.float32)
        spec = spec.astype(jnp.bfloat16).astype(jnp.float32)
        skip = jnp.dot(ks, g_ref[:, x].reshape(channels * ny, nz), preferred_element_type=jnp.float32)
        activ = jnp.tanh(h_ref[:, x].astype(jnp.float32)).reshape(channels * ny, nz)
        grad = (spec + skip) * (1.0 - activ * activ)
        out_ref[:, x] = grad.astype(jnp.bfloat16).reshape(channels, ny, nz)


def synthesis(hidden_pre, cotangent, ysynth, table_z, skip_weight):
    channels, nx, ny, nz = hidden_pre.shape
    modes = table_z.shape[0]
    steps = nx // XB
    field_spec = pl.BlockSpec((channels, XB, ny, nz), lambda i: (0, i, 0, 0))
    return pl.pallas_call(
        synthesis_kernel,
        grid=(steps,),
        in_specs=[
            field_spec,
            field_spec,
            pl.BlockSpec((ysynth.shape[0], 2 * XB, channels * ny), lambda i: (0, i, 0)),
            pl.BlockSpec((modes, nz), lambda i: (0, 0)),
            pl.BlockSpec((channels, channels), lambda i: (0, 0)),
        ],
        out_specs=field_spec,
        out_shape=jax.ShapeDtypeStruct(hidden_pre.shape, jnp.bfloat16),
        scratch_shapes=[pltpu.VMEM((channels * ny, channels * ny), jnp.bfloat16)],
        compiler_params=pltpu.CompilerParams(
            dimension_semantics=("arbitrary",), vmem_limit_bytes=60 * 1024 * 1024
        ),
    )(hidden_pre, cotangent, ysynth, table_z, skip_weight)


def y_synthesis_kernel(xs_ref, tyt_ref, out_ref, stage_ref):
    mz_local, channels, modes, nx = xs_ref.shape
    blocks, _, lanes = out_ref.shape
    ny = lanes // channels
    tyt = jnp.broadcast_to(tyt_ref[...][None], (channels,) + tyt_ref.shape)
    for z in range(mz_local):
        part = jnp.einsum(
            "cym,cmx->cyx", tyt, xs_ref[z], preferred_element_type=jnp.float32
        ).astype(jnp.bfloat16).astype(jnp.float32)
        for d in range(blocks):
            piece = part[:, d * ny:(d + 1) * ny, :].reshape(channels * ny, nx).T
            for q in range(lanes // 128):
                stage_ref[d * (lanes // 128) + q, pl.ds(z, nx, stride=mz_local), :] = (
                    piece[:, q * 128:(q + 1) * 128])
    for d in range(blocks):
        for q in range(lanes // 128):
            out_ref[d, :, q * 128:(q + 1) * 128] = (
                stage_ref[d * (lanes // 128) + q].astype(out_ref.dtype))


def y_synthesis(xsynth, table_yt, blocks):
    mz_local, channels, modes, nx = xsynth.shape
    ny = table_yt.shape[0] // blocks
    vmem = pl.BlockSpec(memory_space=pltpu.VMEM)
    return pl.pallas_call(
        y_synthesis_kernel,
        in_specs=[vmem, vmem],
        out_specs=vmem,
        out_shape=jax.ShapeDtypeStruct((blocks, nx * mz_local, channels * ny), jnp.bfloat16),
        scratch_shapes=[
            pltpu.VMEM((blocks * channels * ny // 128, nx * mz_local, 128), jnp.float32)
        ],
    )(xsynth, table_yt)


def modes_kernel(sp_ref, w_ref, gm_ref, bs_ref):
    highest = lax.Precision.HIGHEST
    channels = sp_ref.shape[1] // 2
    width = channels * channels
    sp = sp_ref[...]
    er = lax.broadcasted_iota(jnp.int32, (channels, width), 0)
    ec = lax.broadcasted_iota(jnp.int32, (channels, width), 1)
    spread = (ec // channels == er).astype(jnp.float32)
    tile = (ec % channels == er).astype(jnp.float32)
    s_rep = jnp.dot(sp[:, :channels], spread, precision=highest, preferred_element_type=jnp.float32)
    q_rep = jnp.dot(sp[:, channels:], tile, precision=highest, preferred_element_type=jnp.float32)
    gm_ref[...] = s_rep * q_rep
    weighted = w_ref[...].astype(jnp.float32) * q_rep
    back = lax.dot_general(
        weighted, spread, (((1,), (1,)), ((), ())), precision=highest,
        preferred_element_type=jnp.float32)
    bs_ref[...] = back.astype(bs_ref.dtype)


def modes_step(spectra, weights):
    rows, both = spectra.shape
    channels = both // 2
    vmem = pl.BlockSpec(memory_space=pltpu.VMEM)
    return pl.pallas_call(
        modes_kernel,
        in_specs=[vmem, vmem],
        out_specs=[vmem, vmem],
        out_shape=[
            jax.ShapeDtypeStruct((rows, channels * channels), jnp.float32),
            jax.ShapeDtypeStruct((rows, channels), jnp.bfloat16),
        ],
    )(spectra, weights)


def per_device(hidden_pre, cotangent, mode_weight, skip_weight):
    highest = lax.Precision.HIGHEST
    channels, nx, ny, nz = hidden_pre.shape
    mode_count = mode_weight.shape[2]
    n_narrow = lax.axis_size("narrow")
    n_wide = lax.axis_size("wide")
    table_x = basis_table(mode_count, NX)
    table_y = basis_table(mode_count, NY)
    table_z = basis_table(mode_count, NZ)

    zc, gram = analysis(hidden_pre, cotangent, table_z)
    mz_local = mode_count // n_narrow
    zc = zc.reshape(n_narrow, mz_local, 2 * channels, nx * ny)
    zc = exchange(zc, "narrow", n_narrow, 0)
    zc = zc.reshape(n_narrow, mz_local, 2 * channels, nx, ny)
    ycoeffs = jnp.einsum(
        "smcxl,nsl->mcnx", zc, table_y.reshape(mode_count, n_narrow, ny),
        preferred_element_type=jnp.float32,
    ).astype(jnp.bfloat16)
    ycoeffs = lax.all_to_all(ycoeffs, "wide", split_axis=2, concat_axis=3, tiled=True)
    spectra = jnp.einsum("zcyx,kx->zykc", ycoeffs, table_x, preferred_element_type=jnp.float32)
    z_local, y_local = (spectra.shape[0], spectra.shape[1])
    grad_modes, back_spec = modes_step(
        spectra.reshape(z_local * y_local * mode_count, 2 * channels),
        mode_weight.reshape(z_local * y_local * mode_count, channels * channels),
    )
    grad_modes = grad_modes.reshape(z_local, y_local, mode_count, channels * channels)
    back_spec = jnp.transpose(
        back_spec.reshape(z_local, y_local, mode_count, channels), (0, 3, 1, 2)
    )
    xsynth = jnp.einsum(
        "zcyk,kx->zcyx", back_spec, table_x, preferred_element_type=jnp.float32
    ).astype(jnp.bfloat16)
    xsynth = lax.all_to_all(xsynth, "wide", split_axis=3, concat_axis=2, tiled=True)
    ysynth = y_synthesis(xsynth, jnp.transpose(table_y), n_narrow)
    ysynth = exchange(ysynth, "narrow", n_narrow, 1)
    table_zp = jnp.transpose(table_z.reshape(n_narrow, mz_local, nz), (1, 0, 2)).reshape(mode_count, nz)
    grad_hidden = synthesis(hidden_pre, cotangent, ysynth, table_zp, skip_weight)

    total = gram.reshape(1, channels * channels)
    for axis, count in (("narrow", n_narrow), ("wide", n_wide)):
        spread = jnp.broadcast_to(total, (count, channels * channels))
        total = lax.all_to_all(spread, axis, 0, 0, tiled=True).sum(0, keepdims=True)
    grad_skip = total.reshape(channels, channels) * (1.0 / math.sqrt(NX * NY * NZ))
    return (grad_hidden, grad_modes, grad_skip)


def solution(mesh):
    in_specs = (
        P(None, "wide", "narrow", None),
        P(None, "wide", "narrow", None),
        P("narrow", "wide", None, None),
        P(),
    )
    out_specs = (P(None, "wide", "narrow", None), P("narrow", "wide", None, None), P())
    return jax.shard_map(
        per_device, mesh=mesh, in_specs=in_specs, out_specs=out_specs, check_vma=False
    )
```

```python
import functools
import math

import jax
import jax.numpy as jnp
from jax import lax
from jax.experimental import pallas as pl
from jax.experimental.pallas import tpu as pltpu
from jax.sharding import PartitionSpec as P

NX = 256
NY = 256
NZ = 256
XB = 8


def basis_table(mode_count, length):
    mode_index = jnp.arange(mode_count, dtype=jnp.int32)
    halfway = mode_count // 2
    frequency = jnp.where(mode_index < halfway, mode_index, mode_index - halfway + 1)
    points = jnp.arange(length, dtype=jnp.int32)
    phases = frequency[:, None] * points[None, :] % length
    angles = phases.astype(jnp.float32) * (2.0 * math.pi / length)
    values_table = jnp.where((mode_index < halfway)[:, None], jnp.cos(angles), jnp.sin(angles))
    return (values_table * (1.0 / math.sqrt(length))).astype(jnp.bfloat16)


def _nt(a, b):
    return lax.dot_general(a, b, (((1,), (1,)), ((), ())), preferred_element_type=jnp.float32)


def analysis_kernel(axis, count, h_ref, g_ref, tz_ref, zc_ref, gram_ref, acc_ref, stage_ref,
                    slot_ref, local_sems, send_sems, recv_sems):
    mesh_ids = pl.DeviceIdType.MESH
    step = pl.program_id(0)
    steps = pl.num_programs(0)
    channels, xb, ny, nz = h_ref.shape
    width = xb * ny
    mz_local = slot_ref.shape[1] // count
    me = lax.axis_index(axis)

    def copies(at):
        slot = lax.rem(at, 2)
        cols = pl.ds(pl.multiple_of(at * width, width), width)
        local = pltpu.make_async_copy(
            slot_ref.at[slot, pl.ds(me * mz_local, mz_local)],
            zc_ref.at[me, :, :, cols],
            local_sems.at[at],
        )
        remote = []
        for k in range(1, count):
            peer = lax.rem(me + k, count)
            remote.append(pltpu.make_async_remote_copy(
                src_ref=slot_ref.at[slot, pl.ds(peer * mz_local, mz_local)],
                dst_ref=zc_ref.at[me, :, :, cols],
                send_sem=send_sems.at[at, k],
                recv_sem=recv_sems.at[at, k],
                device_id={axis: peer},
                device_id_type=mesh_ids,
            ))
        return local, remote

    def wait_sent(at):
        local, remote = copies(at)
        local.wait()
        for copy in remote:
            copy.wait_send()

    @pl.when(step == 0)
    def _():
        acc_ref[...] = jnp.zeros_like(acc_ref)
        barrier = pltpu.get_barrier_semaphore()
        for k in range(1, count):
            peer = lax.rem(me + k, count)
            pl.semaphore_signal(barrier, inc=1, device_id={axis: peer}, device_id_type=mesh_ids)
        pl.semaphore_wait(barrier, count - 1)

    @pl.when(step >= 2)
    def _():
        wait_sent(step - 2)

    tz = tz_ref[...]
    li = jnp.tanh(h_ref[...].astype(jnp.float32)).astype(jnp.bfloat16)
    g = g_ref[...]
    zl = _nt(tz, li.reshape(channels * width, nz))
    zg = _nt(tz, g.reshape(channels * width, nz))
    for c in range(channels):
        stage_ref[:, c, :] = zl[:, c * width:(c + 1) * width]
        stage_ref[:, channels + c, :] = zg[:, c * width:(c + 1) * width]
    slot_ref[lax.rem(step, 2)] = stage_ref[...].astype(jnp.bfloat16)
    local, remote = copies(step)
    local.start()
    for copy in remote:
        copy.start()
    for x in range(xb):
        acc_ref[...] += _nt(li[:, x].reshape(channels * ny, nz), g[:, x].reshape(channels * ny, nz))

    @pl.when(step == steps - 1)
    def _():
        rows = channels * ny
        ri = lax.broadcasted_iota(jnp.int32, (rows, rows), 0)
        ci = lax.broadcasted_iota(jnp.int32, (rows, rows), 1)
        diag = jnp.where(ri % ny == ci % ny, acc_ref[...], 0.0)
        er = lax.broadcasted_iota(jnp.int32, (channels, rows), 0)
        ec = lax.broadcasted_iota(jnp.int32, (channels, rows), 1)
        gather = (ec // ny == er).astype(jnp.float32)
        part = jnp.dot(gather, diag, precision=lax.Precision.HIGHEST, preferred_element_type=jnp.float32)
        gram_ref[...] = lax.dot_general(
            part, gather, (((1,), (1,)), ((), ())), precision=lax.Precision.HIGHEST,
            preferred_element_type=jnp.float32)
        wait_sent(step - 1)
        wait_sent(step)
        for at in range(zc_ref.shape[3] // width):
            cols = pl.ds(at * width, width)
            for k in range(1, count):
                origin = lax.rem(me + count - k, count)
                pltpu.make_async_remote_copy(
                    src_ref=slot_ref.at[0, pl.ds(me * mz_local, mz_local)],
                    dst_ref=zc_ref.at[origin, :, :, cols],
                    send_sem=send_sems.at[at, k],
                    recv_sem=recv_sems.at[at, k],
                    device_id={axis: origin},
                    device_id_type=mesh_ids,
                ).wait_recv()


def analysis(hidden_pre, cotangent, table_z, axis, count):
    channels, nx, ny, nz = hidden_pre.shape
    modes = table_z.shape[0]
    steps = nx // XB
    field_spec = pl.BlockSpec((channels, XB, ny, nz), lambda i: (0, i, 0, 0))
    return pl.pallas_call(
        functools.partial(analysis_kernel, axis, count),
        grid=(steps,),
        in_specs=[field_spec, field_spec, pl.BlockSpec((modes, nz), lambda i: (0, 0))],
        out_specs=[
            pl.BlockSpec(memory_space=pl.ANY),
            pl.BlockSpec((channels, channels), lambda i: (0, 0)),
        ],
        out_shape=[
            jax.ShapeDtypeStruct(
                (count, modes // count, 2 * channels, nx * ny), jnp.bfloat16),
            jax.ShapeDtypeStruct((channels, channels), jnp.float32),
        ],
        scratch_shapes=[
            pltpu.VMEM((channels * ny, channels * ny), jnp.float32),
            pltpu.VMEM((modes, 2 * channels, XB * ny), jnp.float32),
            pltpu.VMEM((2, modes, 2 * channels, XB * ny), jnp.bfloat16),
            pltpu.SemaphoreType.DMA((steps,)),
            pltpu.SemaphoreType.DMA((steps, count)),
            pltpu.SemaphoreType.DMA((steps, count)),
        ],
        compiler_params=pltpu.CompilerParams(
            dimension_semantics=("arbitrary",), vmem_limit_bytes=60 * 1024 * 1024,
            collective_id=0, has_side_effects=True,
        ),
    )(hidden_pre, cotangent, table_z)


def exchange_kernel(axis, count, src_ref, dst_ref, local_sem, send_sems, recv_sems):
    mesh_ids = pl.DeviceIdType.MESH
    me = lax.axis_index(axis)
    barrier = pltpu.get_barrier_semaphore()
    for k in range(1, count):
        peer = lax.rem(me + k, count)
        pl.semaphore_signal(barrier, inc=1, device_id={axis: peer}, device_id_type=mesh_ids)
    pl.semaphore_wait(barrier, count - 1)
    local = pltpu.make_async_copy(src_ref.at[me], dst_ref.at[me], local_sem)
    local.start()
    sends = []
    for k in range(1, count):
        peer = lax.rem(me + k, count)
        copy = pltpu.make_async_remote_copy(
            src_ref=src_ref.at[peer],
            dst_ref=dst_ref.at[me],
            send_sem=send_sems.at[k],
            recv_sem=recv_sems.at[k],
            device_id={axis: peer},
            device_id_type=mesh_ids,
        )
        copy.start()
        sends.append(copy)
    local.wait()
    for k in range(1, count):
        sends[k - 1].wait_send()
        origin = lax.rem(me + count - k, count)
        incoming = pltpu.make_async_remote_copy(
            src_ref=src_ref.at[me],
            dst_ref=dst_ref.at[origin],
            send_sem=send_sems.at[k],
            recv_sem=recv_sems.at[k],
            device_id={axis: origin},
            device_id_type=mesh_ids,
        )
        incoming.wait_recv()


def exchange(chunks, axis, count, collective_id):
    return pl.pallas_call(
        functools.partial(exchange_kernel, axis, count),
        in_specs=[pl.BlockSpec(memory_space=pl.ANY)],
        out_specs=pl.BlockSpec(memory_space=pl.ANY),
        out_shape=jax.ShapeDtypeStruct(chunks.shape, chunks.dtype),
        scratch_shapes=[
            pltpu.SemaphoreType.DMA,
            pltpu.SemaphoreType.DMA((count,)),
            pltpu.SemaphoreType.DMA((count,)),
        ],
        compiler_params=pltpu.CompilerParams(collective_id=collective_id, has_side_effects=True),
    )(chunks)


def synthesis_kernel(h_ref, g_ref, ys_ref, tz_ref, sw_ref, out_ref, ks_ref):
    channels, xb, ny, nz = h_ref.shape
    rows = channels * ny

    @pl.when(pl.program_id(0) == 0)
    def _():
        r = lax.broadcasted_iota(jnp.int32, (rows, channels), 0)
        k = lax.broadcasted_iota(jnp.int32, (rows, channels), 1)
        expand = (r // ny == k).astype(jnp.float32)
        spread = jnp.dot(expand, sw_ref[...].astype(jnp.float32), preferred_element_type=jnp.float32)
        kr = lax.broadcasted_iota(jnp.int32, (channels, rows), 0)
        kc = lax.broadcasted_iota(jnp.int32, (channels, rows), 1)
        expand_t = (kc // ny == kr).astype(jnp.float32)
        full = jnp.dot(spread, expand_t, preferred_element_type=jnp.float32)
        ri = lax.broadcasted_iota(jnp.int32, (rows, rows), 0)
        ci = lax.broadcasted_iota(jnp.int32, (rows, rows), 1)
        ks_ref[...] = jnp.where(ri % ny == ci % ny, full, 0.0).astype(ks_ref.dtype)

    tz = tz_ref[...]
    ks = ks_ref[...]
    ys = ys_ref[...].astype(jnp.float32)
    for x in range(xb):
        lo = ys[:, 2 * x, :]
        hi = ys[:, 2 * x + 1, :]
        lhs = jnp.concatenate([lo, hi], axis=0).T.astype(jnp.bfloat16)
        spec = jnp.dot(lhs, tz, preferred_element_type=jnp.float32)
        spec = spec.astype(jnp.bfloat16).astype(jnp.float32)
        skip = jnp.dot(ks, g_ref[:, x].reshape(channels * ny, nz), preferred_element_type=jnp.float32)
        activ = jnp.tanh(h_ref[:, x].astype(jnp.float32)).reshape(channels * ny, nz)
        grad = (spec + skip) * (1.0 - activ * activ)
        out_ref[:, x] = grad.astype(jnp.bfloat16).reshape(channels, ny, nz)


def synthesis(hidden_pre, cotangent, ysynth, table_z, skip_weight):
    channels, nx, ny, nz = hidden_pre.shape
    modes = table_z.shape[0]
    steps = nx // XB
    field_spec = pl.BlockSpec((channels, XB, ny, nz), lambda i: (0, i, 0, 0))
    return pl.pallas_call(
        synthesis_kernel,
        grid=(steps,),
        in_specs=[
            field_spec,
            field_spec,
            pl.BlockSpec((ysynth.shape[0], 2 * XB, channels * ny), lambda i: (0, i, 0)),
            pl.BlockSpec((modes, nz), lambda i: (0, 0)),
            pl.BlockSpec((channels, channels), lambda i: (0, 0)),
        ],
        out_specs=field_spec,
        out_shape=jax.ShapeDtypeStruct(hidden_pre.shape, jnp.bfloat16),
        scratch_shapes=[pltpu.VMEM((channels * ny, channels * ny), jnp.bfloat16)],
        compiler_params=pltpu.CompilerParams(
            dimension_semantics=("arbitrary",), vmem_limit_bytes=60 * 1024 * 1024
        ),
    )(hidden_pre, cotangent, ysynth, table_z, skip_weight)


def y_synthesis_kernel(xs_ref, tyt_ref, out_ref, stage_ref):
    mz_local, channels, modes, nx = xs_ref.shape
    blocks, _, lanes = out_ref.shape
    ny = lanes // channels
    tyt = jnp.broadcast_to(tyt_ref[...][None], (channels,) + tyt_ref.shape)
    for z in range(mz_local):
        part = jnp.einsum(
            "cym,cmx->cyx", tyt, xs_ref[z], preferred_element_type=jnp.float32
        ).astype(jnp.bfloat16).astype(jnp.float32)
        for d in range(blocks):
            piece = part[:, d * ny:(d + 1) * ny, :].reshape(channels * ny, nx).T
            for q in range(lanes // 128):
                stage_ref[d * (lanes // 128) + q, pl.ds(z, nx, stride=mz_local), :] = (
                    piece[:, q * 128:(q + 1) * 128])
    for d in range(blocks):
        for q in range(lanes // 128):
            out_ref[d, :, q * 128:(q + 1) * 128] = (
                stage_ref[d * (lanes // 128) + q].astype(out_ref.dtype))


def y_synthesis(xsynth, table_yt, blocks):
    mz_local, channels, modes, nx = xsynth.shape
    ny = table_yt.shape[0] // blocks
    vmem = pl.BlockSpec(memory_space=pltpu.VMEM)
    return pl.pallas_call(
        y_synthesis_kernel,
        in_specs=[vmem, vmem],
        out_specs=vmem,
        out_shape=jax.ShapeDtypeStruct((blocks, nx * mz_local, channels * ny), jnp.bfloat16),
        scratch_shapes=[
            pltpu.VMEM((blocks * channels * ny // 128, nx * mz_local, 128), jnp.float32)
        ],
    )(xsynth, table_yt)


def modes_kernel(sp_ref, w_ref, gm_ref, bs_ref):
    highest = lax.Precision.HIGHEST
    channels = sp_ref.shape[1] // 2
    width = channels * channels
    sp = sp_ref[...]
    er = lax.broadcasted_iota(jnp.int32, (channels, width), 0)
    ec = lax.broadcasted_iota(jnp.int32, (channels, width), 1)
    spread = (ec // channels == er).astype(jnp.float32)
    tile = (ec % channels == er).astype(jnp.float32)
    s_rep = jnp.dot(sp[:, :channels], spread, precision=highest, preferred_element_type=jnp.float32)
    q_rep = jnp.dot(sp[:, channels:], tile, precision=highest, preferred_element_type=jnp.float32)
    gm_ref[...] = s_rep * q_rep
    weighted = w_ref[...].astype(jnp.float32) * q_rep
    back = lax.dot_general(
        weighted, spread, (((1,), (1,)), ((), ())), precision=highest,
        preferred_element_type=jnp.float32)
    bs_ref[...] = back.astype(bs_ref.dtype)


def modes_step(spectra, weights):
    rows, both = spectra.shape
    channels = both // 2
    vmem = pl.BlockSpec(memory_space=pltpu.VMEM)
    return pl.pallas_call(
        modes_kernel,
        in_specs=[vmem, vmem],
        out_specs=[vmem, vmem],
        out_shape=[
            jax.ShapeDtypeStruct((rows, channels * channels), jnp.float32),
            jax.ShapeDtypeStruct((rows, channels), jnp.bfloat16),
        ],
    )(spectra, weights)


def per_device(hidden_pre, cotangent, mode_weight, skip_weight):
    highest = lax.Precision.HIGHEST
    channels, nx, ny, nz = hidden_pre.shape
    mode_count = mode_weight.shape[2]
    n_narrow = lax.axis_size("narrow")
    n_wide = lax.axis_size("wide")
    table_x = basis_table(mode_count, NX)
    table_y = basis_table(mode_count, NY)
    table_z = basis_table(mode_count, NZ)

    zc, gram = analysis(hidden_pre, cotangent, table_z, "narrow", n_narrow)
    mz_local = mode_count // n_narrow
    zc = zc.reshape(n_narrow, mz_local, 2 * channels, nx, ny)
    ycoeffs = jnp.einsum(
        "smcxl,nsl->mcnx", zc, table_y.reshape(mode_count, n_narrow, ny),
        preferred_element_type=jnp.float32,
    ).astype(jnp.bfloat16)
    ycoeffs = lax.all_to_all(ycoeffs, "wide", split_axis=2, concat_axis=3, tiled=True)
    spectra = jnp.einsum("zcyx,kx->zykc", ycoeffs, table_x, preferred_element_type=jnp.float32)
    z_local, y_local = (spectra.shape[0], spectra.shape[1])
    grad_modes, back_spec = modes_step(
        spectra.reshape(z_local * y_local * mode_count, 2 * channels),
        mode_weight.reshape(z_local * y_local * mode_count, channels * channels),
    )
    grad_modes = grad_modes.reshape(z_local, y_local, mode_count, channels * channels)
    back_spec = jnp.transpose(
        back_spec.reshape(z_local, y_local, mode_count, channels), (0, 3, 1, 2)
    )
    xsynth = jnp.einsum(
        "zcyk,kx->zcyx", back_spec, table_x, preferred_element_type=jnp.float32
    ).astype(jnp.bfloat16)
    xsynth = lax.all_to_all(xsynth, "wide", split_axis=3, concat_axis=2, tiled=True)
    ysynth = y_synthesis(xsynth, jnp.transpose(table_y), n_narrow)
    ysynth = exchange(ysynth, "narrow", n_narrow, 1)
    table_zp = jnp.transpose(table_z.reshape(n_narrow, mz_local, nz), (1, 0, 2)).reshape(mode_count, nz)
    grad_hidden = synthesis(hidden_pre, cotangent, ysynth, table_zp, skip_weight)

    total = gram.reshape(1, channels * channels)
    for axis, count in (("narrow", n_narrow), ("wide", n_wide)):
        spread = jnp.broadcast_to(total, (count, channels * channels))
        total = lax.all_to_all(spread, axis, 0, 0, tiled=True).sum(0, keepdims=True)
    grad_skip = total.reshape(channels, channels) * (1.0 / math.sqrt(NX * NY * NZ))
    return (grad_hidden, grad_modes, grad_skip)


def solution(mesh):
    in_specs = (
        P(None, "wide", "narrow", None),
        P(None, "wide", "narrow", None),
        P("narrow", "wide", None, None),
        P(),
    )
    out_specs = (P(None, "wide", "narrow", None), P("narrow", "wide", None, None), P())
    return jax.shard_map(
        per_device, mesh=mesh, in_specs=in_specs, out_specs=out_specs, check_vma=False
    )
```

```python
import functools
import math

import jax
import jax.numpy as jnp
from jax import lax
from jax.experimental import pallas as pl
from jax.experimental.pallas import tpu as pltpu
from jax.sharding import PartitionSpec as P

NX = 256
NY = 256
NZ = 256
XB = 8


def basis_table(mode_count, length):
    mode_index = jnp.arange(mode_count, dtype=jnp.int32)
    halfway = mode_count // 2
    frequency = jnp.where(mode_index < halfway, mode_index, mode_index - halfway + 1)
    points = jnp.arange(length, dtype=jnp.int32)
    phases = frequency[:, None] * points[None, :] % length
    angles = phases.astype(jnp.float32) * (2.0 * math.pi / length)
    values_table = jnp.where((mode_index < halfway)[:, None], jnp.cos(angles), jnp.sin(angles))
    return (values_table * (1.0 / math.sqrt(length))).astype(jnp.bfloat16)


def _nt(a, b):
    return lax.dot_general(a, b, (((1,), (1,)), ((), ())), preferred_element_type=jnp.float32)


def analysis_kernel(axis, count, h_ref, g_ref, tz_ref, zc_ref, gram_ref, acc_ref, stage_ref,
                    slot_ref, local_sems, send_sems, recv_sems):
    mesh_ids = pl.DeviceIdType.MESH
    step = pl.program_id(0)
    steps = pl.num_programs(0)
    channels, xb, ny, nz = h_ref.shape
    width = xb * ny
    mz_local = slot_ref.shape[1] // count
    me = lax.axis_index(axis)

    def copies(at):
        slot = lax.rem(at, 2)
        cols = pl.ds(pl.multiple_of(at * width, width), width)
        local = pltpu.make_async_copy(
            slot_ref.at[slot, pl.ds(me * mz_local, mz_local)],
            zc_ref.at[me, :, :, cols],
            local_sems.at[at],
        )
        remote = []
        for k in range(1, count):
            peer = lax.rem(me + k, count)
            remote.append(pltpu.make_async_remote_copy(
                src_ref=slot_ref.at[slot, pl.ds(peer * mz_local, mz_local)],
                dst_ref=zc_ref.at[me, :, :, cols],
                send_sem=send_sems.at[at, k],
                recv_sem=recv_sems.at[at, k],
                device_id={axis: peer},
                device_id_type=mesh_ids,
            ))
        return local, remote

    def wait_sent(at):
        local, remote = copies(at)
        local.wait()
        for copy in remote:
            copy.wait_send()

    @pl.when(step == 0)
    def _():
        acc_ref[...] = jnp.zeros_like(acc_ref)
        barrier = pltpu.get_barrier_semaphore()
        for k in range(1, count):
            peer = lax.rem(me + k, count)
            pl.semaphore_signal(barrier, inc=1, device_id={axis: peer}, device_id_type=mesh_ids)
        pl.semaphore_wait(barrier, count - 1)

    @pl.when(step >= 2)
    def _():
        wait_sent(step - 2)

    tz = tz_ref[...]
    li = jnp.tanh(h_ref[...].astype(jnp.float32)).astype(jnp.bfloat16)
    g = g_ref[...]
    zl = _nt(tz, li.reshape(channels * width, nz))
    zg = _nt(tz, g.reshape(channels * width, nz))
    for c in range(channels):
        stage_ref[:, c, :] = zl[:, c * width:(c + 1) * width]
        stage_ref[:, channels + c, :] = zg[:, c * width:(c + 1) * width]
    slot_ref[lax.rem(step, 2)] = stage_ref[...].astype(jnp.bfloat16)
    local, remote = copies(step)
    local.start()
    for copy in remote:
        copy.start()
    for x in range(xb):
        acc_ref[...] += _nt(li[:, x].reshape(channels * ny, nz), g[:, x].reshape(channels * ny, nz))

    @pl.when(step == steps - 1)
    def _():
        rows = channels * ny
        ri = lax.broadcasted_iota(jnp.int32, (rows, rows), 0)
        ci = lax.broadcasted_iota(jnp.int32, (rows, rows), 1)
        diag = jnp.where(ri % ny == ci % ny, acc_ref[...], 0.0)
        er = lax.broadcasted_iota(jnp.int32, (channels, rows), 0)
        ec = lax.broadcasted_iota(jnp.int32, (channels, rows), 1)
        gather = (ec // ny == er).astype(jnp.float32)
        part = jnp.dot(gather, diag, precision=lax.Precision.HIGHEST, preferred_element_type=jnp.float32)
        gram_ref[...] = lax.dot_general(
            part, gather, (((1,), (1,)), ((), ())), precision=lax.Precision.HIGHEST,
            preferred_element_type=jnp.float32)
        wait_sent(step - 1)
        wait_sent(step)
        for at in range(zc_ref.shape[3] // width):
            cols = pl.ds(at * width, width)
            for k in range(1, count):
                origin = lax.rem(me + count - k, count)
                pltpu.make_async_remote_copy(
                    src_ref=slot_ref.at[0, pl.ds(me * mz_local, mz_local)],
                    dst_ref=zc_ref.at[origin, :, :, cols],
                    send_sem=send_sems.at[at, k],
                    recv_sem=recv_sems.at[at, k],
                    device_id={axis: origin},
                    device_id_type=mesh_ids,
                ).wait_recv()


def analysis(hidden_pre, cotangent, table_z, axis, count):
    channels, nx, ny, nz = hidden_pre.shape
    modes = table_z.shape[0]
    steps = nx // XB
    field_spec = pl.BlockSpec((channels, XB, ny, nz), lambda i: (0, i, 0, 0))
    return pl.pallas_call(
        functools.partial(analysis_kernel, axis, count),
        grid=(steps,),
        in_specs=[field_spec, field_spec, pl.BlockSpec((modes, nz), lambda i: (0, 0))],
        out_specs=[
            pl.BlockSpec(memory_space=pl.ANY),
            pl.BlockSpec((channels, channels), lambda i: (0, 0)),
        ],
        out_shape=[
            jax.ShapeDtypeStruct(
                (count, modes // count, 2 * channels, nx * ny), jnp.bfloat16),
            jax.ShapeDtypeStruct((channels, channels), jnp.float32),
        ],
        scratch_shapes=[
            pltpu.VMEM((channels * ny, channels * ny), jnp.float32),
            pltpu.VMEM((modes, 2 * channels, XB * ny), jnp.float32),
            pltpu.VMEM((2, modes, 2 * channels, XB * ny), jnp.bfloat16),
            pltpu.SemaphoreType.DMA((steps,)),
            pltpu.SemaphoreType.DMA((steps, count)),
            pltpu.SemaphoreType.DMA((steps, count)),
        ],
        compiler_params=pltpu.CompilerParams(
            dimension_semantics=("arbitrary",), vmem_limit_bytes=60 * 1024 * 1024,
            collective_id=0, has_side_effects=True,
        ),
    )(hidden_pre, cotangent, table_z)


def synthesis_kernel(axis, count, h_ref, g_ref, xs_ref, tyt_ref, tz_ref, sw_ref, out_ref,
                     ks_ref, stage_ref, send_ref, recv_ref, local_sems, send_sems, recv_sems):
    mesh_ids = pl.DeviceIdType.MESH
    step = pl.program_id(0)
    steps = pl.num_programs(0)
    channels, xb, ny, nz = h_ref.shape
    rows = channels * ny
    chunk = 2 * xb
    me = lax.axis_index(axis)

    def copies(at):
        part = pl.ds(pl.multiple_of(at * chunk, chunk), chunk)
        local = pltpu.make_async_copy(
            send_ref.at[me, part], recv_ref.at[me, part], local_sems.at[at])
        remote = []
        for k in range(1, count):
            peer = lax.rem(me + k, count)
            remote.append(pltpu.make_async_remote_copy(
                src_ref=send_ref.at[peer, part],
                dst_ref=recv_ref.at[me, part],
                send_sem=send_sems.at[at, k],
                recv_sem=recv_sems.at[at, k],
                device_id={axis: peer},
                device_id_type=mesh_ids,
            ))
        return local, remote

    @pl.when(step == 0)
    def _():
        barrier = pltpu.get_barrier_semaphore()
        for k in range(1, count):
            peer = lax.rem(me + k, count)
            pl.semaphore_signal(barrier, inc=1, device_id={axis: peer}, device_id_type=mesh_ids)
        pl.semaphore_wait(barrier, count - 1)
        y_synthesis_body(xs_ref, tyt_ref, send_ref, stage_ref)
        for at in range(recv_ref.shape[1] // chunk):
            local, remote = copies(at)
            local.start()
            for copy in remote:
                copy.start()
        r = lax.broadcasted_iota(jnp.int32, (rows, channels), 0)
        k = lax.broadcasted_iota(jnp.int32, (rows, channels), 1)
        expand = (r // ny == k).astype(jnp.float32)
        spread = jnp.dot(expand, sw_ref[...].astype(jnp.float32), preferred_element_type=jnp.float32)
        kr = lax.broadcasted_iota(jnp.int32, (channels, rows), 0)
        kc = lax.broadcasted_iota(jnp.int32, (channels, rows), 1)
        expand_t = (kc // ny == kr).astype(jnp.float32)
        full = jnp.dot(spread, expand_t, preferred_element_type=jnp.float32)
        ri = lax.broadcasted_iota(jnp.int32, (rows, rows), 0)
        ci = lax.broadcasted_iota(jnp.int32, (rows, rows), 1)
        ks_ref[...] = jnp.where(ri % ny == ci % ny, full, 0.0).astype(ks_ref.dtype)

    local, _ = copies(step)
    local.wait()
    part = pl.ds(pl.multiple_of(step * chunk, chunk), chunk)
    for k in range(1, count):
        origin = lax.rem(me + count - k, count)
        pltpu.make_async_remote_copy(
            src_ref=send_ref.at[me, part],
            dst_ref=recv_ref.at[origin, part],
            send_sem=send_sems.at[step, k],
            recv_sem=recv_sems.at[step, k],
            device_id={axis: origin},
            device_id_type=mesh_ids,
        ).wait_recv()

    tz = tz_ref[...]
    ks = ks_ref[...]
    ys = recv_ref[:, part, :].astype(jnp.float32)
    for x in range(xb):
        lo = ys[:, 2 * x, :]
        hi = ys[:, 2 * x + 1, :]
        lhs = jnp.concatenate([lo, hi], axis=0).T.astype(jnp.bfloat16)
        spec = jnp.dot(lhs, tz, preferred_element_type=jnp.float32)
        spec = spec.astype(jnp.bfloat16).astype(jnp.float32)
        skip = jnp.dot(ks, g_ref[:, x].reshape(channels * ny, nz), preferred_element_type=jnp.float32)
        activ = jnp.tanh(h_ref[:, x].astype(jnp.float32)).reshape(channels * ny, nz)
        grad = (spec + skip) * (1.0 - activ * activ)
        out_ref[:, x] = grad.astype(jnp.bfloat16).reshape(channels, ny, nz)

    @pl.when(step == steps - 1)
    def _():
        for at in range(recv_ref.shape[1] // chunk):
            _, remote = copies(at)
            for copy in remote:
                copy.wait_send()


def synthesis(hidden_pre, cotangent, xsynth, table_yt, table_z, skip_weight, axis, count):
    channels, nx, ny, nz = hidden_pre.shape
    modes = table_z.shape[0]
    mz_local = xsynth.shape[0]
    steps = nx // XB
    field_spec = pl.BlockSpec((channels, XB, ny, nz), lambda i: (0, i, 0, 0))
    whole = pl.BlockSpec(memory_space=pltpu.VMEM)
    lanes = channels * ny
    return pl.pallas_call(
        functools.partial(synthesis_kernel, axis, count),
        grid=(steps,),
        in_specs=[
            field_spec,
            field_spec,
            whole,
            whole,
            pl.BlockSpec((modes, nz), lambda i: (0, 0)),
            pl.BlockSpec((channels, channels), lambda i: (0, 0)),
        ],
        out_specs=field_spec,
        out_shape=jax.ShapeDtypeStruct(hidden_pre.shape, jnp.bfloat16),
        scratch_shapes=[
            pltpu.VMEM((lanes, lanes), jnp.bfloat16),
            pltpu.VMEM((count * lanes // 128, nx * mz_local, 128), jnp.float32),
            pltpu.VMEM((count, nx * mz_local, lanes), jnp.bfloat16),
            pltpu.VMEM((count, nx * mz_local, lanes), jnp.bfloat16),
            pltpu.SemaphoreType.DMA((steps,)),
            pltpu.SemaphoreType.DMA((steps, count)),
            pltpu.SemaphoreType.DMA((steps, count)),
        ],
        compiler_params=pltpu.CompilerParams(
            dimension_semantics=("arbitrary",), vmem_limit_bytes=60 * 1024 * 1024,
            collective_id=1, has_side_effects=True,
        ),
    )(hidden_pre, cotangent, xsynth, table_yt, table_z, skip_weight)


def y_synthesis_body(xs_ref, tyt_ref, out_ref, stage_ref):
    mz_local, channels, modes, nx = xs_ref.shape
    blocks, _, lanes = out_ref.shape
    ny = lanes // channels
    tyt = jnp.broadcast_to(tyt_ref[...][None], (channels,) + tyt_ref.shape)
    for z in range(mz_local):
        part = jnp.einsum(
            "cym,cmx->cyx", tyt, xs_ref[z], preferred_element_type=jnp.float32
        ).astype(jnp.bfloat16).astype(jnp.float32)
        for d in range(blocks):
            piece = part[:, d * ny:(d + 1) * ny, :].reshape(channels * ny, nx).T
            for q in range(lanes // 128):
                stage_ref[d * (lanes // 128) + q, pl.ds(z, nx, stride=mz_local), :] = (
                    piece[:, q * 128:(q + 1) * 128])
    for d in range(blocks):
        for q in range(lanes // 128):
            out_ref[d, :, q * 128:(q + 1) * 128] = (
                stage_ref[d * (lanes // 128) + q].astype(out_ref.dtype))


def modes_kernel(sp_ref, w_ref, gm_ref, bs_ref):
    highest = lax.Precision.HIGHEST
    channels = sp_ref.shape[1] // 2
    width = channels * channels
    sp = sp_ref[...]
    er = lax.broadcasted_iota(jnp.int32, (channels, width), 0)
    ec = lax.broadcasted_iota(jnp.int32, (channels, width), 1)
    spread = (ec // channels == er).astype(jnp.float32)
    tile = (ec % channels == er).astype(jnp.float32)
    s_rep = jnp.dot(sp[:, :channels], spread, precision=highest, preferred_element_type=jnp.float32)
    q_rep = jnp.dot(sp[:, channels:], tile, precision=highest, preferred_element_type=jnp.float32)
    gm_ref[...] = s_rep * q_rep
    weighted = w_ref[...].astype(jnp.float32) * q_rep
    back = lax.dot_general(
        weighted, spread, (((1,), (1,)), ((), ())), precision=highest,
        preferred_element_type=jnp.float32)
    bs_ref[...] = back.astype(bs_ref.dtype)


def modes_step(spectra, weights):
    rows, both = spectra.shape
    channels = both // 2
    vmem = pl.BlockSpec(memory_space=pltpu.VMEM)
    return pl.pallas_call(
        modes_kernel,
        in_specs=[vmem, vmem],
        out_specs=[vmem, vmem],
        out_shape=[
            jax.ShapeDtypeStruct((rows, channels * channels), jnp.float32),
            jax.ShapeDtypeStruct((rows, channels), jnp.bfloat16),
        ],
    )(spectra, weights)


def per_device(hidden_pre, cotangent, mode_weight, skip_weight):
    highest = lax.Precision.HIGHEST
    channels, nx, ny, nz = hidden_pre.shape
    mode_count = mode_weight.shape[2]
    n_narrow = lax.axis_size("narrow")
    n_wide = lax.axis_size("wide")
    table_x = basis_table(mode_count, NX)
    table_y = basis_table(mode_count, NY)
    table_z = basis_table(mode_count, NZ)

    zc, gram = analysis(hidden_pre, cotangent, table_z, "narrow", n_narrow)
    mz_local = mode_count // n_narrow
    zc = zc.reshape(n_narrow, mz_local, 2 * channels, nx, ny)
    ycoeffs = jnp.einsum(
        "smcxl,nsl->mcnx", zc, table_y.reshape(mode_count, n_narrow, ny),
        preferred_element_type=jnp.float32,
    ).astype(jnp.bfloat16)
    ycoeffs = lax.all_to_all(ycoeffs, "wide", split_axis=2, concat_axis=3, tiled=True)
    spectra = jnp.einsum("zcyx,kx->zykc", ycoeffs, table_x, preferred_element_type=jnp.float32)
    z_local, y_local = (spectra.shape[0], spectra.shape[1])
    grad_modes, back_spec = modes_step(
        spectra.reshape(z_local * y_local * mode_count, 2 * channels),
        mode_weight.reshape(z_local * y_local * mode_count, channels * channels),
    )
    grad_modes = grad_modes.reshape(z_local, y_local, mode_count, channels * channels)
    back_spec = jnp.transpose(
        back_spec.reshape(z_local, y_local, mode_count, channels), (0, 3, 1, 2)
    )
    xsynth = jnp.einsum(
        "zcyk,kx->zcyx", back_spec, table_x, preferred_element_type=jnp.float32
    ).astype(jnp.bfloat16)
    xsynth = lax.all_to_all(xsynth, "wide", split_axis=3, concat_axis=2, tiled=True)
    table_zp = jnp.transpose(table_z.reshape(n_narrow, mz_local, nz), (1, 0, 2)).reshape(mode_count, nz)
    grad_hidden = synthesis(
        hidden_pre, cotangent, xsynth, jnp.transpose(table_y), table_zp, skip_weight,
        "narrow", n_narrow)

    total = gram.reshape(1, channels * channels)
    for axis, count in (("narrow", n_narrow), ("wide", n_wide)):
        spread = jnp.broadcast_to(total, (count, channels * channels))
        total = lax.all_to_all(spread, axis, 0, 0, tiled=True).sum(0, keepdims=True)
    grad_skip = total.reshape(channels, channels) * (1.0 / math.sqrt(NX * NY * NZ))
    return (grad_hidden, grad_modes, grad_skip)


def solution(mesh):
    in_specs = (
        P(None, "wide", "narrow", None),
        P(None, "wide", "narrow", None),
        P("narrow", "wide", None, None),
        P(),
    )
    out_specs = (P(None, "wide", "narrow", None), P("narrow", "wide", None, None), P())
    return jax.shard_map(
        per_device, mesh=mesh, in_specs=in_specs, out_specs=out_specs, check_vma=False
    )
```

```python
import functools
import math

import jax
import jax.numpy as jnp
from jax import lax
from jax.experimental import pallas as pl
from jax.experimental.pallas import tpu as pltpu
from jax.sharding import PartitionSpec as P

NX = 256
NY = 256
NZ = 256
XB = 8


def basis_table(mode_count, length):
    mode_index = jnp.arange(mode_count, dtype=jnp.int32)
    halfway = mode_count // 2
    frequency = jnp.where(mode_index < halfway, mode_index, mode_index - halfway + 1)
    points = jnp.arange(length, dtype=jnp.int32)
    phases = frequency[:, None] * points[None, :] % length
    angles = phases.astype(jnp.float32) * (2.0 * math.pi / length)
    values_table = jnp.where((mode_index < halfway)[:, None], jnp.cos(angles), jnp.sin(angles))
    return (values_table * (1.0 / math.sqrt(length))).astype(jnp.bfloat16)


def _nt(a, b):
    return lax.dot_general(a, b, (((1,), (1,)), ((), ())), preferred_element_type=jnp.float32)


def analysis_kernel(axis, count, h_ref, g_ref, tz_ref, zc_ref, gram_ref, acc_ref, stage_ref,
                    slot_ref, local_sems, send_sems, recv_sems, gstage_ref, gbuf_ref, glocal_sem,
                    gsend_sems, grecv_sems):
    mesh_ids = pl.DeviceIdType.MESH
    step = pl.program_id(0)
    steps = pl.num_programs(0)
    channels, xb, ny, nz = h_ref.shape
    width = xb * ny
    mz_local = slot_ref.shape[1] // count
    me = lax.axis_index(axis)

    def copies(at):
        slot = lax.rem(at, 2)
        cols = pl.ds(pl.multiple_of(at * width, width), width)
        local = pltpu.make_async_copy(
            slot_ref.at[slot, pl.ds(me * mz_local, mz_local)],
            zc_ref.at[me, :, :, cols],
            local_sems.at[at],
        )
        remote = []
        for k in range(1, count):
            peer = lax.rem(me + k, count)
            remote.append(pltpu.make_async_remote_copy(
                src_ref=slot_ref.at[slot, pl.ds(peer * mz_local, mz_local)],
                dst_ref=zc_ref.at[me, :, :, cols],
                send_sem=send_sems.at[at, k],
                recv_sem=recv_sems.at[at, k],
                device_id={axis: peer},
                device_id_type=mesh_ids,
            ))
        return local, remote

    def wait_sent(at):
        local, remote = copies(at)
        local.wait()
        for copy in remote:
            copy.wait_send()

    @pl.when(step == 0)
    def _():
        acc_ref[...] = jnp.zeros_like(acc_ref)
        barrier = pltpu.get_barrier_semaphore()
        for k in range(1, count):
            peer = lax.rem(me + k, count)
            pl.semaphore_signal(barrier, inc=1, device_id={axis: peer}, device_id_type=mesh_ids)
        pl.semaphore_wait(barrier, count - 1)

    @pl.when(step >= 2)
    def _():
        wait_sent(step - 2)

    tz = tz_ref[...]
    li = jnp.tanh(h_ref[...].astype(jnp.float32)).astype(jnp.bfloat16)
    g = g_ref[...]
    zl = _nt(tz, li.reshape(channels * width, nz))
    zg = _nt(tz, g.reshape(channels * width, nz))
    for c in range(channels):
        stage_ref[:, c, :] = zl[:, c * width:(c + 1) * width]
        stage_ref[:, channels + c, :] = zg[:, c * width:(c + 1) * width]
    slot_ref[lax.rem(step, 2)] = stage_ref[...].astype(jnp.bfloat16)
    local, remote = copies(step)
    local.start()
    for copy in remote:
        copy.start()
    for x in range(xb):
        acc_ref[...] += _nt(li[:, x].reshape(channels * ny, nz), g[:, x].reshape(channels * ny, nz))

    @pl.when(step == steps - 1)
    def _():
        rows = channels * ny
        ri = lax.broadcasted_iota(jnp.int32, (rows, rows), 0)
        ci = lax.broadcasted_iota(jnp.int32, (rows, rows), 1)
        diag = jnp.where(ri % ny == ci % ny, acc_ref[...], 0.0)
        er = lax.broadcasted_iota(jnp.int32, (channels, rows), 0)
        ec = lax.broadcasted_iota(jnp.int32, (channels, rows), 1)
        gather = (ec // ny == er).astype(jnp.float32)
        part = jnp.dot(gather, diag, precision=lax.Precision.HIGHEST, preferred_element_type=jnp.float32)
        gstage_ref[...] = lax.dot_general(
            part, gather, (((1,), (1,)), ((), ())), precision=lax.Precision.HIGHEST,
            preferred_element_type=jnp.float32)
        glocal = pltpu.make_async_copy(gstage_ref, gbuf_ref.at[me], glocal_sem)
        glocal.start()
        gsends = []
        for k in range(1, count):
            peer = lax.rem(me + k, count)
            copy = pltpu.make_async_remote_copy(
                src_ref=gstage_ref,
                dst_ref=gbuf_ref.at[me],
                send_sem=gsend_sems.at[k],
                recv_sem=grecv_sems.at[k],
                device_id={axis: peer},
                device_id_type=mesh_ids,
            )
            copy.start()
            gsends.append(copy)
        glocal.wait()
        for k in range(1, count):
            gsends[k - 1].wait_send()
            origin = lax.rem(me + count - k, count)
            pltpu.make_async_remote_copy(
                src_ref=gstage_ref,
                dst_ref=gbuf_ref.at[origin],
                send_sem=gsend_sems.at[k],
                recv_sem=grecv_sems.at[k],
                device_id={axis: origin},
                device_id_type=mesh_ids,
            ).wait_recv()
        total = gbuf_ref[0]
        for src in range(1, count):
            total = total + gbuf_ref[src]
        gram_ref[...] = total
        wait_sent(step - 1)
        wait_sent(step)
        for at in range(zc_ref.shape[3] // width):
            cols = pl.ds(at * width, width)
            for k in range(1, count):
                origin = lax.rem(me + count - k, count)
                pltpu.make_async_remote_copy(
                    src_ref=slot_ref.at[0, pl.ds(me * mz_local, mz_local)],
                    dst_ref=zc_ref.at[origin, :, :, cols],
                    send_sem=send_sems.at[at, k],
                    recv_sem=recv_sems.at[at, k],
                    device_id={axis: origin},
                    device_id_type=mesh_ids,
                ).wait_recv()


def analysis(hidden_pre, cotangent, table_z, axis, count):
    channels, nx, ny, nz = hidden_pre.shape
    modes = table_z.shape[0]
    steps = nx // XB
    field_spec = pl.BlockSpec((channels, XB, ny, nz), lambda i: (0, i, 0, 0))
    return pl.pallas_call(
        functools.partial(analysis_kernel, axis, count),
        grid=(steps,),
        in_specs=[field_spec, field_spec, pl.BlockSpec((modes, nz), lambda i: (0, 0))],
        out_specs=[
            pl.BlockSpec(memory_space=pl.ANY),
            pl.BlockSpec((channels, channels), lambda i: (0, 0)),
        ],
        out_shape=[
            jax.ShapeDtypeStruct(
                (count, modes // count, 2 * channels, nx * ny), jnp.bfloat16),
            jax.ShapeDtypeStruct((channels, channels), jnp.float32),
        ],
        scratch_shapes=[
            pltpu.VMEM((channels * ny, channels * ny), jnp.float32),
            pltpu.VMEM((modes, 2 * channels, XB * ny), jnp.float32),
            pltpu.VMEM((2, modes, 2 * channels, XB * ny), jnp.bfloat16),
            pltpu.SemaphoreType.DMA((steps,)),
            pltpu.SemaphoreType.DMA((steps, count)),
            pltpu.SemaphoreType.DMA((steps, count)),
            pltpu.VMEM((channels, channels), jnp.float32),
            pltpu.VMEM((count, channels, channels), jnp.float32),
            pltpu.SemaphoreType.DMA,
            pltpu.SemaphoreType.DMA((count,)),
            pltpu.SemaphoreType.DMA((count,)),
        ],
        compiler_params=pltpu.CompilerParams(
            dimension_semantics=("arbitrary",), vmem_limit_bytes=60 * 1024 * 1024,
            collective_id=0, has_side_effects=True,
        ),
    )(hidden_pre, cotangent, table_z)


def synthesis_kernel(axis, count, other, others, h_ref, g_ref, xs_ref, tyt_ref, tz_ref, sw_ref,
                     gs_ref, out_ref, skip_out_ref, ks_ref, stage_ref, send_ref, recv_ref,
                     local_sems, send_sems, recv_sems, wbuf_ref, wlocal_sem, wsend_sems,
                     wrecv_sems):
    mesh_ids = pl.DeviceIdType.MESH
    step = pl.program_id(0)
    steps = pl.num_programs(0)
    channels, xb, ny, nz = h_ref.shape
    rows = channels * ny
    chunk = 2 * xb
    me = lax.axis_index(axis)
    me_w = lax.axis_index(other)

    def wide_copies():
        local = pltpu.make_async_copy(gs_ref, wbuf_ref.at[me_w], wlocal_sem)
        remote = []
        for k in range(1, others):
            peer = lax.rem(me_w + k, others)
            remote.append(pltpu.make_async_remote_copy(
                src_ref=gs_ref,
                dst_ref=wbuf_ref.at[me_w],
                send_sem=wsend_sems.at[k],
                recv_sem=wrecv_sems.at[k],
                device_id={other: peer},
                device_id_type=mesh_ids,
            ))
        return local, remote

    def copies(at):
        part = pl.ds(pl.multiple_of(at * chunk, chunk), chunk)
        local = pltpu.make_async_copy(
            send_ref.at[me, part], recv_ref.at[me, part], local_sems.at[at])
        remote = []
        for k in range(1, count):
            peer = lax.rem(me + k, count)
            remote.append(pltpu.make_async_remote_copy(
                src_ref=send_ref.at[peer, part],
                dst_ref=recv_ref.at[me, part],
                send_sem=send_sems.at[at, k],
                recv_sem=recv_sems.at[at, k],
                device_id={axis: peer},
                device_id_type=mesh_ids,
            ))
        return local, remote

    @pl.when(step == 0)
    def _():
        barrier = pltpu.get_barrier_semaphore()
        for k in range(1, count):
            peer = lax.rem(me + k, count)
            pl.semaphore_signal(barrier, inc=1, device_id={axis: peer}, device_id_type=mesh_ids)
        for k in range(1, others):
            peer = lax.rem(me_w + k, others)
            pl.semaphore_signal(barrier, inc=1, device_id={other: peer}, device_id_type=mesh_ids)
        pl.semaphore_wait(barrier, count - 1 + others - 1)
        wlocal, wremote = wide_copies()
        wlocal.start()
        for copy in wremote:
            copy.start()
        y_synthesis_body(xs_ref, tyt_ref, send_ref, stage_ref)
        for at in range(recv_ref.shape[1] // chunk):
            local, remote = copies(at)
            local.start()
            for copy in remote:
                copy.start()
        r = lax.broadcasted_iota(jnp.int32, (rows, channels), 0)
        k = lax.broadcasted_iota(jnp.int32, (rows, channels), 1)
        expand = (r // ny == k).astype(jnp.float32)
        spread = jnp.dot(expand, sw_ref[...].astype(jnp.float32), preferred_element_type=jnp.float32)
        kr = lax.broadcasted_iota(jnp.int32, (channels, rows), 0)
        kc = lax.broadcasted_iota(jnp.int32, (channels, rows), 1)
        expand_t = (kc // ny == kr).astype(jnp.float32)
        full = jnp.dot(spread, expand_t, preferred_element_type=jnp.float32)
        ri = lax.broadcasted_iota(jnp.int32, (rows, rows), 0)
        ci = lax.broadcasted_iota(jnp.int32, (rows, rows), 1)
        ks_ref[...] = jnp.where(ri % ny == ci % ny, full, 0.0).astype(ks_ref.dtype)

    local, _ = copies(step)
    local.wait()
    part = pl.ds(pl.multiple_of(step * chunk, chunk), chunk)
    for k in range(1, count):
        origin = lax.rem(me + count - k, count)
        pltpu.make_async_remote_copy(
            src_ref=send_ref.at[me, part],
            dst_ref=recv_ref.at[origin, part],
            send_sem=send_sems.at[step, k],
            recv_sem=recv_sems.at[step, k],
            device_id={axis: origin},
            device_id_type=mesh_ids,
        ).wait_recv()

    tz = tz_ref[...]
    ks = ks_ref[...]
    ys = recv_ref[:, part, :].astype(jnp.float32)
    for x in range(xb):
        lo = ys[:, 2 * x, :]
        hi = ys[:, 2 * x + 1, :]
        lhs = jnp.concatenate([lo, hi], axis=0).T.astype(jnp.bfloat16)
        spec = jnp.dot(lhs, tz, preferred_element_type=jnp.float32)
        spec = spec.astype(jnp.bfloat16).astype(jnp.float32)
        skip = jnp.dot(ks, g_ref[:, x].reshape(channels * ny, nz), preferred_element_type=jnp.float32)
        activ = jnp.tanh(h_ref[:, x].astype(jnp.float32)).reshape(channels * ny, nz)
        grad = (spec + skip) * (1.0 - activ * activ)
        out_ref[:, x] = grad.astype(jnp.bfloat16).reshape(channels, ny, nz)

    @pl.when(step == steps - 1)
    def _():
        for at in range(recv_ref.shape[1] // chunk):
            _, remote = copies(at)
            for copy in remote:
                copy.wait_send()
        wlocal, wremote = wide_copies()
        wlocal.wait()
        for k in range(1, others):
            wremote[k - 1].wait_send()
            origin = lax.rem(me_w + others - k, others)
            pltpu.make_async_remote_copy(
                src_ref=gs_ref,
                dst_ref=wbuf_ref.at[origin],
                send_sem=wsend_sems.at[k],
                recv_sem=wrecv_sems.at[k],
                device_id={other: origin},
                device_id_type=mesh_ids,
            ).wait_recv()
        total = wbuf_ref[0]
        for src in range(1, others):
            total = total + wbuf_ref[src]
        skip_out_ref[...] = total * (1.0 / math.sqrt(NX * NY * NZ))


def synthesis(hidden_pre, cotangent, xsynth, table_yt, table_z, skip_weight, skip_terms, axis,
              count, other, others):
    channels, nx, ny, nz = hidden_pre.shape
    modes = table_z.shape[0]
    mz_local = xsynth.shape[0]
    steps = nx // XB
    field_spec = pl.BlockSpec((channels, XB, ny, nz), lambda i: (0, i, 0, 0))
    whole = pl.BlockSpec(memory_space=pltpu.VMEM)
    lanes = channels * ny
    return pl.pallas_call(
        functools.partial(synthesis_kernel, axis, count, other, others),
        grid=(steps,),
        in_specs=[
            field_spec,
            field_spec,
            whole,
            whole,
            pl.BlockSpec((modes, nz), lambda i: (0, 0)),
            pl.BlockSpec((channels, channels), lambda i: (0, 0)),
            whole,
        ],
        out_specs=[field_spec, pl.BlockSpec((channels, channels), lambda i: (0, 0))],
        out_shape=[
            jax.ShapeDtypeStruct(hidden_pre.shape, jnp.bfloat16),
            jax.ShapeDtypeStruct((channels, channels), jnp.float32),
        ],
        scratch_shapes=[
            pltpu.VMEM((lanes, lanes), jnp.bfloat16),
            pltpu.VMEM((count * lanes // 128, nx * mz_local, 128), jnp.float32),
            pltpu.VMEM((count, nx * mz_local, lanes), jnp.bfloat16),
            pltpu.VMEM((count, nx * mz_local, lanes), jnp.bfloat16),
            pltpu.SemaphoreType.DMA((steps,)),
            pltpu.SemaphoreType.DMA((steps, count)),
            pltpu.SemaphoreType.DMA((steps, count)),
            pltpu.VMEM((others, channels, channels), jnp.float32),
            pltpu.SemaphoreType.DMA,
            pltpu.SemaphoreType.DMA((others,)),
            pltpu.SemaphoreType.DMA((others,)),
        ],
        compiler_params=pltpu.CompilerParams(
            dimension_semantics=("arbitrary",), vmem_limit_bytes=60 * 1024 * 1024,
            collective_id=1, has_side_effects=True,
        ),
    )(hidden_pre, cotangent, xsynth, table_yt, table_z, skip_weight, skip_terms)


def y_synthesis_body(xs_ref, tyt_ref, out_ref, stage_ref):
    mz_local, channels, modes, nx = xs_ref.shape
    blocks, _, lanes = out_ref.shape
    ny = lanes // channels
    tyt = jnp.broadcast_to(tyt_ref[...][None], (channels,) + tyt_ref.shape)
    for z in range(mz_local):
        part = jnp.einsum(
            "cym,cmx->cyx", tyt, xs_ref[z], preferred_element_type=jnp.float32
        ).astype(jnp.bfloat16).astype(jnp.float32)
        for d in range(blocks):
            piece = part[:, d * ny:(d + 1) * ny, :].reshape(channels * ny, nx).T
            for q in range(lanes // 128):
                stage_ref[d * (lanes // 128) + q, pl.ds(z, nx, stride=mz_local), :] = (
                    piece[:, q * 128:(q + 1) * 128])
    for d in range(blocks):
        for q in range(lanes // 128):
            out_ref[d, :, q * 128:(q + 1) * 128] = (
                stage_ref[d * (lanes // 128) + q].astype(out_ref.dtype))


def modes_kernel(sp_ref, w_ref, gm_ref, bs_ref):
    highest = lax.Precision.HIGHEST
    channels = sp_ref.shape[1] // 2
    width = channels * channels
    sp = sp_ref[...]
    er = lax.broadcasted_iota(jnp.int32, (channels, width), 0)
    ec = lax.broadcasted_iota(jnp.int32, (channels, width), 1)
    spread = (ec // channels == er).astype(jnp.float32)
    tile = (ec % channels == er).astype(jnp.float32)
    s_rep = jnp.dot(sp[:, :channels], spread, precision=highest, preferred_element_type=jnp.float32)
    q_rep = jnp.dot(sp[:, channels:], tile, precision=highest, preferred_element_type=jnp.float32)
    gm_ref[...] = s_rep * q_rep
    weighted = w_ref[...].astype(jnp.float32) * q_rep
    back = lax.dot_general(
        weighted, spread, (((1,), (1,)), ((), ())), precision=highest,
        preferred_element_type=jnp.float32)
    bs_ref[...] = back.astype(bs_ref.dtype)


def modes_step(spectra, weights):
    rows, both = spectra.shape
    channels = both // 2
    vmem = pl.BlockSpec(memory_space=pltpu.VMEM)
    return pl.pallas_call(
        modes_kernel,
        in_specs=[vmem, vmem],
        out_specs=[vmem, vmem],
        out_shape=[
            jax.ShapeDtypeStruct((rows, channels * channels), jnp.float32),
            jax.ShapeDtypeStruct((rows, channels), jnp.bfloat16),
        ],
    )(spectra, weights)


def per_device(hidden_pre, cotangent, mode_weight, skip_weight):
    highest = lax.Precision.HIGHEST
    channels, nx, ny, nz = hidden_pre.shape
    mode_count = mode_weight.shape[2]
    n_narrow = lax.axis_size("narrow")
    n_wide = lax.axis_size("wide")
    table_x = basis_table(mode_count, NX)
    table_y = basis_table(mode_count, NY)
    table_z = basis_table(mode_count, NZ)

    zc, gram = analysis(hidden_pre, cotangent, table_z, "narrow", n_narrow)
    mz_local = mode_count // n_narrow
    zc = zc.reshape(n_narrow, mz_local, 2 * channels, nx, ny)
    ycoeffs = jnp.einsum(
        "smcxl,nsl->mcnx", zc, table_y.reshape(mode_count, n_narrow, ny),
        preferred_element_type=jnp.float32,
    ).astype(jnp.bfloat16)
    ycoeffs = lax.all_to_all(ycoeffs, "wide", split_axis=2, concat_axis=3, tiled=True)
    spectra = jnp.einsum("zcyx,kx->zykc", ycoeffs, table_x, preferred_element_type=jnp.float32)
    z_local, y_local = (spectra.shape[0], spectra.shape[1])
    grad_modes, back_spec = modes_step(
        spectra.reshape(z_local * y_local * mode_count, 2 * channels),
        mode_weight.reshape(z_local * y_local * mode_count, channels * channels),
    )
    grad_modes = grad_modes.reshape(z_local, y_local, mode_count, channels * channels)
    back_spec = jnp.transpose(
        back_spec.reshape(z_local, y_local, mode_count, channels), (0, 3, 1, 2)
    )
    xsynth = jnp.einsum(
        "zcyk,kx->zcyx", back_spec, table_x, preferred_element_type=jnp.float32
    ).astype(jnp.bfloat16)
    xsynth = lax.all_to_all(xsynth, "wide", split_axis=3, concat_axis=2, tiled=True)
    table_zp = jnp.transpose(table_z.reshape(n_narrow, mz_local, nz), (1, 0, 2)).reshape(mode_count, nz)
    grad_hidden, grad_skip = synthesis(
        hidden_pre, cotangent, xsynth, jnp.transpose(table_y), table_zp, skip_weight, gram,
        "narrow", n_narrow, "wide", n_wide)

    return (grad_hidden, grad_modes, grad_skip)


def solution(mesh):
    in_specs = (
        P(None, "wide", "narrow", None),
        P(None, "wide", "narrow", None),
        P("narrow", "wide", None, None),
        P(),
    )
    out_specs = (P(None, "wide", "narrow", None), P("narrow", "wide", None, None), P())
    return jax.shard_map(
        per_device, mesh=mesh, in_specs=in_specs, out_specs=out_specs, check_vma=False
    )
```

```python
import functools
import math

import jax
import jax.numpy as jnp
from jax import lax
from jax.experimental import pallas as pl
from jax.experimental.pallas import tpu as pltpu
from jax.sharding import PartitionSpec as P

NX = 256
NY = 256
NZ = 256
XB = 8


def basis_table(mode_count, length):
    mode_index = jnp.arange(mode_count, dtype=jnp.int32)
    halfway = mode_count // 2
    frequency = jnp.where(mode_index < halfway, mode_index, mode_index - halfway + 1)
    points = jnp.arange(length, dtype=jnp.int32)
    phases = frequency[:, None] * points[None, :] % length
    angles = phases.astype(jnp.float32) * (2.0 * math.pi / length)
    values_table = jnp.where((mode_index < halfway)[:, None], jnp.cos(angles), jnp.sin(angles))
    return (values_table * (1.0 / math.sqrt(length))).astype(jnp.bfloat16)


def _nt(a, b):
    return lax.dot_general(a, b, (((1,), (1,)), ((), ())), preferred_element_type=jnp.float32)


def analysis_kernel(axis, count, h_ref, g_ref, tz_ref, zc_ref, gram_ref, acc_ref, stage_ref,
                    slot_ref, local_sems, send_sems, recv_sems):
    mesh_ids = pl.DeviceIdType.MESH
    step = pl.program_id(0)
    steps = pl.num_programs(0)
    channels, xb, ny, nz = h_ref.shape
    width = xb * ny
    mz_local = slot_ref.shape[1] // count
    me = lax.axis_index(axis)

    def copies(at):
        slot = lax.rem(at, 2)
        cols = pl.ds(pl.multiple_of(at * width, width), width)
        local = pltpu.make_async_copy(
            slot_ref.at[slot, pl.ds(me * mz_local, mz_local)],
            zc_ref.at[me, :, :, cols],
            local_sems.at[at],
        )
        remote = []
        for k in range(1, count):
            peer = lax.rem(me + k, count)
            remote.append(pltpu.make_async_remote_copy(
                src_ref=slot_ref.at[slot, pl.ds(peer * mz_local, mz_local)],
                dst_ref=zc_ref.at[me, :, :, cols],
                send_sem=send_sems.at[at, k],
                recv_sem=recv_sems.at[at, k],
                device_id={axis: peer},
                device_id_type=mesh_ids,
            ))
        return local, remote

    def wait_sent(at):
        local, remote = copies(at)
        local.wait()
        for copy in remote:
            copy.wait_send()

    @pl.when(step == 0)
    def _():
        acc_ref[...] = jnp.zeros_like(acc_ref)
        barrier = pltpu.get_barrier_semaphore()
        for k in range(1, count):
            peer = lax.rem(me + k, count)
            pl.semaphore_signal(barrier, inc=1, device_id={axis: peer}, device_id_type=mesh_ids)
        pl.semaphore_wait(barrier, count - 1)

    @pl.when(step >= 2)
    def _():
        wait_sent(step - 2)

    tz = tz_ref[...]
    li = jnp.tanh(h_ref[...].astype(jnp.float32)).astype(jnp.bfloat16)
    g = g_ref[...]
    zl = _nt(tz, li.reshape(channels * width, nz))
    zg = _nt(tz, g.reshape(channels * width, nz))
    for c in range(channels):
        stage_ref[:, c, :] = zl[:, c * width:(c + 1) * width]
        stage_ref[:, channels + c, :] = zg[:, c * width:(c + 1) * width]
    slot_ref[lax.rem(step, 2)] = stage_ref[...].astype(jnp.bfloat16)
    local, remote = copies(step)
    local.start()
    for copy in remote:
        copy.start()
    for x in range(xb):
        acc_ref[...] += _nt(li[:, x].reshape(channels * ny, nz), g[:, x].reshape(channels * ny, nz))

    @pl.when(step == steps - 1)
    def _():
        rows = channels * ny
        ri = lax.broadcasted_iota(jnp.int32, (rows, rows), 0)
        ci = lax.broadcasted_iota(jnp.int32, (rows, rows), 1)
        diag = jnp.where(ri % ny == ci % ny, acc_ref[...], 0.0)
        er = lax.broadcasted_iota(jnp.int32, (channels, rows), 0)
        ec = lax.broadcasted_iota(jnp.int32, (channels, rows), 1)
        gather = (ec // ny == er).astype(jnp.float32)
        part = jnp.dot(gather, diag, precision=lax.Precision.HIGHEST, preferred_element_type=jnp.float32)
        gram_ref[...] = lax.dot_general(
            part, gather, (((1,), (1,)), ((), ())), precision=lax.Precision.HIGHEST,
            preferred_element_type=jnp.float32)
        wait_sent(step - 1)
        wait_sent(step)
        for at in range(zc_ref.shape[3] // width):
            cols = pl.ds(at * width, width)
            for k in range(1, count):
                origin = lax.rem(me + count - k, count)
                pltpu.make_async_remote_copy(
                    src_ref=slot_ref.at[0, pl.ds(me * mz_local, mz_local)],
                    dst_ref=zc_ref.at[origin, :, :, cols],
                    send_sem=send_sems.at[at, k],
                    recv_sem=recv_sems.at[at, k],
                    device_id={axis: origin},
                    device_id_type=mesh_ids,
                ).wait_recv()


def analysis(hidden_pre, cotangent, table_z, axis, count):
    channels, nx, ny, nz = hidden_pre.shape
    modes = table_z.shape[0]
    steps = nx // XB
    field_spec = pl.BlockSpec((channels, XB, ny, nz), lambda i: (0, i, 0, 0))
    return pl.pallas_call(
        functools.partial(analysis_kernel, axis, count),
        grid=(steps,),
        in_specs=[field_spec, field_spec, pl.BlockSpec((modes, nz), lambda i: (0, 0))],
        out_specs=[
            pl.BlockSpec(memory_space=pl.ANY),
            pl.BlockSpec((channels, channels), lambda i: (0, 0)),
        ],
        out_shape=[
            jax.ShapeDtypeStruct(
                (count, modes // count, 2 * channels, nx * ny), jnp.bfloat16),
            jax.ShapeDtypeStruct((channels, channels), jnp.float32),
        ],
        scratch_shapes=[
            pltpu.VMEM((channels * ny, channels * ny), jnp.float32),
            pltpu.VMEM((modes, 2 * channels, XB * ny), jnp.float32),
            pltpu.VMEM((2, modes, 2 * channels, XB * ny), jnp.bfloat16),
            pltpu.SemaphoreType.DMA((steps,)),
            pltpu.SemaphoreType.DMA((steps, count)),
            pltpu.SemaphoreType.DMA((steps, count)),
        ],
        compiler_params=pltpu.CompilerParams(
            dimension_semantics=("arbitrary",), vmem_limit_bytes=60 * 1024 * 1024,
            collective_id=0, has_side_effects=True,
        ),
    )(hidden_pre, cotangent, table_z)


def synthesis_kernel(axis, count, other, others, h_ref, g_ref, xs_ref, tyt_ref, tz_ref, sw_ref,
                     gs_ref, out_ref, skip_out_ref, ks_ref, stage_ref, send_ref, recv_ref,
                     local_sems, send_sems, recv_sems, wbuf_ref, wlocal_sem, wsend_sems,
                     wrecv_sems, nbuf_ref, nlocal_sem, nsend_sems, nrecv_sems, wstage_ref):
    mesh_ids = pl.DeviceIdType.MESH
    step = pl.program_id(0)
    steps = pl.num_programs(0)
    channels, xb, ny, nz = h_ref.shape
    rows = channels * ny
    chunk = 2 * xb
    me = lax.axis_index(axis)
    me_w = lax.axis_index(other)

    def narrow_copies():
        local = pltpu.make_async_copy(gs_ref, nbuf_ref.at[me], nlocal_sem)
        remote = []
        for k in range(1, count):
            peer = lax.rem(me + k, count)
            remote.append(pltpu.make_async_remote_copy(
                src_ref=gs_ref,
                dst_ref=nbuf_ref.at[me],
                send_sem=nsend_sems.at[k],
                recv_sem=nrecv_sems.at[k],
                device_id={axis: peer},
                device_id_type=mesh_ids,
            ))
        return local, remote

    def wide_copies():
        local = pltpu.make_async_copy(wstage_ref, wbuf_ref.at[me_w], wlocal_sem)
        remote = []
        for k in range(1, others):
            peer = lax.rem(me_w + k, others)
            remote.append(pltpu.make_async_remote_copy(
                src_ref=wstage_ref,
                dst_ref=wbuf_ref.at[me_w],
                send_sem=wsend_sems.at[k],
                recv_sem=wrecv_sems.at[k],
                device_id={other: peer},
                device_id_type=mesh_ids,
            ))
        return local, remote

    def copies(at):
        part = pl.ds(pl.multiple_of(at * chunk, chunk), chunk)
        local = pltpu.make_async_copy(
            send_ref.at[me, part], recv_ref.at[me, part], local_sems.at[at])
        remote = []
        for k in range(1, count):
            peer = lax.rem(me + k, count)
            remote.append(pltpu.make_async_remote_copy(
                src_ref=send_ref.at[peer, part],
                dst_ref=recv_ref.at[me, part],
                send_sem=send_sems.at[at, k],
                recv_sem=recv_sems.at[at, k],
                device_id={axis: peer},
                device_id_type=mesh_ids,
            ))
        return local, remote

    @pl.when(step == 0)
    def _():
        barrier = pltpu.get_barrier_semaphore()
        for k in range(1, count):
            peer = lax.rem(me + k, count)
            pl.semaphore_signal(barrier, inc=1, device_id={axis: peer}, device_id_type=mesh_ids)
        for k in range(1, others):
            peer = lax.rem(me_w + k, others)
            pl.semaphore_signal(barrier, inc=1, device_id={other: peer}, device_id_type=mesh_ids)
        pl.semaphore_wait(barrier, count - 1 + others - 1)
        nlocal, nremote = narrow_copies()
        nlocal.start()
        for copy in nremote:
            copy.start()
        y_synthesis_body(xs_ref, tyt_ref, send_ref, stage_ref)
        for at in range(recv_ref.shape[1] // chunk):
            local, remote = copies(at)
            local.start()
            for copy in remote:
                copy.start()
        r = lax.broadcasted_iota(jnp.int32, (rows, channels), 0)
        k = lax.broadcasted_iota(jnp.int32, (rows, channels), 1)
        expand = (r // ny == k).astype(jnp.float32)
        spread = jnp.dot(expand, sw_ref[...].astype(jnp.float32), preferred_element_type=jnp.float32)
        kr = lax.broadcasted_iota(jnp.int32, (channels, rows), 0)
        kc = lax.broadcasted_iota(jnp.int32, (channels, rows), 1)
        expand_t = (kc // ny == kr).astype(jnp.float32)
        full = jnp.dot(spread, expand_t, preferred_element_type=jnp.float32)
        ri = lax.broadcasted_iota(jnp.int32, (rows, rows), 0)
        ci = lax.broadcasted_iota(jnp.int32, (rows, rows), 1)
        ks_ref[...] = jnp.where(ri % ny == ci % ny, full, 0.0).astype(ks_ref.dtype)

    @pl.when(step == 1)
    def _():
        nlocal, nremote = narrow_copies()
        nlocal.wait()
        for k in range(1, count):
            nremote[k - 1].wait_send()
            origin = lax.rem(me + count - k, count)
            pltpu.make_async_remote_copy(
                src_ref=gs_ref,
                dst_ref=nbuf_ref.at[origin],
                send_sem=nsend_sems.at[k],
                recv_sem=nrecv_sems.at[k],
                device_id={axis: origin},
                device_id_type=mesh_ids,
            ).wait_recv()
        total = nbuf_ref[0]
        for src in range(1, count):
            total = total + nbuf_ref[src]
        wstage_ref[...] = total
        wlocal, wremote = wide_copies()
        wlocal.start()
        for copy in wremote:
            copy.start()

    local, _ = copies(step)
    local.wait()
    part = pl.ds(pl.multiple_of(step * chunk, chunk), chunk)
    for k in range(1, count):
        origin = lax.rem(me + count - k, count)
        pltpu.make_async_remote_copy(
            src_ref=send_ref.at[me, part],
            dst_ref=recv_ref.at[origin, part],
            send_sem=send_sems.at[step, k],
            recv_sem=recv_sems.at[step, k],
            device_id={axis: origin},
            device_id_type=mesh_ids,
        ).wait_recv()

    tz = tz_ref[...]
    ks = ks_ref[...]
    ys = recv_ref[:, part, :].astype(jnp.float32)
    for x in range(xb):
        lo = ys[:, 2 * x, :]
        hi = ys[:, 2 * x + 1, :]
        lhs = jnp.concatenate([lo, hi], axis=0).T.astype(jnp.bfloat16)
        spec = jnp.dot(lhs, tz, preferred_element_type=jnp.float32)
        spec = spec.astype(jnp.bfloat16).astype(jnp.float32)
        skip = jnp.dot(ks, g_ref[:, x].reshape(channels * ny, nz), preferred_element_type=jnp.float32)
        activ = jnp.tanh(h_ref[:, x].astype(jnp.float32)).reshape(channels * ny, nz)
        grad = (spec + skip) * (1.0 - activ * activ)
        out_ref[:, x] = grad.astype(jnp.bfloat16).reshape(channels, ny, nz)

    @pl.when(step == steps - 1)
    def _():
        for at in range(recv_ref.shape[1] // chunk):
            _, remote = copies(at)
            for copy in remote:
                copy.wait_send()
        wlocal, wremote = wide_copies()
        wlocal.wait()
        for k in range(1, others):
            wremote[k - 1].wait_send()
            origin = lax.rem(me_w + others - k, others)
            pltpu.make_async_remote_copy(
                src_ref=wstage_ref,
                dst_ref=wbuf_ref.at[origin],
                send_sem=wsend_sems.at[k],
                recv_sem=wrecv_sems.at[k],
                device_id={other: origin},
                device_id_type=mesh_ids,
            ).wait_recv()
        total = wbuf_ref[0]
        for src in range(1, others):
            total = total + wbuf_ref[src]
        skip_out_ref[...] = total * (1.0 / math.sqrt(NX * NY * NZ))


def synthesis(hidden_pre, cotangent, xsynth, table_yt, table_z, skip_weight, skip_terms, axis,
              count, other, others):
    channels, nx, ny, nz = hidden_pre.shape
    modes = table_z.shape[0]
    mz_local = xsynth.shape[0]
    steps = nx // XB
    field_spec = pl.BlockSpec((channels, XB, ny, nz), lambda i: (0, i, 0, 0))
    whole = pl.BlockSpec(memory_space=pltpu.VMEM)
    lanes = channels * ny
    return pl.pallas_call(
        functools.partial(synthesis_kernel, axis, count, other, others),
        grid=(steps,),
        in_specs=[
            field_spec,
            field_spec,
            whole,
            whole,
            pl.BlockSpec((modes, nz), lambda i: (0, 0)),
            pl.BlockSpec((channels, channels), lambda i: (0, 0)),
            whole,
        ],
        out_specs=[field_spec, pl.BlockSpec((channels, channels), lambda i: (0, 0))],
        out_shape=[
            jax.ShapeDtypeStruct(hidden_pre.shape, jnp.bfloat16),
            jax.ShapeDtypeStruct((channels, channels), jnp.float32),
        ],
        scratch_shapes=[
            pltpu.VMEM((lanes, lanes), jnp.bfloat16),
            pltpu.VMEM((count * lanes // 128, nx * mz_local, 128), jnp.float32),
            pltpu.VMEM((count, nx * mz_local, lanes), jnp.bfloat16),
            pltpu.VMEM((count, nx * mz_local, lanes), jnp.bfloat16),
            pltpu.SemaphoreType.DMA((steps,)),
            pltpu.SemaphoreType.DMA((steps, count)),
            pltpu.SemaphoreType.DMA((steps, count)),
            pltpu.VMEM((others, channels, channels), jnp.float32),
            pltpu.SemaphoreType.DMA,
            pltpu.SemaphoreType.DMA((others,)),
            pltpu.SemaphoreType.DMA((others,)),
            pltpu.VMEM((count, channels, channels), jnp.float32),
            pltpu.SemaphoreType.DMA,
            pltpu.SemaphoreType.DMA((count,)),
            pltpu.SemaphoreType.DMA((count,)),
            pltpu.VMEM((channels, channels), jnp.float32),
        ],
        compiler_params=pltpu.CompilerParams(
            dimension_semantics=("arbitrary",), vmem_limit_bytes=60 * 1024 * 1024,
            collective_id=1, has_side_effects=True,
        ),
    )(hidden_pre, cotangent, xsynth, table_yt, table_z, skip_weight, skip_terms)


def y_synthesis_body(xs_ref, tyt_ref, out_ref, stage_ref):
    mz_local, channels, modes, nx = xs_ref.shape
    blocks, _, lanes = out_ref.shape
    ny = lanes // channels
    tyt = jnp.broadcast_to(tyt_ref[...][None], (channels,) + tyt_ref.shape)
    for z in range(mz_local):
        part = jnp.einsum(
            "cym,cmx->cyx", tyt, xs_ref[z], preferred_element_type=jnp.float32
        ).astype(jnp.bfloat16).astype(jnp.float32)
        for d in range(blocks):
            piece = part[:, d * ny:(d + 1) * ny, :].reshape(channels * ny, nx).T
            for q in range(lanes // 128):
                stage_ref[d * (lanes // 128) + q, pl.ds(z, nx, stride=mz_local), :] = (
                    piece[:, q * 128:(q + 1) * 128])
    for d in range(blocks):
        for q in range(lanes // 128):
            out_ref[d, :, q * 128:(q + 1) * 128] = (
                stage_ref[d * (lanes // 128) + q].astype(out_ref.dtype))


def modes_kernel(sp_ref, w_ref, gm_ref, bs_ref):
    highest = lax.Precision.HIGHEST
    channels = sp_ref.shape[1] // 2
    width = channels * channels
    sp = sp_ref[...]
    er = lax.broadcasted_iota(jnp.int32, (channels, width), 0)
    ec = lax.broadcasted_iota(jnp.int32, (channels, width), 1)
    spread = (ec // channels == er).astype(jnp.float32)
    tile = (ec % channels == er).astype(jnp.float32)
    s_rep = jnp.dot(sp[:, :channels], spread, precision=highest, preferred_element_type=jnp.float32)
    q_rep = jnp.dot(sp[:, channels:], tile, precision=highest, preferred_element_type=jnp.float32)
    gm_ref[...] = s_rep * q_rep
    weighted = w_ref[...].astype(jnp.float32) * q_rep
    back = lax.dot_general(
        weighted, spread, (((1,), (1,)), ((), ())), precision=highest,
        preferred_element_type=jnp.float32)
    bs_ref[...] = back.astype(bs_ref.dtype)


def modes_step(spectra, weights):
    rows, both = spectra.shape
    channels = both // 2
    vmem = pl.BlockSpec(memory_space=pltpu.VMEM)
    return pl.pallas_call(
        modes_kernel,
        in_specs=[vmem, vmem],
        out_specs=[vmem, vmem],
        out_shape=[
            jax.ShapeDtypeStruct((rows, channels * channels), jnp.float32),
            jax.ShapeDtypeStruct((rows, channels), jnp.bfloat16),
        ],
    )(spectra, weights)


def per_device(hidden_pre, cotangent, mode_weight, skip_weight):
    highest = lax.Precision.HIGHEST
    channels, nx, ny, nz = hidden_pre.shape
    mode_count = mode_weight.shape[2]
    n_narrow = lax.axis_size("narrow")
    n_wide = lax.axis_size("wide")
    table_x = basis_table(mode_count, NX)
    table_y = basis_table(mode_count, NY)
    table_z = basis_table(mode_count, NZ)

    zc, gram = analysis(hidden_pre, cotangent, table_z, "narrow", n_narrow)
    mz_local = mode_count // n_narrow
    zc = zc.reshape(n_narrow, mz_local, 2 * channels, nx, ny)
    ycoeffs = jnp.einsum(
        "smcxl,nsl->mcnx", zc, table_y.reshape(mode_count, n_narrow, ny),
        preferred_element_type=jnp.float32,
    ).astype(jnp.bfloat16)
    ycoeffs = lax.all_to_all(ycoeffs, "wide", split_axis=2, concat_axis=3, tiled=True)
    spectra = jnp.einsum("zcyx,kx->zykc", ycoeffs, table_x, preferred_element_type=jnp.float32)
    z_local, y_local = (spectra.shape[0], spectra.shape[1])
    grad_modes, back_spec = modes_step(
        spectra.reshape(z_local * y_local * mode_count, 2 * channels),
        mode_weight.reshape(z_local * y_local * mode_count, channels * channels),
    )
    grad_modes = grad_modes.reshape(z_local, y_local, mode_count, channels * channels)
    back_spec = jnp.transpose(
        back_spec.reshape(z_local, y_local, mode_count, channels), (0, 3, 1, 2)
    )
    xsynth = jnp.einsum(
        "zcyk,kx->zcyx", back_spec, table_x, preferred_element_type=jnp.float32
    ).astype(jnp.bfloat16)
    xsynth = lax.all_to_all(xsynth, "wide", split_axis=3, concat_axis=2, tiled=True)
    table_zp = jnp.transpose(table_z.reshape(n_narrow, mz_local, nz), (1, 0, 2)).reshape(mode_count, nz)
    grad_hidden, grad_skip = synthesis(
        hidden_pre, cotangent, xsynth, jnp.transpose(table_y), table_zp, skip_weight, gram,
        "narrow", n_narrow, "wide", n_wide)

    return (grad_hidden, grad_modes, grad_skip)


def solution(mesh):
    in_specs = (
        P(None, "wide", "narrow", None),
        P(None, "wide", "narrow", None),
        P("narrow", "wide", None, None),
        P(),
    )
    out_specs = (P(None, "wide", "narrow", None), P("narrow", "wide", None, None), P())
    return jax.shard_map(
        per_device, mesh=mesh, in_specs=in_specs, out_specs=out_specs, check_vma=False
    )
```

```python
import functools
import math

import jax
import jax.numpy as jnp
from jax import lax
from jax.experimental import pallas as pl
from jax.experimental.pallas import tpu as pltpu
from jax.sharding import PartitionSpec as P

NX = 256
NY = 256
NZ = 256
XB = 8


def basis_table(mode_count, length):
    mode_index = jnp.arange(mode_count, dtype=jnp.int32)
    halfway = mode_count // 2
    frequency = jnp.where(mode_index < halfway, mode_index, mode_index - halfway + 1)
    points = jnp.arange(length, dtype=jnp.int32)
    phases = frequency[:, None] * points[None, :] % length
    angles = phases.astype(jnp.float32) * (2.0 * math.pi / length)
    values_table = jnp.where((mode_index < halfway)[:, None], jnp.cos(angles), jnp.sin(angles))
    return (values_table * (1.0 / math.sqrt(length))).astype(jnp.bfloat16)


def _nt(a, b):
    return lax.dot_general(a, b, (((1,), (1,)), ((), ())), preferred_element_type=jnp.float32)


def analysis_kernel(axis, count, h_ref, g_ref, tz_ref, zc_ref, gram_ref, acc_ref, stage_ref,
                    slot_ref, local_sems, send_sems, recv_sems):
    mesh_ids = pl.DeviceIdType.MESH
    step = pl.program_id(0)
    steps = pl.num_programs(0)
    channels, xb, ny, nz = h_ref.shape
    width = xb * ny
    mz_local = slot_ref.shape[1] // count
    me = lax.axis_index(axis)

    def copies(at):
        slot = lax.rem(at, 2)
        cols = pl.ds(pl.multiple_of(at * width, width), width)
        local = pltpu.make_async_copy(
            slot_ref.at[slot, pl.ds(me * mz_local, mz_local)],
            zc_ref.at[me, :, :, cols],
            local_sems.at[at],
        )
        remote = []
        for k in range(1, count):
            peer = lax.rem(me + k, count)
            remote.append(pltpu.make_async_remote_copy(
                src_ref=slot_ref.at[slot, pl.ds(peer * mz_local, mz_local)],
                dst_ref=zc_ref.at[me, :, :, cols],
                send_sem=send_sems.at[at, k],
                recv_sem=recv_sems.at[at, k],
                device_id={axis: peer},
                device_id_type=mesh_ids,
            ))
        return local, remote

    def wait_sent(at):
        local, remote = copies(at)
        local.wait()
        for copy in remote:
            copy.wait_send()

    @pl.when(step == 0)
    def _():
        acc_ref[...] = jnp.zeros_like(acc_ref)
        barrier = pltpu.get_barrier_semaphore()
        for k in range(1, count):
            peer = lax.rem(me + k, count)
            pl.semaphore_signal(barrier, inc=1, device_id={axis: peer}, device_id_type=mesh_ids)
        pl.semaphore_wait(barrier, count - 1)

    @pl.when(step >= 2)
    def _():
        wait_sent(step - 2)

    tz = tz_ref[...]
    li = jnp.tanh(h_ref[...].astype(jnp.float32)).astype(jnp.bfloat16)
    g = g_ref[...]
    zl = _nt(tz, li.reshape(channels * width, nz))
    zg = _nt(tz, g.reshape(channels * width, nz))
    for c in range(channels):
        stage_ref[:, c, :] = zl[:, c * width:(c + 1) * width]
        stage_ref[:, channels + c, :] = zg[:, c * width:(c + 1) * width]
    slot_ref[lax.rem(step, 2)] = stage_ref[...].astype(jnp.bfloat16)
    local, remote = copies(step)
    local.start()
    for copy in remote:
        copy.start()
    for x in range(xb):
        acc_ref[...] += _nt(li[:, x].reshape(channels * ny, nz), g[:, x].reshape(channels * ny, nz))

    @pl.when(step == steps - 1)
    def _():
        rows = channels * ny
        ri = lax.broadcasted_iota(jnp.int32, (rows, rows), 0)
        ci = lax.broadcasted_iota(jnp.int32, (rows, rows), 1)
        diag = jnp.where(ri % ny == ci % ny, acc_ref[...], 0.0)
        er = lax.broadcasted_iota(jnp.int32, (channels, rows), 0)
        ec = lax.broadcasted_iota(jnp.int32, (channels, rows), 1)
        gather = (ec // ny == er).astype(jnp.float32)
        part = jnp.dot(gather, diag, precision=lax.Precision.HIGHEST, preferred_element_type=jnp.float32)
        gram_ref[...] = lax.dot_general(
            part, gather, (((1,), (1,)), ((), ())), precision=lax.Precision.HIGHEST,
            preferred_element_type=jnp.float32)
        wait_sent(step - 1)
        wait_sent(step)
        for at in range(zc_ref.shape[3] // width):
            cols = pl.ds(at * width, width)
            for k in range(1, count):
                origin = lax.rem(me + count - k, count)
                pltpu.make_async_remote_copy(
                    src_ref=slot_ref.at[0, pl.ds(me * mz_local, mz_local)],
                    dst_ref=zc_ref.at[origin, :, :, cols],
                    send_sem=send_sems.at[at, k],
                    recv_sem=recv_sems.at[at, k],
                    device_id={axis: origin},
                    device_id_type=mesh_ids,
                ).wait_recv()


def analysis(hidden_pre, cotangent, table_z, axis, count):
    channels, nx, ny, nz = hidden_pre.shape
    modes = table_z.shape[0]
    steps = nx // XB
    field_spec = pl.BlockSpec((channels, XB, ny, nz), lambda i: (0, i, 0, 0))
    return pl.pallas_call(
        functools.partial(analysis_kernel, axis, count),
        grid=(steps,),
        in_specs=[field_spec, field_spec, pl.BlockSpec((modes, nz), lambda i: (0, 0))],
        out_specs=[
            pl.BlockSpec(memory_space=pl.ANY),
            pl.BlockSpec((channels, channels), lambda i: (0, 0)),
        ],
        out_shape=[
            jax.ShapeDtypeStruct(
                (count, modes // count, 2 * channels, nx * ny), jnp.bfloat16),
            jax.ShapeDtypeStruct((channels, channels), jnp.float32),
        ],
        scratch_shapes=[
            pltpu.VMEM((channels * ny, channels * ny), jnp.float32),
            pltpu.VMEM((modes, 2 * channels, XB * ny), jnp.float32),
            pltpu.VMEM((2, modes, 2 * channels, XB * ny), jnp.bfloat16),
            pltpu.SemaphoreType.DMA((steps,)),
            pltpu.SemaphoreType.DMA((steps, count)),
            pltpu.SemaphoreType.DMA((steps, count)),
        ],
        compiler_params=pltpu.CompilerParams(
            dimension_semantics=("arbitrary",), vmem_limit_bytes=60 * 1024 * 1024,
            collective_id=0, has_side_effects=True,
        ),
    )(hidden_pre, cotangent, table_z)


def synthesis_kernel(axis, count, other, others, h_ref, g_ref, xs_ref, tyt_ref, tz_ref, sw_ref,
                     gs_ref, out_ref, skip_out_ref, ks_ref, stage_ref, send_ref, recv_ref,
                     local_sems, send_sems, recv_sems, wbuf_ref, wlocal_sem, wsend_sems,
                     wrecv_sems, nbuf_ref, nlocal_sem, nsend_sems, nrecv_sems, wstage_ref):
    mesh_ids = pl.DeviceIdType.MESH
    step = pl.program_id(0)
    steps = pl.num_programs(0)
    channels, xb, ny, nz = h_ref.shape
    rows = channels * ny
    chunk = 2 * xb
    me = lax.axis_index(axis)
    me_w = lax.axis_index(other)

    def narrow_copies():
        local = pltpu.make_async_copy(gs_ref, nbuf_ref.at[me], nlocal_sem)
        remote = []
        for k in range(1, count):
            peer = lax.rem(me + k, count)
            remote.append(pltpu.make_async_remote_copy(
                src_ref=gs_ref,
                dst_ref=nbuf_ref.at[me],
                send_sem=nsend_sems.at[k],
                recv_sem=nrecv_sems.at[k],
                device_id={axis: peer},
                device_id_type=mesh_ids,
            ))
        return local, remote

    def wide_copies():
        local = pltpu.make_async_copy(wstage_ref, wbuf_ref.at[me_w], wlocal_sem)
        remote = []
        for k in range(1, others):
            peer = lax.rem(me_w + k, others)
            remote.append(pltpu.make_async_remote_copy(
                src_ref=wstage_ref,
                dst_ref=wbuf_ref.at[me_w],
                send_sem=wsend_sems.at[k],
                recv_sem=wrecv_sems.at[k],
                device_id={other: peer},
                device_id_type=mesh_ids,
            ))
        return local, remote

    def copies(at):
        part = pl.ds(pl.multiple_of(at * chunk, chunk), chunk)
        local = pltpu.make_async_copy(
            send_ref.at[me, part], recv_ref.at[me, part], local_sems.at[at])
        remote = []
        for k in range(1, count):
            peer = lax.rem(me + k, count)
            remote.append(pltpu.make_async_remote_copy(
                src_ref=send_ref.at[peer, part],
                dst_ref=recv_ref.at[me, part],
                send_sem=send_sems.at[at, k],
                recv_sem=recv_sems.at[at, k],
                device_id={axis: peer},
                device_id_type=mesh_ids,
            ))
        return local, remote

    @pl.when(step == 0)
    def _():
        barrier = pltpu.get_barrier_semaphore()
        for k in range(1, count):
            peer = lax.rem(me + k, count)
            pl.semaphore_signal(barrier, inc=1, device_id={axis: peer}, device_id_type=mesh_ids)
        for k in range(1, others):
            peer = lax.rem(me_w + k, others)
            pl.semaphore_signal(barrier, inc=1, device_id={other: peer}, device_id_type=mesh_ids)
        pl.semaphore_wait(barrier, count - 1 + others - 1)
        nlocal, nremote = narrow_copies()
        nlocal.start()
        for copy in nremote:
            copy.start()
        y_synthesis_body(xs_ref, tyt_ref, send_ref, stage_ref)
        for at in range(recv_ref.shape[1] // chunk):
            local, remote = copies(at)
            local.start()
            for copy in remote:
                copy.start()
        r = lax.broadcasted_iota(jnp.int32, (rows, channels), 0)
        k = lax.broadcasted_iota(jnp.int32, (rows, channels), 1)
        expand = (r // ny == k).astype(jnp.float32)
        spread = jnp.dot(expand, sw_ref[...].astype(jnp.float32), preferred_element_type=jnp.float32)
        kr = lax.broadcasted_iota(jnp.int32, (channels, rows), 0)
        kc = lax.broadcasted_iota(jnp.int32, (channels, rows), 1)
        expand_t = (kc // ny == kr).astype(jnp.float32)
        full = jnp.dot(spread, expand_t, preferred_element_type=jnp.float32)
        ri = lax.broadcasted_iota(jnp.int32, (rows, rows), 0)
        ci = lax.broadcasted_iota(jnp.int32, (rows, rows), 1)
        ks_ref[...] = jnp.where(ri % ny == ci % ny, full, 0.0).astype(ks_ref.dtype)

    @pl.when(step == 1)
    def _():
        nlocal, nremote = narrow_copies()
        nlocal.wait()
        for k in range(1, count):
            nremote[k - 1].wait_send()
            origin = lax.rem(me + count - k, count)
            pltpu.make_async_remote_copy(
                src_ref=gs_ref,
                dst_ref=nbuf_ref.at[origin],
                send_sem=nsend_sems.at[k],
                recv_sem=nrecv_sems.at[k],
                device_id={axis: origin},
                device_id_type=mesh_ids,
            ).wait_recv()
        total = nbuf_ref[0]
        for src in range(1, count):
            total = total + nbuf_ref[src]
        wstage_ref[...] = total
        wlocal, wremote = wide_copies()
        wlocal.start()
        for copy in wremote:
            copy.start()

    local, _ = copies(step)
    local.wait()
    part = pl.ds(pl.multiple_of(step * chunk, chunk), chunk)
    for k in range(1, count):
        origin = lax.rem(me + count - k, count)
        pltpu.make_async_remote_copy(
            src_ref=send_ref.at[me, part],
            dst_ref=recv_ref.at[origin, part],
            send_sem=send_sems.at[step, k],
            recv_sem=recv_sems.at[step, k],
            device_id={axis: origin},
            device_id_type=mesh_ids,
        ).wait_recv()

    tz = tz_ref[...]
    ks = ks_ref[...]
    ys = recv_ref[:, part, :].astype(jnp.float32)
    for x in range(xb):
        lo = ys[:, 2 * x, :]
        hi = ys[:, 2 * x + 1, :]
        lhs = jnp.concatenate([lo, hi], axis=0).T.astype(jnp.bfloat16)
        spec = jnp.dot(lhs, tz, preferred_element_type=jnp.float32)
        spec = spec.astype(jnp.bfloat16).astype(jnp.float32)
        skip = jnp.dot(ks, g_ref[:, x].reshape(channels * ny, nz), preferred_element_type=jnp.float32)
        activ = jnp.tanh(h_ref[:, x].astype(jnp.float32)).reshape(channels * ny, nz)
        grad = (spec + skip) * (1.0 - activ * activ)
        out_ref[:, x] = grad.astype(jnp.bfloat16).reshape(channels, ny, nz)

    @pl.when(step == steps - 1)
    def _():
        for at in range(recv_ref.shape[1] // chunk):
            _, remote = copies(at)
            for copy in remote:
                copy.wait_send()
        wlocal, wremote = wide_copies()
        wlocal.wait()
        for k in range(1, others):
            wremote[k - 1].wait_send()
            origin = lax.rem(me_w + others - k, others)
            pltpu.make_async_remote_copy(
                src_ref=wstage_ref,
                dst_ref=wbuf_ref.at[origin],
                send_sem=wsend_sems.at[k],
                recv_sem=wrecv_sems.at[k],
                device_id={other: origin},
                device_id_type=mesh_ids,
            ).wait_recv()
        total = wbuf_ref[0]
        for src in range(1, others):
            total = total + wbuf_ref[src]
        skip_out_ref[...] = total * (1.0 / math.sqrt(NX * NY * NZ))


def synthesis(hidden_pre, cotangent, xsynth, table_yt, table_z, skip_weight, skip_terms, axis,
              count, other, others):
    channels, nx, ny, nz = hidden_pre.shape
    modes = table_z.shape[0]
    mz_local = xsynth.shape[0]
    steps = nx // XB
    field_spec = pl.BlockSpec((channels, XB, ny, nz), lambda i: (0, i, 0, 0))
    whole = pl.BlockSpec(memory_space=pltpu.VMEM)
    lanes = channels * ny
    return pl.pallas_call(
        functools.partial(synthesis_kernel, axis, count, other, others),
        grid=(steps,),
        in_specs=[
            field_spec,
            field_spec,
            whole,
            whole,
            pl.BlockSpec((modes, nz), lambda i: (0, 0)),
            pl.BlockSpec((channels, channels), lambda i: (0, 0)),
            whole,
        ],
        out_specs=[field_spec, pl.BlockSpec((channels, channels), lambda i: (0, 0))],
        out_shape=[
            jax.ShapeDtypeStruct(hidden_pre.shape, jnp.bfloat16),
            jax.ShapeDtypeStruct((channels, channels), jnp.float32),
        ],
        scratch_shapes=[
            pltpu.VMEM((lanes, lanes), jnp.bfloat16),
            pltpu.VMEM((count * lanes // 128, nx * mz_local, 128), jnp.float32),
            pltpu.VMEM((count, nx * mz_local, lanes), jnp.bfloat16),
            pltpu.VMEM((count, nx * mz_local, lanes), jnp.bfloat16),
            pltpu.SemaphoreType.DMA((steps,)),
            pltpu.SemaphoreType.DMA((steps, count)),
            pltpu.SemaphoreType.DMA((steps, count)),
            pltpu.VMEM((others, channels, channels), jnp.float32),
            pltpu.SemaphoreType.DMA,
            pltpu.SemaphoreType.DMA((others,)),
            pltpu.SemaphoreType.DMA((others,)),
            pltpu.VMEM((count, channels, channels), jnp.float32),
            pltpu.SemaphoreType.DMA,
            pltpu.SemaphoreType.DMA((count,)),
            pltpu.SemaphoreType.DMA((count,)),
            pltpu.VMEM((channels, channels), jnp.float32),
        ],
        compiler_params=pltpu.CompilerParams(
            dimension_semantics=("arbitrary",), vmem_limit_bytes=60 * 1024 * 1024,
            collective_id=1, has_side_effects=True,
        ),
    )(hidden_pre, cotangent, xsynth, table_yt, table_z, skip_weight, skip_terms)


def y_synthesis_body(xs_ref, tyt_ref, out_ref, stage_ref):
    mz_local, channels, modes, nx = xs_ref.shape
    blocks, _, lanes = out_ref.shape
    ny = lanes // channels
    tyt = jnp.broadcast_to(tyt_ref[...][None], (channels,) + tyt_ref.shape)
    for z in range(mz_local):
        part = jnp.einsum(
            "cym,cmx->cyx", tyt, xs_ref[z], preferred_element_type=jnp.float32
        ).astype(jnp.bfloat16).astype(jnp.float32)
        for d in range(blocks):
            piece = part[:, d * ny:(d + 1) * ny, :].reshape(channels * ny, nx).T
            for q in range(lanes // 128):
                stage_ref[d * (lanes // 128) + q, pl.ds(z, nx, stride=mz_local), :] = (
                    piece[:, q * 128:(q + 1) * 128])
    for d in range(blocks):
        for q in range(lanes // 128):
            out_ref[d, :, q * 128:(q + 1) * 128] = (
                stage_ref[d * (lanes // 128) + q].astype(out_ref.dtype))


def modes_kernel(sp_ref, w_ref, gm_ref, bs_ref):
    channels = sp_ref.shape[1] // 2
    sp = sp_ref[...]
    q = sp[:, channels:]
    columns = []
    for c in range(channels):
        gm_ref[:, c * channels:(c + 1) * channels] = sp[:, c:c + 1] * q
        weights = w_ref[:, c * channels:(c + 1) * channels].astype(jnp.float32)
        columns.append(jnp.sum(weights * q, axis=1, keepdims=True))
    bs_ref[...] = jnp.concatenate(columns, axis=1).astype(bs_ref.dtype)


def modes_step(spectra, weights):
    rows, both = spectra.shape
    channels = both // 2
    vmem = pl.BlockSpec(memory_space=pltpu.VMEM)
    return pl.pallas_call(
        modes_kernel,
        in_specs=[vmem, vmem],
        out_specs=[vmem, vmem],
        out_shape=[
            jax.ShapeDtypeStruct((rows, channels * channels), jnp.float32),
            jax.ShapeDtypeStruct((rows, channels), jnp.bfloat16),
        ],
    )(spectra, weights)


def per_device(hidden_pre, cotangent, mode_weight, skip_weight):
    highest = lax.Precision.HIGHEST
    channels, nx, ny, nz = hidden_pre.shape
    mode_count = mode_weight.shape[2]
    n_narrow = lax.axis_size("narrow")
    n_wide = lax.axis_size("wide")
    table_x = basis_table(mode_count, NX)
    table_y = basis_table(mode_count, NY)
    table_z = basis_table(mode_count, NZ)

    zc, gram = analysis(hidden_pre, cotangent, table_z, "narrow", n_narrow)
    mz_local = mode_count // n_narrow
    zc = zc.reshape(n_narrow, mz_local, 2 * channels, nx, ny)
    ycoeffs = jnp.einsum(
        "smcxl,nsl->mcnx", zc, table_y.reshape(mode_count, n_narrow, ny),
        preferred_element_type=jnp.float32,
    ).astype(jnp.bfloat16)
    ycoeffs = lax.all_to_all(ycoeffs, "wide", split_axis=2, concat_axis=3, tiled=True)
    spectra = jnp.einsum("zcyx,kx->zykc", ycoeffs, table_x, preferred_element_type=jnp.float32)
    z_local, y_local = (spectra.shape[0], spectra.shape[1])
    grad_modes, back_spec = modes_step(
        spectra.reshape(z_local * y_local * mode_count, 2 * channels),
        mode_weight.reshape(z_local * y_local * mode_count, channels * channels),
    )
    grad_modes = grad_modes.reshape(z_local, y_local, mode_count, channels * channels)
    back_spec = jnp.transpose(
        back_spec.reshape(z_local, y_local, mode_count, channels), (0, 3, 1, 2)
    )
    xsynth = jnp.einsum(
        "zcyk,kx->zcyx", back_spec, table_x, preferred_element_type=jnp.float32
    ).astype(jnp.bfloat16)
    xsynth = lax.all_to_all(xsynth, "wide", split_axis=3, concat_axis=2, tiled=True)
    table_zp = jnp.transpose(table_z.reshape(n_narrow, mz_local, nz), (1, 0, 2)).reshape(mode_count, nz)
    grad_hidden, grad_skip = synthesis(
        hidden_pre, cotangent, xsynth, jnp.transpose(table_y), table_zp, skip_weight, gram,
        "narrow", n_narrow, "wide", n_wide)

    return (grad_hidden, grad_modes, grad_skip)


def solution(mesh):
    in_specs = (
        P(None, "wide", "narrow", None),
        P(None, "wide", "narrow", None),
        P("narrow", "wide", None, None),
        P(),
    )
    out_specs = (P(None, "wide", "narrow", None), P("narrow", "wide", None, None), P())
    return jax.shard_map(
        per_device, mesh=mesh, in_specs=in_specs, out_specs=out_specs, check_vma=False
    )
```

```python
import functools
import math

import jax
import jax.numpy as jnp
from jax import lax
from jax.experimental import pallas as pl
from jax.experimental.pallas import tpu as pltpu
from jax.sharding import PartitionSpec as P

NX = 256
NY = 256
NZ = 256
XB = 8


def basis_table(mode_count, length):
    mode_index = jnp.arange(mode_count, dtype=jnp.int32)
    halfway = mode_count // 2
    frequency = jnp.where(mode_index < halfway, mode_index, mode_index - halfway + 1)
    points = jnp.arange(length, dtype=jnp.int32)
    phases = frequency[:, None] * points[None, :] % length
    angles = phases.astype(jnp.float32) * (2.0 * math.pi / length)
    values_table = jnp.where((mode_index < halfway)[:, None], jnp.cos(angles), jnp.sin(angles))
    return (values_table * (1.0 / math.sqrt(length))).astype(jnp.bfloat16)


def _nt(a, b):
    return lax.dot_general(a, b, (((1,), (1,)), ((), ())), preferred_element_type=jnp.float32)


def analysis_kernel(axis, count, h_ref, g_ref, tz_ref, zc_ref, gram_ref, acc_ref, stage_ref,
                    slot_ref, local_sems, send_sems, recv_sems):
    mesh_ids = pl.DeviceIdType.MESH
    step = pl.program_id(0)
    steps = pl.num_programs(0)
    channels, xb, ny, nz = h_ref.shape
    width = xb * ny
    mz_local = slot_ref.shape[1] // count
    me = lax.axis_index(axis)

    def copies(at):
        slot = lax.rem(at, 2)
        cols = pl.ds(pl.multiple_of(at * width, width), width)
        local = pltpu.make_async_copy(
            slot_ref.at[slot, pl.ds(me * mz_local, mz_local)],
            zc_ref.at[me, :, :, cols],
            local_sems.at[at],
        )
        remote = []
        for k in range(1, count):
            peer = lax.rem(me + k, count)
            remote.append(pltpu.make_async_remote_copy(
                src_ref=slot_ref.at[slot, pl.ds(peer * mz_local, mz_local)],
                dst_ref=zc_ref.at[me, :, :, cols],
                send_sem=send_sems.at[at, k],
                recv_sem=recv_sems.at[at, k],
                device_id={axis: peer},
                device_id_type=mesh_ids,
            ))
        return local, remote

    def wait_sent(at):
        local, remote = copies(at)
        local.wait()
        for copy in remote:
            copy.wait_send()

    @pl.when(step == 0)
    def _():
        acc_ref[...] = jnp.zeros_like(acc_ref)
        barrier = pltpu.get_barrier_semaphore()
        for k in range(1, count):
            peer = lax.rem(me + k, count)
            pl.semaphore_signal(barrier, inc=1, device_id={axis: peer}, device_id_type=mesh_ids)
        pl.semaphore_wait(barrier, count - 1)

    @pl.when(step >= 2)
    def _():
        wait_sent(step - 2)

    tz = tz_ref[...]
    li = jnp.tanh(h_ref[...].astype(jnp.float32)).astype(jnp.bfloat16)
    g = g_ref[...]
    zl = _nt(tz, li.reshape(channels * width, nz))
    zg = _nt(tz, g.reshape(channels * width, nz))
    for c in range(channels):
        stage_ref[:, c, :] = zl[:, c * width:(c + 1) * width]
        stage_ref[:, channels + c, :] = zg[:, c * width:(c + 1) * width]
    slot_ref[lax.rem(step, 2)] = stage_ref[...].astype(jnp.bfloat16)
    local, remote = copies(step)
    local.start()
    for copy in remote:
        copy.start()
    for x in range(xb):
        acc_ref[...] += _nt(li[:, x].reshape(channels * ny, nz), g[:, x].reshape(channels * ny, nz))

    @pl.when(step == steps - 1)
    def _():
        rows = channels * ny
        ri = lax.broadcasted_iota(jnp.int32, (rows, rows), 0)
        ci = lax.broadcasted_iota(jnp.int32, (rows, rows), 1)
        diag = jnp.where(ri % ny == ci % ny, acc_ref[...], 0.0)
        er = lax.broadcasted_iota(jnp.int32, (channels, rows), 0)
        ec = lax.broadcasted_iota(jnp.int32, (channels, rows), 1)
        gather = (ec // ny == er).astype(jnp.float32)
        part = jnp.dot(gather, diag, precision=lax.Precision.HIGHEST, preferred_element_type=jnp.float32)
        gram_ref[...] = lax.dot_general(
            part, gather, (((1,), (1,)), ((), ())), precision=lax.Precision.HIGHEST,
            preferred_element_type=jnp.float32)
        wait_sent(step - 1)
        wait_sent(step)
        for at in range(zc_ref.shape[3] // width):
            cols = pl.ds(at * width, width)
            for k in range(1, count):
                origin = lax.rem(me + count - k, count)
                pltpu.make_async_remote_copy(
                    src_ref=slot_ref.at[0, pl.ds(me * mz_local, mz_local)],
                    dst_ref=zc_ref.at[origin, :, :, cols],
                    send_sem=send_sems.at[at, k],
                    recv_sem=recv_sems.at[at, k],
                    device_id={axis: origin},
                    device_id_type=mesh_ids,
                ).wait_recv()


def analysis(hidden_pre, cotangent, table_z, axis, count):
    channels, nx, ny, nz = hidden_pre.shape
    modes = table_z.shape[0]
    steps = nx // XB
    field_spec = pl.BlockSpec((channels, XB, ny, nz), lambda i: (0, i, 0, 0))
    return pl.pallas_call(
        functools.partial(analysis_kernel, axis, count),
        grid=(steps,),
        in_specs=[field_spec, field_spec, pl.BlockSpec((modes, nz), lambda i: (0, 0))],
        out_specs=[
            pl.BlockSpec(memory_space=pl.ANY),
            pl.BlockSpec((channels, channels), lambda i: (0, 0)),
        ],
        out_shape=[
            jax.ShapeDtypeStruct(
                (count, modes // count, 2 * channels, nx * ny), jnp.bfloat16),
            jax.ShapeDtypeStruct((channels, channels), jnp.float32),
        ],
        scratch_shapes=[
            pltpu.VMEM((channels * ny, channels * ny), jnp.float32),
            pltpu.VMEM((modes, 2 * channels, XB * ny), jnp.float32),
            pltpu.VMEM((2, modes, 2 * channels, XB * ny), jnp.bfloat16),
            pltpu.SemaphoreType.DMA((steps,)),
            pltpu.SemaphoreType.DMA((steps, count)),
            pltpu.SemaphoreType.DMA((steps, count)),
        ],
        compiler_params=pltpu.CompilerParams(
            dimension_semantics=("arbitrary",), vmem_limit_bytes=60 * 1024 * 1024,
            collective_id=0, has_side_effects=True,
        ),
    )(hidden_pre, cotangent, table_z)


def exchange_kernel(axis, count, src_ref, dst_ref, local_sem, send_sems, recv_sems):
    mesh_ids = pl.DeviceIdType.MESH
    me = lax.axis_index(axis)
    barrier = pltpu.get_barrier_semaphore()
    for k in range(1, count):
        peer = lax.rem(me + k, count)
        pl.semaphore_signal(barrier, inc=1, device_id={axis: peer}, device_id_type=mesh_ids)
    pl.semaphore_wait(barrier, count - 1)
    local = pltpu.make_async_copy(src_ref.at[me], dst_ref.at[me], local_sem)
    local.start()
    sends = []
    for k in range(1, count):
        peer = lax.rem(me + k, count)
        copy = pltpu.make_async_remote_copy(
            src_ref=src_ref.at[peer],
            dst_ref=dst_ref.at[me],
            send_sem=send_sems.at[k],
            recv_sem=recv_sems.at[k],
            device_id={axis: peer},
            device_id_type=mesh_ids,
        )
        copy.start()
        sends.append(copy)
    local.wait()
    for k in range(1, count):
        sends[k - 1].wait_send()
        origin = lax.rem(me + count - k, count)
        incoming = pltpu.make_async_remote_copy(
            src_ref=src_ref.at[me],
            dst_ref=dst_ref.at[origin],
            send_sem=send_sems.at[k],
            recv_sem=recv_sems.at[k],
            device_id={axis: origin},
            device_id_type=mesh_ids,
        )
        incoming.wait_recv()


def exchange(chunks, axis, count, collective_id):
    return pl.pallas_call(
        functools.partial(exchange_kernel, axis, count),
        in_specs=[pl.BlockSpec(memory_space=pl.ANY)],
        out_specs=pl.BlockSpec(memory_space=pl.ANY),
        out_shape=jax.ShapeDtypeStruct(chunks.shape, chunks.dtype),
        scratch_shapes=[
            pltpu.SemaphoreType.DMA,
            pltpu.SemaphoreType.DMA((count,)),
            pltpu.SemaphoreType.DMA((count,)),
        ],
        compiler_params=pltpu.CompilerParams(collective_id=collective_id, has_side_effects=True),
    )(chunks)


def synthesis_kernel(axis, count, other, others, h_ref, g_ref, xs_ref, tyt_ref, tz_ref, sw_ref,
                     gs_ref, out_ref, skip_out_ref, ks_ref, stage_ref, send_ref, recv_ref,
                     local_sems, send_sems, recv_sems, wbuf_ref, wlocal_sem, wsend_sems,
                     wrecv_sems, nbuf_ref, nlocal_sem, nsend_sems, nrecv_sems, wstage_ref):
    mesh_ids = pl.DeviceIdType.MESH
    step = pl.program_id(0)
    steps = pl.num_programs(0)
    channels, xb, ny, nz = h_ref.shape
    rows = channels * ny
    chunk = 2 * xb
    me = lax.axis_index(axis)
    me_w = lax.axis_index(other)

    def narrow_copies():
        local = pltpu.make_async_copy(gs_ref, nbuf_ref.at[me], nlocal_sem)
        remote = []
        for k in range(1, count):
            peer = lax.rem(me + k, count)
            remote.append(pltpu.make_async_remote_copy(
                src_ref=gs_ref,
                dst_ref=nbuf_ref.at[me],
                send_sem=nsend_sems.at[k],
                recv_sem=nrecv_sems.at[k],
                device_id={axis: peer},
                device_id_type=mesh_ids,
            ))
        return local, remote

    def wide_copies():
        local = pltpu.make_async_copy(wstage_ref, wbuf_ref.at[me_w], wlocal_sem)
        remote = []
        for k in range(1, others):
            peer = lax.rem(me_w + k, others)
            remote.append(pltpu.make_async_remote_copy(
                src_ref=wstage_ref,
                dst_ref=wbuf_ref.at[me_w],
                send_sem=wsend_sems.at[k],
                recv_sem=wrecv_sems.at[k],
                device_id={other: peer},
                device_id_type=mesh_ids,
            ))
        return local, remote

    def copies(at):
        part = pl.ds(pl.multiple_of(at * chunk, chunk), chunk)
        local = pltpu.make_async_copy(
            send_ref.at[me, part], recv_ref.at[me, part], local_sems.at[at])
        remote = []
        for k in range(1, count):
            peer = lax.rem(me + k, count)
            remote.append(pltpu.make_async_remote_copy(
                src_ref=send_ref.at[peer, part],
                dst_ref=recv_ref.at[me, part],
                send_sem=send_sems.at[at, k],
                recv_sem=recv_sems.at[at, k],
                device_id={axis: peer},
                device_id_type=mesh_ids,
            ))
        return local, remote

    @pl.when(step == 0)
    def _():
        barrier = pltpu.get_barrier_semaphore()
        for k in range(1, count):
            peer = lax.rem(me + k, count)
            pl.semaphore_signal(barrier, inc=1, device_id={axis: peer}, device_id_type=mesh_ids)
        for k in range(1, others):
            peer = lax.rem(me_w + k, others)
            pl.semaphore_signal(barrier, inc=1, device_id={other: peer}, device_id_type=mesh_ids)
        pl.semaphore_wait(barrier, count - 1 + others - 1)
        nlocal, nremote = narrow_copies()
        nlocal.start()
        for copy in nremote:
            copy.start()
        y_synthesis_body(xs_ref, tyt_ref, send_ref, stage_ref)
        for at in range(recv_ref.shape[1] // chunk):
            local, remote = copies(at)
            local.start()
            for copy in remote:
                copy.start()
        r = lax.broadcasted_iota(jnp.int32, (rows, channels), 0)
        k = lax.broadcasted_iota(jnp.int32, (rows, channels), 1)
        expand = (r // ny == k).astype(jnp.float32)
        spread = jnp.dot(expand, sw_ref[...].astype(jnp.float32), preferred_element_type=jnp.float32)
        kr = lax.broadcasted_iota(jnp.int32, (channels, rows), 0)
        kc = lax.broadcasted_iota(jnp.int32, (channels, rows), 1)
        expand_t = (kc // ny == kr).astype(jnp.float32)
        full = jnp.dot(spread, expand_t, preferred_element_type=jnp.float32)
        ri = lax.broadcasted_iota(jnp.int32, (rows, rows), 0)
        ci = lax.broadcasted_iota(jnp.int32, (rows, rows), 1)
        ks_ref[...] = jnp.where(ri % ny == ci % ny, full, 0.0).astype(ks_ref.dtype)

    @pl.when(step == 1)
    def _():
        nlocal, nremote = narrow_copies()
        nlocal.wait()
        for k in range(1, count):
            nremote[k - 1].wait_send()
            origin = lax.rem(me + count - k, count)
            pltpu.make_async_remote_copy(
                src_ref=gs_ref,
                dst_ref=nbuf_ref.at[origin],
                send_sem=nsend_sems.at[k],
                recv_sem=nrecv_sems.at[k],
                device_id={axis: origin},
                device_id_type=mesh_ids,
            ).wait_recv()
        total = nbuf_ref[0]
        for src in range(1, count):
            total = total + nbuf_ref[src]
        wstage_ref[...] = total
        wlocal, wremote = wide_copies()
        wlocal.start()
        for copy in wremote:
            copy.start()

    local, _ = copies(step)
    local.wait()
    part = pl.ds(pl.multiple_of(step * chunk, chunk), chunk)
    for k in range(1, count):
        origin = lax.rem(me + count - k, count)
        pltpu.make_async_remote_copy(
            src_ref=send_ref.at[me, part],
            dst_ref=recv_ref.at[origin, part],
            send_sem=send_sems.at[step, k],
            recv_sem=recv_sems.at[step, k],
            device_id={axis: origin},
            device_id_type=mesh_ids,
        ).wait_recv()

    tz = tz_ref[...]
    ks = ks_ref[...]
    ys = recv_ref[:, part, :].astype(jnp.float32)
    for x in range(xb):
        lo = ys[:, 2 * x, :]
        hi = ys[:, 2 * x + 1, :]
        lhs = jnp.concatenate([lo, hi], axis=0).T.astype(jnp.bfloat16)
        spec = jnp.dot(lhs, tz, preferred_element_type=jnp.float32)
        spec = spec.astype(jnp.bfloat16).astype(jnp.float32)
        skip = jnp.dot(ks, g_ref[:, x].reshape(channels * ny, nz), preferred_element_type=jnp.float32)
        activ = jnp.tanh(h_ref[:, x].astype(jnp.float32)).reshape(channels * ny, nz)
        grad = (spec + skip) * (1.0 - activ * activ)
        out_ref[:, x] = grad.astype(jnp.bfloat16).reshape(channels, ny, nz)

    @pl.when(step == steps - 1)
    def _():
        for at in range(recv_ref.shape[1] // chunk):
            _, remote = copies(at)
            for copy in remote:
                copy.wait_send()
        wlocal, wremote = wide_copies()
        wlocal.wait()
        for k in range(1, others):
            wremote[k - 1].wait_send()
            origin = lax.rem(me_w + others - k, others)
            pltpu.make_async_remote_copy(
                src_ref=wstage_ref,
                dst_ref=wbuf_ref.at[origin],
                send_sem=wsend_sems.at[k],
                recv_sem=wrecv_sems.at[k],
                device_id={other: origin},
                device_id_type=mesh_ids,
            ).wait_recv()
        total = wbuf_ref[0]
        for src in range(1, others):
            total = total + wbuf_ref[src]
        skip_out_ref[...] = total * (1.0 / math.sqrt(NX * NY * NZ))


def synthesis(hidden_pre, cotangent, xsynth, table_yt, table_z, skip_weight, skip_terms, axis,
              count, other, others):
    channels, nx, ny, nz = hidden_pre.shape
    modes = table_z.shape[0]
    mz_local = xsynth.shape[0]
    steps = nx // XB
    field_spec = pl.BlockSpec((channels, XB, ny, nz), lambda i: (0, i, 0, 0))
    whole = pl.BlockSpec(memory_space=pltpu.VMEM)
    lanes = channels * ny
    return pl.pallas_call(
        functools.partial(synthesis_kernel, axis, count, other, others),
        grid=(steps,),
        in_specs=[
            field_spec,
            field_spec,
            whole,
            whole,
            pl.BlockSpec((modes, nz), lambda i: (0, 0)),
            pl.BlockSpec((channels, channels), lambda i: (0, 0)),
            whole,
        ],
        out_specs=[field_spec, pl.BlockSpec((channels, channels), lambda i: (0, 0))],
        out_shape=[
            jax.ShapeDtypeStruct(hidden_pre.shape, jnp.bfloat16),
            jax.ShapeDtypeStruct((channels, channels), jnp.float32),
        ],
        scratch_shapes=[
            pltpu.VMEM((lanes, lanes), jnp.bfloat16),
            pltpu.VMEM((count * lanes // 128, nx * mz_local, 128), jnp.float32),
            pltpu.VMEM((count, nx * mz_local, lanes), jnp.bfloat16),
            pltpu.VMEM((count, nx * mz_local, lanes), jnp.bfloat16),
            pltpu.SemaphoreType.DMA((steps,)),
            pltpu.SemaphoreType.DMA((steps, count)),
            pltpu.SemaphoreType.DMA((steps, count)),
            pltpu.VMEM((others, channels, channels), jnp.float32),
            pltpu.SemaphoreType.DMA,
            pltpu.SemaphoreType.DMA((others,)),
            pltpu.SemaphoreType.DMA((others,)),
            pltpu.VMEM((count, channels, channels), jnp.float32),
            pltpu.SemaphoreType.DMA,
            pltpu.SemaphoreType.DMA((count,)),
            pltpu.SemaphoreType.DMA((count,)),
            pltpu.VMEM((channels, channels), jnp.float32),
        ],
        compiler_params=pltpu.CompilerParams(
            dimension_semantics=("arbitrary",), vmem_limit_bytes=60 * 1024 * 1024,
            collective_id=1, has_side_effects=True,
        ),
    )(hidden_pre, cotangent, xsynth, table_yt, table_z, skip_weight, skip_terms)


def y_synthesis_body(xs_ref, tyt_ref, out_ref, stage_ref):
    mz_local, channels, modes, nx = xs_ref.shape
    blocks, _, lanes = out_ref.shape
    ny = lanes // channels
    tyt = jnp.broadcast_to(tyt_ref[...][None], (channels,) + tyt_ref.shape)
    for z in range(mz_local):
        part = jnp.einsum(
            "cym,cmx->cyx", tyt, xs_ref[z], preferred_element_type=jnp.float32
        ).astype(jnp.bfloat16).astype(jnp.float32)
        for d in range(blocks):
            piece = part[:, d * ny:(d + 1) * ny, :].reshape(channels * ny, nx).T
            for q in range(lanes // 128):
                stage_ref[d * (lanes // 128) + q, pl.ds(z, nx, stride=mz_local), :] = (
                    piece[:, q * 128:(q + 1) * 128])
    for d in range(blocks):
        for q in range(lanes // 128):
            out_ref[d, :, q * 128:(q + 1) * 128] = (
                stage_ref[d * (lanes // 128) + q].astype(out_ref.dtype))


def modes_kernel(sp_ref, w_ref, gm_ref, bs_ref):
    highest = lax.Precision.HIGHEST
    channels = sp_ref.shape[1] // 2
    width = channels * channels
    sp = sp_ref[...]
    er = lax.broadcasted_iota(jnp.int32, (channels, width), 0)
    ec = lax.broadcasted_iota(jnp.int32, (channels, width), 1)
    spread = (ec // channels == er).astype(jnp.float32)
    tile = (ec % channels == er).astype(jnp.float32)
    s_rep = jnp.dot(sp[:, :channels], spread, precision=highest, preferred_element_type=jnp.float32)
    q_rep = jnp.dot(sp[:, channels:], tile, precision=highest, preferred_element_type=jnp.float32)
    gm_ref[...] = s_rep * q_rep
    weighted = w_ref[...].astype(jnp.float32) * q_rep
    back = lax.dot_general(
        weighted, spread, (((1,), (1,)), ((), ())), precision=highest,
        preferred_element_type=jnp.float32)
    bs_ref[...] = back.astype(bs_ref.dtype)


def modes_step(spectra, weights):
    rows, both = spectra.shape
    channels = both // 2
    vmem = pl.BlockSpec(memory_space=pltpu.VMEM)
    return pl.pallas_call(
        modes_kernel,
        in_specs=[vmem, vmem],
        out_specs=[vmem, vmem],
        out_shape=[
            jax.ShapeDtypeStruct((rows, channels * channels), jnp.float32),
            jax.ShapeDtypeStruct((rows, channels), jnp.bfloat16),
        ],
    )(spectra, weights)


def per_device(hidden_pre, cotangent, mode_weight, skip_weight):
    highest = lax.Precision.HIGHEST
    channels, nx, ny, nz = hidden_pre.shape
    mode_count = mode_weight.shape[2]
    n_narrow = lax.axis_size("narrow")
    n_wide = lax.axis_size("wide")
    table_x = basis_table(mode_count, NX)
    table_y = basis_table(mode_count, NY)
    table_z = basis_table(mode_count, NZ)

    zc, gram = analysis(hidden_pre, cotangent, table_z, "narrow", n_narrow)
    mz_local = mode_count // n_narrow
    zc = zc.reshape(n_narrow, mz_local, 2 * channels, nx, ny)
    my_local = mode_count // n_wide
    ycoeffs = jnp.einsum(
        "smcxl,dnsl->dnmcx", zc, table_y.reshape(n_wide, my_local, n_narrow, ny),
        preferred_element_type=jnp.float32,
    ).astype(jnp.bfloat16)
    ycoeffs = ycoeffs.reshape(n_wide, 16, -1)
    ycoeffs = exchange(ycoeffs, "wide", n_wide, 2)
    ycoeffs = ycoeffs.reshape(n_wide, my_local, mz_local, 2 * channels, nx)
    spectra = jnp.einsum(
        "snmcx,ksx->mnkc", ycoeffs, table_x.reshape(mode_count, n_wide, nx),
        preferred_element_type=jnp.float32,
    )
    z_local, y_local = (spectra.shape[0], spectra.shape[1])
    grad_modes, back_spec = modes_step(
        spectra.reshape(z_local * y_local * mode_count, 2 * channels),
        mode_weight.reshape(z_local * y_local * mode_count, channels * channels),
    )
    grad_modes = grad_modes.reshape(z_local, y_local, mode_count, channels * channels)
    back_spec = jnp.transpose(
        back_spec.reshape(z_local, y_local, mode_count, channels), (0, 3, 1, 2)
    )
    xsynth = jnp.einsum(
        "zcyk,kdx->dzcyx", back_spec, table_x.reshape(mode_count, n_wide, nx),
        preferred_element_type=jnp.float32,
    ).astype(jnp.bfloat16)
    xsynth = xsynth.reshape(n_wide, mz_local * channels, -1)
    xsynth = exchange(xsynth, "wide", n_wide, 3)
    xsynth = xsynth.reshape(n_wide, mz_local, channels, my_local, nx)
    xsynth = jnp.transpose(xsynth, (1, 2, 0, 3, 4)).reshape(mz_local, channels, mode_count, nx)
    table_zp = jnp.transpose(table_z.reshape(n_narrow, mz_local, nz), (1, 0, 2)).reshape(mode_count, nz)
    grad_hidden, grad_skip = synthesis(
        hidden_pre, cotangent, xsynth, jnp.transpose(table_y), table_zp, skip_weight, gram,
        "narrow", n_narrow, "wide", n_wide)

    return (grad_hidden, grad_modes, grad_skip)


def solution(mesh):
    in_specs = (
        P(None, "wide", "narrow", None),
        P(None, "wide", "narrow", None),
        P("narrow", "wide", None, None),
        P(),
    )
    out_specs = (P(None, "wide", "narrow", None), P("narrow", "wide", None, None), P())
    return jax.shard_map(
        per_device, mesh=mesh, in_specs=in_specs, out_specs=out_specs, check_vma=False
    )
```

```python
import functools
import math

import jax
import jax.numpy as jnp
from jax import lax
from jax.experimental import pallas as pl
from jax.experimental.pallas import tpu as pltpu
from jax.sharding import PartitionSpec as P

NX = 256
NY = 256
NZ = 256
XB = 8


def basis_table(mode_count, length):
    mode_index = jnp.arange(mode_count, dtype=jnp.int32)
    halfway = mode_count // 2
    frequency = jnp.where(mode_index < halfway, mode_index, mode_index - halfway + 1)
    points = jnp.arange(length, dtype=jnp.int32)
    phases = frequency[:, None] * points[None, :] % length
    angles = phases.astype(jnp.float32) * (2.0 * math.pi / length)
    values_table = jnp.where((mode_index < halfway)[:, None], jnp.cos(angles), jnp.sin(angles))
    return (values_table * (1.0 / math.sqrt(length))).astype(jnp.bfloat16)


def _nt(a, b):
    return lax.dot_general(a, b, (((1,), (1,)), ((), ())), preferred_element_type=jnp.float32)


def analysis_kernel(axis, count, h_ref, g_ref, tz_ref, zc_ref, gram_ref, acc_ref, stage_ref,
                    slot_ref, local_sems, send_sems, recv_sems):
    mesh_ids = pl.DeviceIdType.MESH
    step = pl.program_id(0)
    steps = pl.num_programs(0)
    channels, xb, ny, nz = h_ref.shape
    width = xb * ny
    mz_local = slot_ref.shape[1] // count
    me = lax.axis_index(axis)

    def copies(at):
        slot = lax.rem(at, 2)
        cols = pl.ds(pl.multiple_of(at * width, width), width)
        local = pltpu.make_async_copy(
            slot_ref.at[slot, pl.ds(me * mz_local, mz_local)],
            zc_ref.at[me, :, :, cols],
            local_sems.at[at],
        )
        remote = []
        for k in range(1, count):
            peer = lax.rem(me + k, count)
            remote.append(pltpu.make_async_remote_copy(
                src_ref=slot_ref.at[slot, pl.ds(peer * mz_local, mz_local)],
                dst_ref=zc_ref.at[me, :, :, cols],
                send_sem=send_sems.at[at, k],
                recv_sem=recv_sems.at[at, k],
                device_id={axis: peer},
                device_id_type=mesh_ids,
            ))
        return local, remote

    def wait_sent(at):
        local, remote = copies(at)
        local.wait()
        for copy in remote:
            copy.wait_send()

    @pl.when(step == 0)
    def _():
        acc_ref[...] = jnp.zeros_like(acc_ref)
        barrier = pltpu.get_barrier_semaphore()
        for k in range(1, count):
            peer = lax.rem(me + k, count)
            pl.semaphore_signal(barrier, inc=1, device_id={axis: peer}, device_id_type=mesh_ids)
        pl.semaphore_wait(barrier, count - 1)

    @pl.when(step >= 2)
    def _():
        wait_sent(step - 2)

    tz = tz_ref[...]
    li = jnp.tanh(h_ref[...].astype(jnp.float32)).astype(jnp.bfloat16)
    g = g_ref[...]
    zl = _nt(tz, li.reshape(channels * width, nz))
    zg = _nt(tz, g.reshape(channels * width, nz))
    for c in range(channels):
        stage_ref[:, c, :] = zl[:, c * width:(c + 1) * width]
        stage_ref[:, channels + c, :] = zg[:, c * width:(c + 1) * width]
    slot_ref[lax.rem(step, 2)] = stage_ref[...].astype(jnp.bfloat16)
    local, remote = copies(step)
    local.start()
    for copy in remote:
        copy.start()
    for x in range(xb):
        acc_ref[...] += _nt(li[:, x].reshape(channels * ny, nz), g[:, x].reshape(channels * ny, nz))

    @pl.when(step == steps - 1)
    def _():
        rows = channels * ny
        ri = lax.broadcasted_iota(jnp.int32, (rows, rows), 0)
        ci = lax.broadcasted_iota(jnp.int32, (rows, rows), 1)
        diag = jnp.where(ri % ny == ci % ny, acc_ref[...], 0.0)
        er = lax.broadcasted_iota(jnp.int32, (channels, rows), 0)
        ec = lax.broadcasted_iota(jnp.int32, (channels, rows), 1)
        gather = (ec // ny == er).astype(jnp.float32)
        part = jnp.dot(gather, diag, precision=lax.Precision.HIGHEST, preferred_element_type=jnp.float32)
        gram_ref[...] = lax.dot_general(
            part, gather, (((1,), (1,)), ((), ())), precision=lax.Precision.HIGHEST,
            preferred_element_type=jnp.float32)
        wait_sent(step - 1)
        wait_sent(step)
        for at in range(zc_ref.shape[3] // width):
            cols = pl.ds(at * width, width)
            for k in range(1, count):
                origin = lax.rem(me + count - k, count)
                pltpu.make_async_remote_copy(
                    src_ref=slot_ref.at[0, pl.ds(me * mz_local, mz_local)],
                    dst_ref=zc_ref.at[origin, :, :, cols],
                    send_sem=send_sems.at[at, k],
                    recv_sem=recv_sems.at[at, k],
                    device_id={axis: origin},
                    device_id_type=mesh_ids,
                ).wait_recv()


def analysis(hidden_pre, cotangent, table_z, axis, count):
    channels, nx, ny, nz = hidden_pre.shape
    modes = table_z.shape[0]
    steps = nx // XB
    field_spec = pl.BlockSpec((channels, XB, ny, nz), lambda i: (0, i, 0, 0))
    return pl.pallas_call(
        functools.partial(analysis_kernel, axis, count),
        grid=(steps,),
        in_specs=[field_spec, field_spec, pl.BlockSpec((modes, nz), lambda i: (0, 0))],
        out_specs=[
            pl.BlockSpec(memory_space=pl.ANY),
            pl.BlockSpec((channels, channels), lambda i: (0, 0)),
        ],
        out_shape=[
            jax.ShapeDtypeStruct(
                (count, modes // count, 2 * channels, nx * ny), jnp.bfloat16),
            jax.ShapeDtypeStruct((channels, channels), jnp.float32),
        ],
        scratch_shapes=[
            pltpu.VMEM((channels * ny, channels * ny), jnp.float32),
            pltpu.VMEM((modes, 2 * channels, XB * ny), jnp.float32),
            pltpu.VMEM((2, modes, 2 * channels, XB * ny), jnp.bfloat16),
            pltpu.SemaphoreType.DMA((steps,)),
            pltpu.SemaphoreType.DMA((steps, count)),
            pltpu.SemaphoreType.DMA((steps, count)),
        ],
        compiler_params=pltpu.CompilerParams(
            dimension_semantics=("arbitrary",), vmem_limit_bytes=60 * 1024 * 1024,
            collective_id=0, has_side_effects=True,
        ),
    )(hidden_pre, cotangent, table_z)


def synthesis_kernel(axis, count, other, others, h_ref, g_ref, xs_ref, tyt_ref, tz_ref, sw_ref,
                     gs_ref, out_ref, skip_out_ref, ks_ref, stage_ref, send_ref, recv_ref,
                     local_sems, send_sems, recv_sems, wbuf_ref, wlocal_sem, wsend_sems,
                     wrecv_sems, nbuf_ref, nlocal_sem, nsend_sems, nrecv_sems, wstage_ref):
    mesh_ids = pl.DeviceIdType.MESH
    step = pl.program_id(0)
    steps = pl.num_programs(0)
    channels, xb, ny, nz = h_ref.shape
    rows = channels * ny
    chunk = 2 * xb
    me = lax.axis_index(axis)
    me_w = lax.axis_index(other)

    def narrow_copies():
        local = pltpu.make_async_copy(gs_ref, nbuf_ref.at[me], nlocal_sem)
        remote = []
        for k in range(1, count):
            peer = lax.rem(me + k, count)
            remote.append(pltpu.make_async_remote_copy(
                src_ref=gs_ref,
                dst_ref=nbuf_ref.at[me],
                send_sem=nsend_sems.at[k],
                recv_sem=nrecv_sems.at[k],
                device_id={axis: peer},
                device_id_type=mesh_ids,
            ))
        return local, remote

    def wide_copies():
        local = pltpu.make_async_copy(wstage_ref, wbuf_ref.at[me_w], wlocal_sem)
        remote = []
        for k in range(1, others):
            peer = lax.rem(me_w + k, others)
            remote.append(pltpu.make_async_remote_copy(
                src_ref=wstage_ref,
                dst_ref=wbuf_ref.at[me_w],
                send_sem=wsend_sems.at[k],
                recv_sem=wrecv_sems.at[k],
                device_id={other: peer},
                device_id_type=mesh_ids,
            ))
        return local, remote

    def copies(at):
        part = pl.ds(pl.multiple_of(at * chunk, chunk), chunk)
        local = pltpu.make_async_copy(
            send_ref.at[me, part], recv_ref.at[me, part], local_sems.at[at])
        remote = []
        for k in range(1, count):
            peer = lax.rem(me + k, count)
            remote.append(pltpu.make_async_remote_copy(
                src_ref=send_ref.at[peer, part],
                dst_ref=recv_ref.at[me, part],
                send_sem=send_sems.at[at, k],
                recv_sem=recv_sems.at[at, k],
                device_id={axis: peer},
                device_id_type=mesh_ids,
            ))
        return local, remote

    @pl.when(step == 0)
    def _():
        barrier = pltpu.get_barrier_semaphore()
        for k in range(1, count):
            peer = lax.rem(me + k, count)
            pl.semaphore_signal(barrier, inc=1, device_id={axis: peer}, device_id_type=mesh_ids)
        for k in range(1, others):
            peer = lax.rem(me_w + k, others)
            pl.semaphore_signal(barrier, inc=1, device_id={other: peer}, device_id_type=mesh_ids)
        pl.semaphore_wait(barrier, count - 1 + others - 1)
        nlocal, nremote = narrow_copies()
        nlocal.start()
        for copy in nremote:
            copy.start()
        y_synthesis_body(xs_ref, tyt_ref, send_ref, stage_ref, chunk, copies)
        r = lax.broadcasted_iota(jnp.int32, (rows, channels), 0)
        k = lax.broadcasted_iota(jnp.int32, (rows, channels), 1)
        expand = (r // ny == k).astype(jnp.float32)
        spread = jnp.dot(expand, sw_ref[...].astype(jnp.float32), preferred_element_type=jnp.float32)
        kr = lax.broadcasted_iota(jnp.int32, (channels, rows), 0)
        kc = lax.broadcasted_iota(jnp.int32, (channels, rows), 1)
        expand_t = (kc // ny == kr).astype(jnp.float32)
        full = jnp.dot(spread, expand_t, preferred_element_type=jnp.float32)
        ri = lax.broadcasted_iota(jnp.int32, (rows, rows), 0)
        ci = lax.broadcasted_iota(jnp.int32, (rows, rows), 1)
        ks_ref[...] = jnp.where(ri % ny == ci % ny, full, 0.0).astype(ks_ref.dtype)

    @pl.when(step == 1)
    def _():
        nlocal, nremote = narrow_copies()
        nlocal.wait()
        for k in range(1, count):
            nremote[k - 1].wait_send()
            origin = lax.rem(me + count - k, count)
            pltpu.make_async_remote_copy(
                src_ref=gs_ref,
                dst_ref=nbuf_ref.at[origin],
                send_sem=nsend_sems.at[k],
                recv_sem=nrecv_sems.at[k],
                device_id={axis: origin},
                device_id_type=mesh_ids,
            ).wait_recv()
        total = nbuf_ref[0]
        for src in range(1, count):
            total = total + nbuf_ref[src]
        wstage_ref[...] = total
        wlocal, wremote = wide_copies()
        wlocal.start()
        for copy in wremote:
            copy.start()

    local, _ = copies(step)
    local.wait()
    part = pl.ds(pl.multiple_of(step * chunk, chunk), chunk)
    for k in range(1, count):
        origin = lax.rem(me + count - k, count)
        pltpu.make_async_remote_copy(
            src_ref=send_ref.at[me, part],
            dst_ref=recv_ref.at[origin, part],
            send_sem=send_sems.at[step, k],
            recv_sem=recv_sems.at[step, k],
            device_id={axis: origin},
            device_id_type=mesh_ids,
        ).wait_recv()

    tz = tz_ref[...]
    ks = ks_ref[...]
    ys = recv_ref[:, part, :].astype(jnp.float32)
    for x in range(xb):
        lo = ys[:, 2 * x, :]
        hi = ys[:, 2 * x + 1, :]
        lhs = jnp.concatenate([lo, hi], axis=0).T.astype(jnp.bfloat16)
        spec = jnp.dot(lhs, tz, preferred_element_type=jnp.float32)
        spec = spec.astype(jnp.bfloat16).astype(jnp.float32)
        skip = jnp.dot(ks, g_ref[:, x].reshape(channels * ny, nz), preferred_element_type=jnp.float32)
        activ = jnp.tanh(h_ref[:, x].astype(jnp.float32)).reshape(channels * ny, nz)
        grad = (spec + skip) * (1.0 - activ * activ)
        out_ref[:, x] = grad.astype(jnp.bfloat16).reshape(channels, ny, nz)

    @pl.when(step == steps - 1)
    def _():
        for at in range(recv_ref.shape[1] // chunk):
            _, remote = copies(at)
            for copy in remote:
                copy.wait_send()
        wlocal, wremote = wide_copies()
        wlocal.wait()
        for k in range(1, others):
            wremote[k - 1].wait_send()
            origin = lax.rem(me_w + others - k, others)
            pltpu.make_async_remote_copy(
                src_ref=wstage_ref,
                dst_ref=wbuf_ref.at[origin],
                send_sem=wsend_sems.at[k],
                recv_sem=wrecv_sems.at[k],
                device_id={other: origin},
                device_id_type=mesh_ids,
            ).wait_recv()
        total = wbuf_ref[0]
        for src in range(1, others):
            total = total + wbuf_ref[src]
        skip_out_ref[...] = total * (1.0 / math.sqrt(NX * NY * NZ))


def synthesis(hidden_pre, cotangent, xsynth, table_yt, table_z, skip_weight, skip_terms, axis,
              count, other, others):
    channels, nx, ny, nz = hidden_pre.shape
    modes = table_z.shape[0]
    mz_local = xsynth.shape[0]
    steps = nx // XB
    field_spec = pl.BlockSpec((channels, XB, ny, nz), lambda i: (0, i, 0, 0))
    whole = pl.BlockSpec(memory_space=pltpu.VMEM)
    lanes = channels * ny
    return pl.pallas_call(
        functools.partial(synthesis_kernel, axis, count, other, others),
        grid=(steps,),
        in_specs=[
            field_spec,
            field_spec,
            whole,
            whole,
            pl.BlockSpec((modes, nz), lambda i: (0, 0)),
            pl.BlockSpec((channels, channels), lambda i: (0, 0)),
            whole,
        ],
        out_specs=[field_spec, pl.BlockSpec((channels, channels), lambda i: (0, 0))],
        out_shape=[
            jax.ShapeDtypeStruct(hidden_pre.shape, jnp.bfloat16),
            jax.ShapeDtypeStruct((channels, channels), jnp.float32),
        ],
        scratch_shapes=[
            pltpu.VMEM((lanes, lanes), jnp.bfloat16),
            pltpu.VMEM((count * lanes // 128, nx * mz_local, 128), jnp.float32),
            pltpu.VMEM((count, nx * mz_local, lanes), jnp.bfloat16),
            pltpu.VMEM((count, nx * mz_local, lanes), jnp.bfloat16),
            pltpu.SemaphoreType.DMA((steps,)),
            pltpu.SemaphoreType.DMA((steps, count)),
            pltpu.SemaphoreType.DMA((steps, count)),
            pltpu.VMEM((others, channels, channels), jnp.float32),
            pltpu.SemaphoreType.DMA,
            pltpu.SemaphoreType.DMA((others,)),
            pltpu.SemaphoreType.DMA((others,)),
            pltpu.VMEM((count, channels, channels), jnp.float32),
            pltpu.SemaphoreType.DMA,
            pltpu.SemaphoreType.DMA((count,)),
            pltpu.SemaphoreType.DMA((count,)),
            pltpu.VMEM((channels, channels), jnp.float32),
        ],
        compiler_params=pltpu.CompilerParams(
            dimension_semantics=("arbitrary",), vmem_limit_bytes=60 * 1024 * 1024,
            collective_id=1, has_side_effects=True,
        ),
    )(hidden_pre, cotangent, xsynth, table_yt, table_z, skip_weight, skip_terms)


def y_synthesis_body(xs_ref, tyt_ref, out_ref, stage_ref, chunk, copies):
    mz_local, channels, modes, nx = xs_ref.shape
    blocks, _, lanes = out_ref.shape
    ny = lanes // channels
    quarters = lanes // 128
    xs_per = chunk // mz_local
    tyt = jnp.broadcast_to(tyt_ref[...][None], (channels,) + tyt_ref.shape)
    parts = []
    for z in range(mz_local):
        parts.append(jnp.einsum(
            "cym,cmx->cyx", tyt, xs_ref[z], preferred_element_type=jnp.float32
        ).astype(jnp.bfloat16).astype(jnp.float32))
    for at in range(nx // xs_per):
        for z in range(mz_local):
            for d in range(blocks):
                piece = parts[z][:, d * ny:(d + 1) * ny, at * xs_per:(at + 1) * xs_per]
                piece = piece.reshape(channels * ny, xs_per).T
                for q in range(quarters):
                    stage_ref[d * quarters + q, pl.ds(at * chunk + z, xs_per, stride=mz_local), :] = (
                        piece[:, q * 128:(q + 1) * 128])
        for d in range(blocks):
            for q in range(quarters):
                out_ref[d, at * chunk:(at + 1) * chunk, q * 128:(q + 1) * 128] = (
                    stage_ref[d * quarters + q, at * chunk:(at + 1) * chunk].astype(out_ref.dtype))
        local, remote = copies(at)
        local.start()
        for copy in remote:
            copy.start()


def modes_kernel(sp_ref, w_ref, gm_ref, bs_ref):
    highest = lax.Precision.HIGHEST
    channels = sp_ref.shape[1] // 2
    width = channels * channels
    sp = sp_ref[...]
    er = lax.broadcasted_iota(jnp.int32, (channels, width), 0)
    ec = lax.broadcasted_iota(jnp.int32, (channels, width), 1)
    spread = (ec // channels == er).astype(jnp.float32)
    tile = (ec % channels == er).astype(jnp.float32)
    s_rep = jnp.dot(sp[:, :channels], spread, precision=highest, preferred_element_type=jnp.float32)
    q_rep = jnp.dot(sp[:, channels:], tile, precision=highest, preferred_element_type=jnp.float32)
    gm_ref[...] = s_rep * q_rep
    weighted = w_ref[...].astype(jnp.float32) * q_rep
    back = lax.dot_general(
        weighted, spread, (((1,), (1,)), ((), ())), precision=highest,
        preferred_element_type=jnp.float32)
    bs_ref[...] = back.astype(bs_ref.dtype)


def modes_step(spectra, weights):
    rows, both = spectra.shape
    channels = both // 2
    vmem = pl.BlockSpec(memory_space=pltpu.VMEM)
    return pl.pallas_call(
        modes_kernel,
        in_specs=[vmem, vmem],
        out_specs=[vmem, vmem],
        out_shape=[
            jax.ShapeDtypeStruct((rows, channels * channels), jnp.float32),
            jax.ShapeDtypeStruct((rows, channels), jnp.bfloat16),
        ],
    )(spectra, weights)


def per_device(hidden_pre, cotangent, mode_weight, skip_weight):
    highest = lax.Precision.HIGHEST
    channels, nx, ny, nz = hidden_pre.shape
    mode_count = mode_weight.shape[2]
    n_narrow = lax.axis_size("narrow")
    n_wide = lax.axis_size("wide")
    table_x = basis_table(mode_count, NX)
    table_y = basis_table(mode_count, NY)
    table_z = basis_table(mode_count, NZ)

    zc, gram = analysis(hidden_pre, cotangent, table_z, "narrow", n_narrow)
    mz_local = mode_count // n_narrow
    zc = zc.reshape(n_narrow, mz_local, 2 * channels, nx, ny)
    ycoeffs = jnp.einsum(
        "smcxl,nsl->mcnx", zc, table_y.reshape(mode_count, n_narrow, ny),
        preferred_element_type=jnp.float32,
    ).astype(jnp.bfloat16)
    ycoeffs = lax.all_to_all(ycoeffs, "wide", split_axis=2, concat_axis=3, tiled=True)
    spectra = jnp.einsum("zcyx,kx->zykc", ycoeffs, table_x, preferred_element_type=jnp.float32)
    z_local, y_local = (spectra.shape[0], spectra.shape[1])
    grad_modes, back_spec = modes_step(
        spectra.reshape(z_local * y_local * mode_count, 2 * channels),
        mode_weight.reshape(z_local * y_local * mode_count, channels * channels),
    )
    grad_modes = grad_modes.reshape(z_local, y_local, mode_count, channels * channels)
    back_spec = jnp.transpose(
        back_spec.reshape(z_local, y_local, mode_count, channels), (0, 3, 1, 2)
    )
    xsynth = jnp.einsum(
        "zcyk,kx->zcyx", back_spec, table_x, preferred_element_type=jnp.float32
    ).astype(jnp.bfloat16)
    xsynth = lax.all_to_all(xsynth, "wide", split_axis=3, concat_axis=2, tiled=True)
    table_zp = jnp.transpose(table_z.reshape(n_narrow, mz_local, nz), (1, 0, 2)).reshape(mode_count, nz)
    grad_hidden, grad_skip = synthesis(
        hidden_pre, cotangent, xsynth, jnp.transpose(table_y), table_zp, skip_weight, gram,
        "narrow", n_narrow, "wide", n_wide)

    return (grad_hidden, grad_modes, grad_skip)


def solution(mesh):
    in_specs = (
        P(None, "wide", "narrow", None),
        P(None, "wide", "narrow", None),
        P("narrow", "wide", None, None),
        P(),
    )
    out_specs = (P(None, "wide", "narrow", None), P("narrow", "wide", None, None), P())
    return jax.shard_map(
        per_device, mesh=mesh, in_specs=in_specs, out_specs=out_specs, check_vma=False
    )
```

```python
import functools
import math

import jax
import jax.numpy as jnp
from jax import lax
from jax.experimental import pallas as pl
from jax.experimental.pallas import tpu as pltpu
from jax.sharding import PartitionSpec as P

NX = 256
NY = 256
NZ = 256
XB = 8


def basis_table(mode_count, length):
    mode_index = jnp.arange(mode_count, dtype=jnp.int32)
    halfway = mode_count // 2
    frequency = jnp.where(mode_index < halfway, mode_index, mode_index - halfway + 1)
    points = jnp.arange(length, dtype=jnp.int32)
    phases = frequency[:, None] * points[None, :] % length
    angles = phases.astype(jnp.float32) * (2.0 * math.pi / length)
    values_table = jnp.where((mode_index < halfway)[:, None], jnp.cos(angles), jnp.sin(angles))
    return (values_table * (1.0 / math.sqrt(length))).astype(jnp.bfloat16)


def _nt(a, b):
    return lax.dot_general(a, b, (((1,), (1,)), ((), ())), preferred_element_type=jnp.float32)


def analysis_kernel(axis, count, h_ref, g_ref, tz_ref, zc_ref, gram_ref, acc_ref, stage_ref,
                    slot_ref, local_sems, send_sems, recv_sems):
    mesh_ids = pl.DeviceIdType.MESH
    step = pl.program_id(0)
    steps = pl.num_programs(0)
    channels, xb, ny, nz = h_ref.shape
    width = xb * ny
    mz_local = slot_ref.shape[1] // count
    me = lax.axis_index(axis)

    def copies(at):
        slot = lax.rem(at, 2)
        cols = pl.ds(pl.multiple_of(at * width, width), width)
        local = pltpu.make_async_copy(
            slot_ref.at[slot, pl.ds(me * mz_local, mz_local)],
            zc_ref.at[me, :, :, cols],
            local_sems.at[at],
        )
        remote = []
        for k in range(1, count):
            peer = lax.rem(me + k, count)
            remote.append(pltpu.make_async_remote_copy(
                src_ref=slot_ref.at[slot, pl.ds(peer * mz_local, mz_local)],
                dst_ref=zc_ref.at[me, :, :, cols],
                send_sem=send_sems.at[at, k],
                recv_sem=recv_sems.at[at, k],
                device_id={axis: peer},
                device_id_type=mesh_ids,
            ))
        return local, remote

    def wait_sent(at):
        local, remote = copies(at)
        local.wait()
        for copy in remote:
            copy.wait_send()

    @pl.when(step == 0)
    def _():
        acc_ref[...] = jnp.zeros_like(acc_ref)
        barrier = pltpu.get_barrier_semaphore()
        for k in range(1, count):
            peer = lax.rem(me + k, count)
            pl.semaphore_signal(barrier, inc=1, device_id={axis: peer}, device_id_type=mesh_ids)
        pl.semaphore_wait(barrier, count - 1)

    @pl.when(step >= 2)
    def _():
        wait_sent(step - 2)

    tz = tz_ref[...]
    li = jnp.tanh(h_ref[...].astype(jnp.float32)).astype(jnp.bfloat16)
    g = g_ref[...]
    zl = _nt(tz, li.reshape(channels * width, nz))
    zg = _nt(tz, g.reshape(channels * width, nz))
    for c in range(channels):
        stage_ref[:, c, :] = zl[:, c * width:(c + 1) * width]
        stage_ref[:, channels + c, :] = zg[:, c * width:(c + 1) * width]
    slot_ref[lax.rem(step, 2)] = stage_ref[...].astype(jnp.bfloat16)
    local, remote = copies(step)
    local.start()
    for copy in remote:
        copy.start()
    for x in range(xb):
        acc_ref[...] += _nt(li[:, x].reshape(channels * ny, nz), g[:, x].reshape(channels * ny, nz))

    @pl.when(step == steps - 1)
    def _():
        rows = channels * ny
        ri = lax.broadcasted_iota(jnp.int32, (rows, rows), 0)
        ci = lax.broadcasted_iota(jnp.int32, (rows, rows), 1)
        diag = jnp.where(ri % ny == ci % ny, acc_ref[...], 0.0)
        er = lax.broadcasted_iota(jnp.int32, (channels, rows), 0)
        ec = lax.broadcasted_iota(jnp.int32, (channels, rows), 1)
        gather = (ec // ny == er).astype(jnp.float32)
        part = jnp.dot(gather, diag, precision=lax.Precision.HIGHEST, preferred_element_type=jnp.float32)
        gram_ref[...] = lax.dot_general(
            part, gather, (((1,), (1,)), ((), ())), precision=lax.Precision.HIGHEST,
            preferred_element_type=jnp.float32)
        wait_sent(step - 1)
        wait_sent(step)
        for at in range(zc_ref.shape[3] // width):
            cols = pl.ds(at * width, width)
            for k in range(1, count):
                origin = lax.rem(me + count - k, count)
                pltpu.make_async_remote_copy(
                    src_ref=slot_ref.at[0, pl.ds(me * mz_local, mz_local)],
                    dst_ref=zc_ref.at[origin, :, :, cols],
                    send_sem=send_sems.at[at, k],
                    recv_sem=recv_sems.at[at, k],
                    device_id={axis: origin},
                    device_id_type=mesh_ids,
                ).wait_recv()


def analysis(hidden_pre, cotangent, table_z, axis, count):
    channels, nx, ny, nz = hidden_pre.shape
    modes = table_z.shape[0]
    steps = nx // XB
    field_spec = pl.BlockSpec((channels, XB, ny, nz), lambda i: (0, i, 0, 0))
    return pl.pallas_call(
        functools.partial(analysis_kernel, axis, count),
        grid=(steps,),
        in_specs=[field_spec, field_spec, pl.BlockSpec((modes, nz), lambda i: (0, 0))],
        out_specs=[
            pl.BlockSpec(memory_space=pl.ANY),
            pl.BlockSpec((channels, channels), lambda i: (0, 0)),
        ],
        out_shape=[
            jax.ShapeDtypeStruct(
                (count, modes // count, 2 * channels, nx * ny), jnp.bfloat16),
            jax.ShapeDtypeStruct((channels, channels), jnp.float32),
        ],
        scratch_shapes=[
            pltpu.VMEM((channels * ny, channels * ny), jnp.float32),
            pltpu.VMEM((modes, 2 * channels, XB * ny), jnp.float32),
            pltpu.VMEM((2, modes, 2 * channels, XB * ny), jnp.bfloat16),
            pltpu.SemaphoreType.DMA((steps,)),
            pltpu.SemaphoreType.DMA((steps, count)),
            pltpu.SemaphoreType.DMA((steps, count)),
        ],
        compiler_params=pltpu.CompilerParams(
            dimension_semantics=("arbitrary",), vmem_limit_bytes=60 * 1024 * 1024,
            collective_id=0, has_side_effects=True,
        ),
    )(hidden_pre, cotangent, table_z)


def synthesis_kernel(axis, count, other, others, h_ref, g_ref, xs_ref, tyt_ref, tz_ref, sw_ref,
                     gs_ref, out_ref, skip_out_ref, ks_ref, stage_ref, send_ref, recv_ref,
                     local_sems, send_sems, recv_sems, wbuf_ref, wlocal_sem, wsend_sems,
                     wrecv_sems, nbuf_ref, nlocal_sem, nsend_sems, nrecv_sems, wstage_ref):
    mesh_ids = pl.DeviceIdType.MESH
    step = pl.program_id(0)
    steps = pl.num_programs(0)
    channels, xb, ny, nz = h_ref.shape
    rows = channels * ny
    chunk = 2 * xb
    me = lax.axis_index(axis)
    me_w = lax.axis_index(other)

    def narrow_copies():
        local = pltpu.make_async_copy(gs_ref, nbuf_ref.at[me], nlocal_sem)
        remote = []
        for k in range(1, count):
            peer = lax.rem(me + k, count)
            remote.append(pltpu.make_async_remote_copy(
                src_ref=gs_ref,
                dst_ref=nbuf_ref.at[me],
                send_sem=nsend_sems.at[k],
                recv_sem=nrecv_sems.at[k],
                device_id={axis: peer},
                device_id_type=mesh_ids,
            ))
        return local, remote

    def wide_copies():
        local = pltpu.make_async_copy(wstage_ref, wbuf_ref.at[me_w], wlocal_sem)
        remote = []
        for k in range(1, others):
            peer = lax.rem(me_w + k, others)
            remote.append(pltpu.make_async_remote_copy(
                src_ref=wstage_ref,
                dst_ref=wbuf_ref.at[me_w],
                send_sem=wsend_sems.at[k],
                recv_sem=wrecv_sems.at[k],
                device_id={other: peer},
                device_id_type=mesh_ids,
            ))
        return local, remote

    def copies(at):
        part = pl.ds(pl.multiple_of(at * chunk, chunk), chunk)
        local = pltpu.make_async_copy(
            send_ref.at[me, part], recv_ref.at[me, part], local_sems.at[at])
        remote = []
        for k in range(1, count):
            peer = lax.rem(me + k, count)
            remote.append(pltpu.make_async_remote_copy(
                src_ref=send_ref.at[peer, part],
                dst_ref=recv_ref.at[me, part],
                send_sem=send_sems.at[at, k],
                recv_sem=recv_sems.at[at, k],
                device_id={axis: peer},
                device_id_type=mesh_ids,
            ))
        return local, remote

    @pl.when(step == 0)
    def _():
        barrier = pltpu.get_barrier_semaphore()
        for k in range(1, count):
            peer = lax.rem(me + k, count)
            pl.semaphore_signal(barrier, inc=1, device_id={axis: peer}, device_id_type=mesh_ids)
        for k in range(1, others):
            peer = lax.rem(me_w + k, others)
            pl.semaphore_signal(barrier, inc=1, device_id={other: peer}, device_id_type=mesh_ids)
        pl.semaphore_wait(barrier, count - 1 + others - 1)
        nlocal, nremote = narrow_copies()
        nlocal.start()
        for copy in nremote:
            copy.start()
        y_synthesis_body(xs_ref, tyt_ref, send_ref, stage_ref)
        for at in range(recv_ref.shape[1] // chunk):
            local, remote = copies(at)
            local.start()
            for copy in remote:
                copy.start()
        r = lax.broadcasted_iota(jnp.int32, (rows, channels), 0)
        k = lax.broadcasted_iota(jnp.int32, (rows, channels), 1)
        expand = (r // ny == k).astype(jnp.float32)
        spread = jnp.dot(expand, sw_ref[...].astype(jnp.float32), preferred_element_type=jnp.float32)
        kr = lax.broadcasted_iota(jnp.int32, (channels, rows), 0)
        kc = lax.broadcasted_iota(jnp.int32, (channels, rows), 1)
        expand_t = (kc // ny == kr).astype(jnp.float32)
        full = jnp.dot(spread, expand_t, preferred_element_type=jnp.float32)
        ri = lax.broadcasted_iota(jnp.int32, (rows, rows), 0)
        ci = lax.broadcasted_iota(jnp.int32, (rows, rows), 1)
        ks_ref[...] = jnp.where(ri % ny == ci % ny, full, 0.0).astype(ks_ref.dtype)

    @pl.when(step == 1)
    def _():
        nlocal, nremote = narrow_copies()
        nlocal.wait()
        for k in range(1, count):
            nremote[k - 1].wait_send()
            origin = lax.rem(me + count - k, count)
            pltpu.make_async_remote_copy(
                src_ref=gs_ref,
                dst_ref=nbuf_ref.at[origin],
                send_sem=nsend_sems.at[k],
                recv_sem=nrecv_sems.at[k],
                device_id={axis: origin},
                device_id_type=mesh_ids,
            ).wait_recv()
        total = nbuf_ref[0]
        for src in range(1, count):
            total = total + nbuf_ref[src]
        wstage_ref[...] = total
        wlocal, wremote = wide_copies()
        wlocal.start()
        for copy in wremote:
            copy.start()

    local, _ = copies(step)
    local.wait()
    part = pl.ds(pl.multiple_of(step * chunk, chunk), chunk)
    for k in range(1, count):
        origin = lax.rem(me + count - k, count)
        pltpu.make_async_remote_copy(
            src_ref=send_ref.at[me, part],
            dst_ref=recv_ref.at[origin, part],
            send_sem=send_sems.at[step, k],
            recv_sem=recv_sems.at[step, k],
            device_id={axis: origin},
            device_id_type=mesh_ids,
        ).wait_recv()

    tz = tz_ref[...]
    ks = ks_ref[...]
    ys = recv_ref[:, part, :].astype(jnp.float32)
    for x in range(xb):
        lo = ys[:, 2 * x, :]
        hi = ys[:, 2 * x + 1, :]
        lhs = jnp.concatenate([lo, hi], axis=0).T.astype(jnp.bfloat16)
        spec = jnp.dot(lhs, tz, preferred_element_type=jnp.float32)
        spec = spec.astype(jnp.bfloat16).astype(jnp.float32)
        skip = jnp.dot(ks, g_ref[:, x].reshape(channels * ny, nz), preferred_element_type=jnp.float32)
        activ = jnp.tanh(h_ref[:, x].astype(jnp.float32)).reshape(channels * ny, nz)
        grad = (spec + skip) * (1.0 - activ * activ)
        out_ref[:, x] = grad.astype(jnp.bfloat16).reshape(channels, ny, nz)

    @pl.when(step == steps - 1)
    def _():
        for at in range(recv_ref.shape[1] // chunk):
            _, remote = copies(at)
            for copy in remote:
                copy.wait_send()
        wlocal, wremote = wide_copies()
        wlocal.wait()
        for k in range(1, others):
            wremote[k - 1].wait_send()
            origin = lax.rem(me_w + others - k, others)
            pltpu.make_async_remote_copy(
                src_ref=wstage_ref,
                dst_ref=wbuf_ref.at[origin],
                send_sem=wsend_sems.at[k],
                recv_sem=wrecv_sems.at[k],
                device_id={other: origin},
                device_id_type=mesh_ids,
            ).wait_recv()
        total = wbuf_ref[0]
        for src in range(1, others):
            total = total + wbuf_ref[src]
        skip_out_ref[...] = total * (1.0 / math.sqrt(NX * NY * NZ))


def synthesis(hidden_pre, cotangent, xsynth, table_yt, table_z, skip_weight, skip_terms, axis,
              count, other, others):
    channels, nx, ny, nz = hidden_pre.shape
    modes = table_z.shape[0]
    mz_local = xsynth.shape[0]
    steps = nx // XB
    field_spec = pl.BlockSpec((channels, XB, ny, nz), lambda i: (0, i, 0, 0))
    whole = pl.BlockSpec(memory_space=pltpu.VMEM)
    lanes = channels * ny
    return pl.pallas_call(
        functools.partial(synthesis_kernel, axis, count, other, others),
        grid=(steps,),
        in_specs=[
            field_spec,
            field_spec,
            whole,
            whole,
            pl.BlockSpec((modes, nz), lambda i: (0, 0)),
            pl.BlockSpec((channels, channels), lambda i: (0, 0)),
            whole,
        ],
        out_specs=[field_spec, pl.BlockSpec((channels, channels), lambda i: (0, 0))],
        out_shape=[
            jax.ShapeDtypeStruct(hidden_pre.shape, jnp.bfloat16),
            jax.ShapeDtypeStruct((channels, channels), jnp.float32),
        ],
        scratch_shapes=[
            pltpu.VMEM((lanes, lanes), jnp.bfloat16),
            pltpu.VMEM((count * lanes // 128, nx * mz_local, 128), jnp.float32),
            pltpu.VMEM((count, nx * mz_local, lanes), jnp.bfloat16),
            pltpu.VMEM((count, nx * mz_local, lanes), jnp.bfloat16),
            pltpu.SemaphoreType.DMA((steps,)),
            pltpu.SemaphoreType.DMA((steps, count)),
            pltpu.SemaphoreType.DMA((steps, count)),
            pltpu.VMEM((others, channels, channels), jnp.float32),
            pltpu.SemaphoreType.DMA,
            pltpu.SemaphoreType.DMA((others,)),
            pltpu.SemaphoreType.DMA((others,)),
            pltpu.VMEM((count, channels, channels), jnp.float32),
            pltpu.SemaphoreType.DMA,
            pltpu.SemaphoreType.DMA((count,)),
            pltpu.SemaphoreType.DMA((count,)),
            pltpu.VMEM((channels, channels), jnp.float32),
        ],
        compiler_params=pltpu.CompilerParams(
            dimension_semantics=("arbitrary",), vmem_limit_bytes=60 * 1024 * 1024,
            collective_id=1, has_side_effects=True,
        ),
    )(hidden_pre, cotangent, xsynth, table_yt, table_z, skip_weight, skip_terms)


def y_synthesis_body(xs_ref, tyt_ref, out_ref, stage_ref):
    mz_local, channels, modes, nx = xs_ref.shape
    blocks, _, lanes = out_ref.shape
    ny = lanes // channels
    tyt = jnp.broadcast_to(tyt_ref[...][None], (channels,) + tyt_ref.shape)
    for z in range(mz_local):
        part = jnp.einsum(
            "cym,cmx->cyx", tyt, xs_ref[z], preferred_element_type=jnp.float32
        ).astype(jnp.bfloat16).astype(jnp.float32)
        for d in range(blocks):
            piece = part[:, d * ny:(d + 1) * ny, :].reshape(channels * ny, nx).T
            for q in range(lanes // 128):
                stage_ref[d * (lanes // 128) + q, pl.ds(z, nx, stride=mz_local), :] = (
                    piece[:, q * 128:(q + 1) * 128])
    for d in range(blocks):
        for q in range(lanes // 128):
            out_ref[d, :, q * 128:(q + 1) * 128] = (
                stage_ref[d * (lanes // 128) + q].astype(out_ref.dtype))


def modes_kernel(sp_ref, w_ref, gm_ref, bs_ref):
    highest = lax.Precision.HIGHEST
    channels = sp_ref.shape[1] // 2
    width = channels * channels
    sp = sp_ref[...]
    er = lax.broadcasted_iota(jnp.int32, (channels, width), 0)
    ec = lax.broadcasted_iota(jnp.int32, (channels, width), 1)
    spread = (ec // channels == er).astype(jnp.float32)
    tile = (ec % channels == er).astype(jnp.float32)
    q_rep = jnp.dot(sp[:, channels:], tile, precision=highest, preferred_element_type=jnp.float32)
    q = sp[:, channels:]
    for c in range(channels):
        gm_ref[:, c * channels:(c + 1) * channels] = sp[:, c:c + 1] * q
    weighted = w_ref[...].astype(jnp.float32) * q_rep
    back = lax.dot_general(
        weighted, spread, (((1,), (1,)), ((), ())), precision=highest,
        preferred_element_type=jnp.float32)
    bs_ref[...] = back.astype(bs_ref.dtype)


def modes_step(spectra, weights):
    rows, both = spectra.shape
    channels = both // 2
    vmem = pl.BlockSpec(memory_space=pltpu.VMEM)
    return pl.pallas_call(
        modes_kernel,
        in_specs=[vmem, vmem],
        out_specs=[vmem, vmem],
        out_shape=[
            jax.ShapeDtypeStruct((rows, channels * channels), jnp.float32),
            jax.ShapeDtypeStruct((rows, channels), jnp.bfloat16),
        ],
    )(spectra, weights)


def per_device(hidden_pre, cotangent, mode_weight, skip_weight):
    highest = lax.Precision.HIGHEST
    channels, nx, ny, nz = hidden_pre.shape
    mode_count = mode_weight.shape[2]
    n_narrow = lax.axis_size("narrow")
    n_wide = lax.axis_size("wide")
    table_x = basis_table(mode_count, NX)
    table_y = basis_table(mode_count, NY)
    table_z = basis_table(mode_count, NZ)

    zc, gram = analysis(hidden_pre, cotangent, table_z, "narrow", n_narrow)
    mz_local = mode_count // n_narrow
    zc = zc.reshape(n_narrow, mz_local, 2 * channels, nx, ny)
    ycoeffs = jnp.einsum(
        "smcxl,nsl->mcnx", zc, table_y.reshape(mode_count, n_narrow, ny),
        preferred_element_type=jnp.float32,
    ).astype(jnp.bfloat16)
    ycoeffs = lax.all_to_all(ycoeffs, "wide", split_axis=2, concat_axis=3, tiled=True)
    spectra = jnp.einsum("zcyx,kx->zykc", ycoeffs, table_x, preferred_element_type=jnp.float32)
    z_local, y_local = (spectra.shape[0], spectra.shape[1])
    grad_modes, back_spec = modes_step(
        spectra.reshape(z_local * y_local * mode_count, 2 * channels),
        mode_weight.reshape(z_local * y_local * mode_count, channels * channels),
    )
    grad_modes = grad_modes.reshape(z_local, y_local, mode_count, channels * channels)
    back_spec = jnp.transpose(
        back_spec.reshape(z_local, y_local, mode_count, channels), (0, 3, 1, 2)
    )
    xsynth = jnp.einsum(
        "zcyk,kx->zcyx", back_spec, table_x, preferred_element_type=jnp.float32
    ).astype(jnp.bfloat16)
    xsynth = lax.all_to_all(xsynth, "wide", split_axis=3, concat_axis=2, tiled=True)
    table_zp = jnp.transpose(table_z.reshape(n_narrow, mz_local, nz), (1, 0, 2)).reshape(mode_count, nz)
    grad_hidden, grad_skip = synthesis(
        hidden_pre, cotangent, xsynth, jnp.transpose(table_y), table_zp, skip_weight, gram,
        "narrow", n_narrow, "wide", n_wide)

    return (grad_hidden, grad_modes, grad_skip)


def solution(mesh):
    in_specs = (
        P(None, "wide", "narrow", None),
        P(None, "wide", "narrow", None),
        P("narrow", "wide", None, None),
        P(),
    )
    out_specs = (P(None, "wide", "narrow", None), P("narrow", "wide", None, None), P())
    return jax.shard_map(
        per_device, mesh=mesh, in_specs=in_specs, out_specs=out_specs, check_vma=False
    )
```

```python
import functools
import math

import jax
import jax.numpy as jnp
from jax import lax
from jax.experimental import pallas as pl
from jax.experimental.pallas import tpu as pltpu
from jax.sharding import PartitionSpec as P

NX = 256
NY = 256
NZ = 256
XB = 8


def basis_table(mode_count, length):
    mode_index = jnp.arange(mode_count, dtype=jnp.int32)
    halfway = mode_count // 2
    frequency = jnp.where(mode_index < halfway, mode_index, mode_index - halfway + 1)
    points = jnp.arange(length, dtype=jnp.int32)
    phases = frequency[:, None] * points[None, :] % length
    angles = phases.astype(jnp.float32) * (2.0 * math.pi / length)
    values_table = jnp.where((mode_index < halfway)[:, None], jnp.cos(angles), jnp.sin(angles))
    return (values_table * (1.0 / math.sqrt(length))).astype(jnp.bfloat16)


def _nt(a, b):
    return lax.dot_general(a, b, (((1,), (1,)), ((), ())), preferred_element_type=jnp.float32)


def analysis_kernel(axis, count, h_ref, g_ref, tz_ref, zc_ref, gram_ref, acc_ref, stage_ref,
                    slot_ref, local_sems, send_sems, recv_sems):
    mesh_ids = pl.DeviceIdType.MESH
    step = pl.program_id(0)
    steps = pl.num_programs(0)
    channels, xb, ny, nz = h_ref.shape
    width = xb * ny
    mz_local = slot_ref.shape[1] // count
    me = lax.axis_index(axis)

    def copies(at):
        slot = lax.rem(at, 2)
        cols = pl.ds(pl.multiple_of(at * width, width), width)
        local = pltpu.make_async_copy(
            slot_ref.at[slot, pl.ds(me * mz_local, mz_local)],
            zc_ref.at[me, :, :, cols],
            local_sems.at[at],
        )
        remote = []
        order = [k for pair in zip(range(1, count), range(count - 1, 0, -1)) for k in pair]
        for k in sorted(set(order), key=order.index):
            peer = lax.rem(me + k, count)
            remote.append(pltpu.make_async_remote_copy(
                src_ref=slot_ref.at[slot, pl.ds(peer * mz_local, mz_local)],
                dst_ref=zc_ref.at[me, :, :, cols],
                send_sem=send_sems.at[at, k],
                recv_sem=recv_sems.at[at, k],
                device_id={axis: peer},
                device_id_type=mesh_ids,
            ))
        return local, remote

    def wait_sent(at):
        local, remote = copies(at)
        local.wait()
        for copy in remote:
            copy.wait_send()

    @pl.when(step == 0)
    def _():
        acc_ref[...] = jnp.zeros_like(acc_ref)
        barrier = pltpu.get_barrier_semaphore()
        for k in range(1, count):
            peer = lax.rem(me + k, count)
            pl.semaphore_signal(barrier, inc=1, device_id={axis: peer}, device_id_type=mesh_ids)
        pl.semaphore_wait(barrier, count - 1)

    @pl.when(step >= 2)
    def _():
        wait_sent(step - 2)

    tz = tz_ref[...]
    li = jnp.tanh(h_ref[...].astype(jnp.float32)).astype(jnp.bfloat16)
    g = g_ref[...]
    zl = _nt(tz, li.reshape(channels * width, nz))
    zg = _nt(tz, g.reshape(channels * width, nz))
    for c in range(channels):
        stage_ref[:, c, :] = zl[:, c * width:(c + 1) * width]
        stage_ref[:, channels + c, :] = zg[:, c * width:(c + 1) * width]
    slot_ref[lax.rem(step, 2)] = stage_ref[...].astype(jnp.bfloat16)
    local, remote = copies(step)
    local.start()
    for copy in remote:
        copy.start()
    for x in range(xb):
        acc_ref[...] += _nt(li[:, x].reshape(channels * ny, nz), g[:, x].reshape(channels * ny, nz))

    @pl.when(step == steps - 1)
    def _():
        rows = channels * ny
        ri = lax.broadcasted_iota(jnp.int32, (rows, rows), 0)
        ci = lax.broadcasted_iota(jnp.int32, (rows, rows), 1)
        diag = jnp.where(ri % ny == ci % ny, acc_ref[...], 0.0)
        er = lax.broadcasted_iota(jnp.int32, (channels, rows), 0)
        ec = lax.broadcasted_iota(jnp.int32, (channels, rows), 1)
        gather = (ec // ny == er).astype(jnp.float32)
        part = jnp.dot(gather, diag, precision=lax.Precision.HIGHEST, preferred_element_type=jnp.float32)
        gram_ref[...] = lax.dot_general(
            part, gather, (((1,), (1,)), ((), ())), precision=lax.Precision.HIGHEST,
            preferred_element_type=jnp.float32)
        wait_sent(step - 1)
        wait_sent(step)
        for at in range(zc_ref.shape[3] // width):
            cols = pl.ds(at * width, width)
            for k in range(1, count):
                origin = lax.rem(me + count - k, count)
                pltpu.make_async_remote_copy(
                    src_ref=slot_ref.at[0, pl.ds(me * mz_local, mz_local)],
                    dst_ref=zc_ref.at[origin, :, :, cols],
                    send_sem=send_sems.at[at, k],
                    recv_sem=recv_sems.at[at, k],
                    device_id={axis: origin},
                    device_id_type=mesh_ids,
                ).wait_recv()


def analysis(hidden_pre, cotangent, table_z, axis, count):
    channels, nx, ny, nz = hidden_pre.shape
    modes = table_z.shape[0]
    steps = nx // XB
    field_spec = pl.BlockSpec((channels, XB, ny, nz), lambda i: (0, i, 0, 0))
    return pl.pallas_call(
        functools.partial(analysis_kernel, axis, count),
        grid=(steps,),
        in_specs=[field_spec, field_spec, pl.BlockSpec((modes, nz), lambda i: (0, 0))],
        out_specs=[
            pl.BlockSpec(memory_space=pl.ANY),
            pl.BlockSpec((channels, channels), lambda i: (0, 0)),
        ],
        out_shape=[
            jax.ShapeDtypeStruct(
                (count, modes // count, 2 * channels, nx * ny), jnp.bfloat16),
            jax.ShapeDtypeStruct((channels, channels), jnp.float32),
        ],
        scratch_shapes=[
            pltpu.VMEM((channels * ny, channels * ny), jnp.float32),
            pltpu.VMEM((modes, 2 * channels, XB * ny), jnp.float32),
            pltpu.VMEM((2, modes, 2 * channels, XB * ny), jnp.bfloat16),
            pltpu.SemaphoreType.DMA((steps,)),
            pltpu.SemaphoreType.DMA((steps, count)),
            pltpu.SemaphoreType.DMA((steps, count)),
        ],
        compiler_params=pltpu.CompilerParams(
            dimension_semantics=("arbitrary",), vmem_limit_bytes=60 * 1024 * 1024,
            collective_id=0, has_side_effects=True,
        ),
    )(hidden_pre, cotangent, table_z)


def synthesis_kernel(axis, count, other, others, h_ref, g_ref, xs_ref, tyt_ref, tz_ref, sw_ref,
                     gs_ref, out_ref, skip_out_ref, ks_ref, stage_ref, send_ref, recv_ref,
                     local_sems, send_sems, recv_sems, wbuf_ref, wlocal_sem, wsend_sems,
                     wrecv_sems, nbuf_ref, nlocal_sem, nsend_sems, nrecv_sems, wstage_ref):
    mesh_ids = pl.DeviceIdType.MESH
    step = pl.program_id(0)
    steps = pl.num_programs(0)
    channels, xb, ny, nz = h_ref.shape
    rows = channels * ny
    chunk = 2 * xb
    me = lax.axis_index(axis)
    me_w = lax.axis_index(other)

    def narrow_copies():
        local = pltpu.make_async_copy(gs_ref, nbuf_ref.at[me], nlocal_sem)
        remote = []
        for k in range(1, count):
            peer = lax.rem(me + k, count)
            remote.append(pltpu.make_async_remote_copy(
                src_ref=gs_ref,
                dst_ref=nbuf_ref.at[me],
                send_sem=nsend_sems.at[k],
                recv_sem=nrecv_sems.at[k],
                device_id={axis: peer},
                device_id_type=mesh_ids,
            ))
        return local, remote

    def wide_copies():
        local = pltpu.make_async_copy(wstage_ref, wbuf_ref.at[me_w], wlocal_sem)
        remote = []
        for k in range(1, others):
            peer = lax.rem(me_w + k, others)
            remote.append(pltpu.make_async_remote_copy(
                src_ref=wstage_ref,
                dst_ref=wbuf_ref.at[me_w],
                send_sem=wsend_sems.at[k],
                recv_sem=wrecv_sems.at[k],
                device_id={other: peer},
                device_id_type=mesh_ids,
            ))
        return local, remote

    def copies(at):
        part = pl.ds(pl.multiple_of(at * chunk, chunk), chunk)
        local = pltpu.make_async_copy(
            send_ref.at[me, part], recv_ref.at[me, part], local_sems.at[at])
        remote = []
        for k in range(1, count):
            peer = lax.rem(me + k, count)
            remote.append(pltpu.make_async_remote_copy(
                src_ref=send_ref.at[peer, part],
                dst_ref=recv_ref.at[me, part],
                send_sem=send_sems.at[at, k],
                recv_sem=recv_sems.at[at, k],
                device_id={axis: peer},
                device_id_type=mesh_ids,
            ))
        return local, remote

    @pl.when(step == 0)
    def _():
        barrier = pltpu.get_barrier_semaphore()
        for k in range(1, count):
            peer = lax.rem(me + k, count)
            pl.semaphore_signal(barrier, inc=1, device_id={axis: peer}, device_id_type=mesh_ids)
        for k in range(1, others):
            peer = lax.rem(me_w + k, others)
            pl.semaphore_signal(barrier, inc=1, device_id={other: peer}, device_id_type=mesh_ids)
        pl.semaphore_wait(barrier, count - 1 + others - 1)
        nlocal, nremote = narrow_copies()
        nlocal.start()
        for copy in nremote:
            copy.start()
        y_synthesis_body(xs_ref, tyt_ref, send_ref, stage_ref)
        for at in range(recv_ref.shape[1] // chunk):
            local, remote = copies(at)
            local.start()
            for copy in remote:
                copy.start()
        r = lax.broadcasted_iota(jnp.int32, (rows, channels), 0)
        k = lax.broadcasted_iota(jnp.int32, (rows, channels), 1)
        expand = (r // ny == k).astype(jnp.float32)
        spread = jnp.dot(expand, sw_ref[...].astype(jnp.float32), preferred_element_type=jnp.float32)
        kr = lax.broadcasted_iota(jnp.int32, (channels, rows), 0)
        kc = lax.broadcasted_iota(jnp.int32, (channels, rows), 1)
        expand_t = (kc // ny == kr).astype(jnp.float32)
        full = jnp.dot(spread, expand_t, preferred_element_type=jnp.float32)
        ri = lax.broadcasted_iota(jnp.int32, (rows, rows), 0)
        ci = lax.broadcasted_iota(jnp.int32, (rows, rows), 1)
        ks_ref[...] = jnp.where(ri % ny == ci % ny, full, 0.0).astype(ks_ref.dtype)

    @pl.when(step == 1)
    def _():
        nlocal, nremote = narrow_copies()
        nlocal.wait()
        for k in range(1, count):
            nremote[k - 1].wait_send()
            origin = lax.rem(me + count - k, count)
            pltpu.make_async_remote_copy(
                src_ref=gs_ref,
                dst_ref=nbuf_ref.at[origin],
                send_sem=nsend_sems.at[k],
                recv_sem=nrecv_sems.at[k],
                device_id={axis: origin},
                device_id_type=mesh_ids,
            ).wait_recv()
        total = nbuf_ref[0]
        for src in range(1, count):
            total = total + nbuf_ref[src]
        wstage_ref[...] = total
        wlocal, wremote = wide_copies()
        wlocal.start()
        for copy in wremote:
            copy.start()

    local, _ = copies(step)
    local.wait()
    part = pl.ds(pl.multiple_of(step * chunk, chunk), chunk)
    for k in range(1, count):
        origin = lax.rem(me + count - k, count)
        pltpu.make_async_remote_copy(
            src_ref=send_ref.at[me, part],
            dst_ref=recv_ref.at[origin, part],
            send_sem=send_sems.at[step, k],
            recv_sem=recv_sems.at[step, k],
            device_id={axis: origin},
            device_id_type=mesh_ids,
        ).wait_recv()

    tz = tz_ref[...]
    ks = ks_ref[...]
    ys = recv_ref[:, part, :].astype(jnp.float32)
    for x in range(xb):
        lo = ys[:, 2 * x, :]
        hi = ys[:, 2 * x + 1, :]
        lhs = jnp.concatenate([lo, hi], axis=0).T.astype(jnp.bfloat16)
        spec = jnp.dot(lhs, tz, preferred_element_type=jnp.float32)
        spec = spec.astype(jnp.bfloat16).astype(jnp.float32)
        skip = jnp.dot(ks, g_ref[:, x].reshape(channels * ny, nz), preferred_element_type=jnp.float32)
        activ = jnp.tanh(h_ref[:, x].astype(jnp.float32)).reshape(channels * ny, nz)
        grad = (spec + skip) * (1.0 - activ * activ)
        out_ref[:, x] = grad.astype(jnp.bfloat16).reshape(channels, ny, nz)

    @pl.when(step == steps - 1)
    def _():
        for at in range(recv_ref.shape[1] // chunk):
            _, remote = copies(at)
            for copy in remote:
                copy.wait_send()
        wlocal, wremote = wide_copies()
        wlocal.wait()
        for k in range(1, others):
            wremote[k - 1].wait_send()
            origin = lax.rem(me_w + others - k, others)
            pltpu.make_async_remote_copy(
                src_ref=wstage_ref,
                dst_ref=wbuf_ref.at[origin],
                send_sem=wsend_sems.at[k],
                recv_sem=wrecv_sems.at[k],
                device_id={other: origin},
                device_id_type=mesh_ids,
            ).wait_recv()
        total = wbuf_ref[0]
        for src in range(1, others):
            total = total + wbuf_ref[src]
        skip_out_ref[...] = total * (1.0 / math.sqrt(NX * NY * NZ))


def synthesis(hidden_pre, cotangent, xsynth, table_yt, table_z, skip_weight, skip_terms, axis,
              count, other, others):
    channels, nx, ny, nz = hidden_pre.shape
    modes = table_z.shape[0]
    mz_local = xsynth.shape[0]
    steps = nx // XB
    field_spec = pl.BlockSpec((channels, XB, ny, nz), lambda i: (0, i, 0, 0))
    whole = pl.BlockSpec(memory_space=pltpu.VMEM)
    lanes = channels * ny
    return pl.pallas_call(
        functools.partial(synthesis_kernel, axis, count, other, others),
        grid=(steps,),
        in_specs=[
            field_spec,
            field_spec,
            whole,
            whole,
            pl.BlockSpec((modes, nz), lambda i: (0, 0)),
            pl.BlockSpec((channels, channels), lambda i: (0, 0)),
            whole,
        ],
        out_specs=[field_spec, pl.BlockSpec((channels, channels), lambda i: (0, 0))],
        out_shape=[
            jax.ShapeDtypeStruct(hidden_pre.shape, jnp.bfloat16),
            jax.ShapeDtypeStruct((channels, channels), jnp.float32),
        ],
        scratch_shapes=[
            pltpu.VMEM((lanes, lanes), jnp.bfloat16),
            pltpu.VMEM((count * lanes // 128, nx * mz_local, 128), jnp.float32),
            pltpu.VMEM((count, nx * mz_local, lanes), jnp.bfloat16),
            pltpu.VMEM((count, nx * mz_local, lanes), jnp.bfloat16),
            pltpu.SemaphoreType.DMA((steps,)),
            pltpu.SemaphoreType.DMA((steps, count)),
            pltpu.SemaphoreType.DMA((steps, count)),
            pltpu.VMEM((others, channels, channels), jnp.float32),
            pltpu.SemaphoreType.DMA,
            pltpu.SemaphoreType.DMA((others,)),
            pltpu.SemaphoreType.DMA((others,)),
            pltpu.VMEM((count, channels, channels), jnp.float32),
            pltpu.SemaphoreType.DMA,
            pltpu.SemaphoreType.DMA((count,)),
            pltpu.SemaphoreType.DMA((count,)),
            pltpu.VMEM((channels, channels), jnp.float32),
        ],
        compiler_params=pltpu.CompilerParams(
            dimension_semantics=("arbitrary",), vmem_limit_bytes=60 * 1024 * 1024,
            collective_id=1, has_side_effects=True,
        ),
    )(hidden_pre, cotangent, xsynth, table_yt, table_z, skip_weight, skip_terms)


def y_synthesis_body(xs_ref, tyt_ref, out_ref, stage_ref):
    mz_local, channels, modes, nx = xs_ref.shape
    blocks, _, lanes = out_ref.shape
    ny = lanes // channels
    tyt = jnp.broadcast_to(tyt_ref[...][None], (channels,) + tyt_ref.shape)
    for z in range(mz_local):
        part = jnp.einsum(
            "cym,cmx->cyx", tyt, xs_ref[z], preferred_element_type=jnp.float32
        ).astype(jnp.bfloat16).astype(jnp.float32)
        for d in range(blocks):
            piece = part[:, d * ny:(d + 1) * ny, :].reshape(channels * ny, nx).T
            for q in range(lanes // 128):
                stage_ref[d * (lanes // 128) + q, pl.ds(z, nx, stride=mz_local), :] = (
                    piece[:, q * 128:(q + 1) * 128])
    for d in range(blocks):
        for q in range(lanes // 128):
            out_ref[d, :, q * 128:(q + 1) * 128] = (
                stage_ref[d * (lanes // 128) + q].astype(out_ref.dtype))


def modes_kernel(sp_ref, w_ref, gm_ref, bs_ref):
    highest = lax.Precision.HIGHEST
    channels = sp_ref.shape[1] // 2
    width = channels * channels
    sp = sp_ref[...]
    er = lax.broadcasted_iota(jnp.int32, (channels, width), 0)
    ec = lax.broadcasted_iota(jnp.int32, (channels, width), 1)
    spread = (ec // channels == er).astype(jnp.float32)
    tile = (ec % channels == er).astype(jnp.float32)
    q_rep = jnp.dot(sp[:, channels:], tile, precision=highest, preferred_element_type=jnp.float32)
    q = sp[:, channels:]
    for c in range(channels):
        gm_ref[:, c * channels:(c + 1) * channels] = sp[:, c:c + 1] * q
    weighted = w_ref[...].astype(jnp.float32) * q_rep
    back = lax.dot_general(
        weighted, spread, (((1,), (1,)), ((), ())), precision=highest,
        preferred_element_type=jnp.float32)
    bs_ref[...] = back.astype(bs_ref.dtype)


def modes_step(spectra, weights):
    rows, both = spectra.shape
    channels = both // 2
    vmem = pl.BlockSpec(memory_space=pltpu.VMEM)
    return pl.pallas_call(
        modes_kernel,
        in_specs=[vmem, vmem],
        out_specs=[vmem, vmem],
        out_shape=[
            jax.ShapeDtypeStruct((rows, channels * channels), jnp.float32),
            jax.ShapeDtypeStruct((rows, channels), jnp.bfloat16),
        ],
    )(spectra, weights)


def per_device(hidden_pre, cotangent, mode_weight, skip_weight):
    highest = lax.Precision.HIGHEST
    channels, nx, ny, nz = hidden_pre.shape
    mode_count = mode_weight.shape[2]
    n_narrow = lax.axis_size("narrow")
    n_wide = lax.axis_size("wide")
    table_x = basis_table(mode_count, NX)
    table_y = basis_table(mode_count, NY)
    table_z = basis_table(mode_count, NZ)

    zc, gram = analysis(hidden_pre, cotangent, table_z, "narrow", n_narrow)
    mz_local = mode_count // n_narrow
    zc = zc.reshape(n_narrow, mz_local, 2 * channels, nx, ny)
    ycoeffs = jnp.einsum(
        "smcxl,nsl->mcnx", zc, table_y.reshape(mode_count, n_narrow, ny),
        preferred_element_type=jnp.float32,
    ).astype(jnp.bfloat16)
    ycoeffs = lax.all_to_all(ycoeffs, "wide", split_axis=2, concat_axis=3, tiled=True)
    spectra = jnp.einsum("zcyx,kx->zykc", ycoeffs, table_x, preferred_element_type=jnp.float32)
    z_local, y_local = (spectra.shape[0], spectra.shape[1])
    grad_modes, back_spec = modes_step(
        spectra.reshape(z_local * y_local * mode_count, 2 * channels),
        mode_weight.reshape(z_local * y_local * mode_count, channels * channels),
    )
    grad_modes = grad_modes.reshape(z_local, y_local, mode_count, channels * channels)
    back_spec = jnp.transpose(
        back_spec.reshape(z_local, y_local, mode_count, channels), (0, 3, 1, 2)
    )
    xsynth = jnp.einsum(
        "zcyk,kx->zcyx", back_spec, table_x, preferred_element_type=jnp.float32
    ).astype(jnp.bfloat16)
    xsynth = lax.all_to_all(xsynth, "wide", split_axis=3, concat_axis=2, tiled=True)
    table_zp = jnp.transpose(table_z.reshape(n_narrow, mz_local, nz), (1, 0, 2)).reshape(mode_count, nz)
    grad_hidden, grad_skip = synthesis(
        hidden_pre, cotangent, xsynth, jnp.transpose(table_y), table_zp, skip_weight, gram,
        "narrow", n_narrow, "wide", n_wide)

    return (grad_hidden, grad_modes, grad_skip)


def solution(mesh):
    in_specs = (
        P(None, "wide", "narrow", None),
        P(None, "wide", "narrow", None),
        P("narrow", "wide", None, None),
        P(),
    )
    out_specs = (P(None, "wide", "narrow", None), P("narrow", "wide", None, None), P())
    return jax.shard_map(
        per_device, mesh=mesh, in_specs=in_specs, out_specs=out_specs, check_vma=False
    )
```

```python
import functools
import math

import jax
import jax.numpy as jnp
from jax import lax
from jax.experimental import pallas as pl
from jax.experimental.pallas import tpu as pltpu
from jax.sharding import PartitionSpec as P

NX = 256
NY = 256
NZ = 256
XB = 8


def basis_table(mode_count, length):
    mode_index = jnp.arange(mode_count, dtype=jnp.int32)
    halfway = mode_count // 2
    frequency = jnp.where(mode_index < halfway, mode_index, mode_index - halfway + 1)
    points = jnp.arange(length, dtype=jnp.int32)
    phases = frequency[:, None] * points[None, :] % length
    angles = phases.astype(jnp.float32) * (2.0 * math.pi / length)
    values_table = jnp.where((mode_index < halfway)[:, None], jnp.cos(angles), jnp.sin(angles))
    return (values_table * (1.0 / math.sqrt(length))).astype(jnp.bfloat16)


def _nt(a, b):
    return lax.dot_general(a, b, (((1,), (1,)), ((), ())), preferred_element_type=jnp.float32)


def analysis_kernel(axis, count, h_ref, g_ref, tz_ref, zc_ref, gram_ref, acc_ref, stage_ref,
                    slot_ref, local_sems, send_sems, recv_sems):
    mesh_ids = pl.DeviceIdType.MESH
    step = pl.program_id(0)
    steps = pl.num_programs(0)
    channels, xb, ny, nz = h_ref.shape
    width = xb * ny
    mz_local = slot_ref.shape[1] // count
    me = lax.axis_index(axis)

    def copies(at):
        slot = lax.rem(at, 2)
        cols = pl.ds(pl.multiple_of(at * width, width), width)
        local = pltpu.make_async_copy(
            slot_ref.at[slot, pl.ds(me * mz_local, mz_local)],
            zc_ref.at[me, :, :, cols],
            local_sems.at[at],
        )
        remote = []
        order = [k for pair in zip(range(1, count), range(count - 1, 0, -1)) for k in pair]
        for k in sorted(set(order), key=order.index):
            peer = lax.rem(me + k, count)
            remote.append(pltpu.make_async_remote_copy(
                src_ref=slot_ref.at[slot, pl.ds(peer * mz_local, mz_local)],
                dst_ref=zc_ref.at[me, :, :, cols],
                send_sem=send_sems.at[at, k],
                recv_sem=recv_sems.at[at, k],
                device_id={axis: peer},
                device_id_type=mesh_ids,
            ))
        return local, remote

    def wait_sent(at):
        local, remote = copies(at)
        local.wait()
        for copy in remote:
            copy.wait_send()

    @pl.when(step == 0)
    def _():
        acc_ref[...] = jnp.zeros_like(acc_ref)
        barrier = pltpu.get_barrier_semaphore()
        for k in range(1, count):
            peer = lax.rem(me + k, count)
            pl.semaphore_signal(barrier, inc=1, device_id={axis: peer}, device_id_type=mesh_ids)
        pl.semaphore_wait(barrier, count - 1)

    @pl.when(step >= 2)
    def _():
        wait_sent(step - 2)

    tz = tz_ref[...]
    li = jnp.tanh(h_ref[...].astype(jnp.float32)).astype(jnp.bfloat16)
    g = g_ref[...]
    zl = _nt(tz, li.reshape(channels * width, nz))
    zg = _nt(tz, g.reshape(channels * width, nz))
    for c in range(channels):
        stage_ref[:, c, :] = zl[:, c * width:(c + 1) * width]
        stage_ref[:, channels + c, :] = zg[:, c * width:(c + 1) * width]
    slot_ref[lax.rem(step, 2)] = stage_ref[...].astype(jnp.bfloat16)
    local, remote = copies(step)
    local.start()
    for copy in remote:
        copy.start()
    for x in range(xb):
        acc_ref[...] += _nt(li[:, x].reshape(channels * ny, nz), g[:, x].reshape(channels * ny, nz))

    @pl.when(step == steps - 1)
    def _():
        rows = channels * ny
        ri = lax.broadcasted_iota(jnp.int32, (rows, rows), 0)
        ci = lax.broadcasted_iota(jnp.int32, (rows, rows), 1)
        diag = jnp.where(ri % ny == ci % ny, acc_ref[...], 0.0)
        er = lax.broadcasted_iota(jnp.int32, (channels, rows), 0)
        ec = lax.broadcasted_iota(jnp.int32, (channels, rows), 1)
        gather = (ec // ny == er).astype(jnp.float32)
        part = jnp.dot(gather, diag, precision=lax.Precision.HIGHEST, preferred_element_type=jnp.float32)
        gram_ref[...] = lax.dot_general(
            part, gather, (((1,), (1,)), ((), ())), precision=lax.Precision.HIGHEST,
            preferred_element_type=jnp.float32)
        wait_sent(step - 1)
        wait_sent(step)
        for at in range(zc_ref.shape[3] // width):
            cols = pl.ds(at * width, width)
            for k in range(1, count):
                origin = lax.rem(me + count - k, count)
                pltpu.make_async_remote_copy(
                    src_ref=slot_ref.at[0, pl.ds(me * mz_local, mz_local)],
                    dst_ref=zc_ref.at[origin, :, :, cols],
                    send_sem=send_sems.at[at, k],
                    recv_sem=recv_sems.at[at, k],
                    device_id={axis: origin},
                    device_id_type=mesh_ids,
                ).wait_recv()


def analysis(hidden_pre, cotangent, table_z, axis, count):
    channels, nx, ny, nz = hidden_pre.shape
    modes = table_z.shape[0]
    steps = nx // XB
    field_spec = pl.BlockSpec((channels, XB, ny, nz), lambda i: (0, i, 0, 0))
    return pl.pallas_call(
        functools.partial(analysis_kernel, axis, count),
        grid=(steps,),
        in_specs=[field_spec, field_spec, pl.BlockSpec((modes, nz), lambda i: (0, 0))],
        out_specs=[
            pl.BlockSpec(memory_space=pl.ANY),
            pl.BlockSpec((channels, channels), lambda i: (0, 0)),
        ],
        out_shape=[
            jax.ShapeDtypeStruct(
                (count, modes // count, 2 * channels, nx * ny), jnp.bfloat16),
            jax.ShapeDtypeStruct((channels, channels), jnp.float32),
        ],
        scratch_shapes=[
            pltpu.VMEM((channels * ny, channels * ny), jnp.float32),
            pltpu.VMEM((modes, 2 * channels, XB * ny), jnp.float32),
            pltpu.VMEM((2, modes, 2 * channels, XB * ny), jnp.bfloat16),
            pltpu.SemaphoreType.DMA((steps,)),
            pltpu.SemaphoreType.DMA((steps, count)),
            pltpu.SemaphoreType.DMA((steps, count)),
        ],
        compiler_params=pltpu.CompilerParams(
            dimension_semantics=("arbitrary",), vmem_limit_bytes=60 * 1024 * 1024,
            collective_id=0, has_side_effects=True,
        ),
    )(hidden_pre, cotangent, table_z)


def synthesis_kernel(axis, count, other, others, h_ref, g_ref, xs_ref, tyt_ref, tz_ref, sw_ref,
                     gs_ref, out_ref, skip_out_ref, ks_ref, stage_ref, send_ref, recv_ref,
                     local_sems, send_sems, recv_sems, wbuf_ref, wlocal_sem, wsend_sems,
                     wrecv_sems, nbuf_ref, nlocal_sem, nsend_sems, nrecv_sems, wstage_ref):
    mesh_ids = pl.DeviceIdType.MESH
    step = pl.program_id(0)
    steps = pl.num_programs(0)
    channels, xb, ny, nz = h_ref.shape
    rows = channels * ny
    chunk = 2 * xb
    me = lax.axis_index(axis)
    me_w = lax.axis_index(other)

    def narrow_copies():
        local = pltpu.make_async_copy(gs_ref, nbuf_ref.at[me], nlocal_sem)
        remote = []
        for k in range(1, count):
            peer = lax.rem(me + k, count)
            remote.append(pltpu.make_async_remote_copy(
                src_ref=gs_ref,
                dst_ref=nbuf_ref.at[me],
                send_sem=nsend_sems.at[k],
                recv_sem=nrecv_sems.at[k],
                device_id={axis: peer},
                device_id_type=mesh_ids,
            ))
        return local, remote

    def wide_copies():
        local = pltpu.make_async_copy(wstage_ref, wbuf_ref.at[me_w], wlocal_sem)
        remote = []
        for k in range(1, others):
            peer = lax.rem(me_w + k, others)
            remote.append(pltpu.make_async_remote_copy(
                src_ref=wstage_ref,
                dst_ref=wbuf_ref.at[me_w],
                send_sem=wsend_sems.at[k],
                recv_sem=wrecv_sems.at[k],
                device_id={other: peer},
                device_id_type=mesh_ids,
            ))
        return local, remote

    def copies(at):
        part = pl.ds(pl.multiple_of(at * chunk, chunk), chunk)
        local = pltpu.make_async_copy(
            send_ref.at[me, part], recv_ref.at[me, part], local_sems.at[at])
        remote = []
        order = [k for pair in zip(range(1, count), range(count - 1, 0, -1)) for k in pair]
        for k in sorted(set(order), key=order.index):
            peer = lax.rem(me + k, count)
            remote.append(pltpu.make_async_remote_copy(
                src_ref=send_ref.at[peer, part],
                dst_ref=recv_ref.at[me, part],
                send_sem=send_sems.at[at, k],
                recv_sem=recv_sems.at[at, k],
                device_id={axis: peer},
                device_id_type=mesh_ids,
            ))
        return local, remote

    @pl.when(step == 0)
    def _():
        barrier = pltpu.get_barrier_semaphore()
        for k in range(1, count):
            peer = lax.rem(me + k, count)
            pl.semaphore_signal(barrier, inc=1, device_id={axis: peer}, device_id_type=mesh_ids)
        for k in range(1, others):
            peer = lax.rem(me_w + k, others)
            pl.semaphore_signal(barrier, inc=1, device_id={other: peer}, device_id_type=mesh_ids)
        pl.semaphore_wait(barrier, count - 1 + others - 1)
        nlocal, nremote = narrow_copies()
        nlocal.start()
        for copy in nremote:
            copy.start()
        y_synthesis_body(xs_ref, tyt_ref, send_ref, stage_ref)
        for at in range(recv_ref.shape[1] // chunk):
            local, remote = copies(at)
            local.start()
            for copy in remote:
                copy.start()
        r = lax.broadcasted_iota(jnp.int32, (rows, channels), 0)
        k = lax.broadcasted_iota(jnp.int32, (rows, channels), 1)
        expand = (r // ny == k).astype(jnp.float32)
        spread = jnp.dot(expand, sw_ref[...].astype(jnp.float32), preferred_element_type=jnp.float32)
        kr = lax.broadcasted_iota(jnp.int32, (channels, rows), 0)
        kc = lax.broadcasted_iota(jnp.int32, (channels, rows), 1)
        expand_t = (kc // ny == kr).astype(jnp.float32)
        full = jnp.dot(spread, expand_t, preferred_element_type=jnp.float32)
        ri = lax.broadcasted_iota(jnp.int32, (rows, rows), 0)
        ci = lax.broadcasted_iota(jnp.int32, (rows, rows), 1)
        ks_ref[...] = jnp.where(ri % ny == ci % ny, full, 0.0).astype(ks_ref.dtype)

    @pl.when(step == 1)
    def _():
        nlocal, nremote = narrow_copies()
        nlocal.wait()
        for k in range(1, count):
            nremote[k - 1].wait_send()
            origin = lax.rem(me + count - k, count)
            pltpu.make_async_remote_copy(
                src_ref=gs_ref,
                dst_ref=nbuf_ref.at[origin],
                send_sem=nsend_sems.at[k],
                recv_sem=nrecv_sems.at[k],
                device_id={axis: origin},
                device_id_type=mesh_ids,
            ).wait_recv()
        total = nbuf_ref[0]
        for src in range(1, count):
            total = total + nbuf_ref[src]
        wstage_ref[...] = total
        wlocal, wremote = wide_copies()
        wlocal.start()
        for copy in wremote:
            copy.start()

    local, _ = copies(step)
    local.wait()
    part = pl.ds(pl.multiple_of(step * chunk, chunk), chunk)
    for k in range(1, count):
        origin = lax.rem(me + count - k, count)
        pltpu.make_async_remote_copy(
            src_ref=send_ref.at[me, part],
            dst_ref=recv_ref.at[origin, part],
            send_sem=send_sems.at[step, k],
            recv_sem=recv_sems.at[step, k],
            device_id={axis: origin},
            device_id_type=mesh_ids,
        ).wait_recv()

    tz = tz_ref[...]
    ks = ks_ref[...]
    ys = recv_ref[:, part, :].astype(jnp.float32)
    for x in range(xb):
        lo = ys[:, 2 * x, :]
        hi = ys[:, 2 * x + 1, :]
        lhs = jnp.concatenate([lo, hi], axis=0).T.astype(jnp.bfloat16)
        spec = jnp.dot(lhs, tz, preferred_element_type=jnp.float32)
        spec = spec.astype(jnp.bfloat16).astype(jnp.float32)
        skip = jnp.dot(ks, g_ref[:, x].reshape(channels * ny, nz), preferred_element_type=jnp.float32)
        activ = jnp.tanh(h_ref[:, x].astype(jnp.float32)).reshape(channels * ny, nz)
        grad = (spec + skip) * (1.0 - activ * activ)
        out_ref[:, x] = grad.astype(jnp.bfloat16).reshape(channels, ny, nz)

    @pl.when(step == steps - 1)
    def _():
        for at in range(recv_ref.shape[1] // chunk):
            _, remote = copies(at)
            for copy in remote:
                copy.wait_send()
        wlocal, wremote = wide_copies()
        wlocal.wait()
        for k in range(1, others):
            wremote[k - 1].wait_send()
            origin = lax.rem(me_w + others - k, others)
            pltpu.make_async_remote_copy(
                src_ref=wstage_ref,
                dst_ref=wbuf_ref.at[origin],
                send_sem=wsend_sems.at[k],
                recv_sem=wrecv_sems.at[k],
                device_id={other: origin},
                device_id_type=mesh_ids,
            ).wait_recv()
        total = wbuf_ref[0]
        for src in range(1, others):
            total = total + wbuf_ref[src]
        skip_out_ref[...] = total * (1.0 / math.sqrt(NX * NY * NZ))


def synthesis(hidden_pre, cotangent, xsynth, table_yt, table_z, skip_weight, skip_terms, axis,
              count, other, others):
    channels, nx, ny, nz = hidden_pre.shape
    modes = table_z.shape[0]
    mz_local = xsynth.shape[0]
    steps = nx // XB
    field_spec = pl.BlockSpec((channels, XB, ny, nz), lambda i: (0, i, 0, 0))
    whole = pl.BlockSpec(memory_space=pltpu.VMEM)
    lanes = channels * ny
    return pl.pallas_call(
        functools.partial(synthesis_kernel, axis, count, other, others),
        grid=(steps,),
        in_specs=[
            field_spec,
            field_spec,
            whole,
            whole,
            pl.BlockSpec((modes, nz), lambda i: (0, 0)),
            pl.BlockSpec((channels, channels), lambda i: (0, 0)),
            whole,
        ],
        out_specs=[field_spec, pl.BlockSpec((channels, channels), lambda i: (0, 0))],
        out_shape=[
            jax.ShapeDtypeStruct(hidden_pre.shape, jnp.bfloat16),
            jax.ShapeDtypeStruct((channels, channels), jnp.float32),
        ],
        scratch_shapes=[
            pltpu.VMEM((lanes, lanes), jnp.bfloat16),
            pltpu.VMEM((count * lanes // 128, nx * mz_local, 128), jnp.float32),
            pltpu.VMEM((count, nx * mz_local, lanes), jnp.bfloat16),
            pltpu.VMEM((count, nx * mz_local, lanes), jnp.bfloat16),
            pltpu.SemaphoreType.DMA((steps,)),
            pltpu.SemaphoreType.DMA((steps, count)),
            pltpu.SemaphoreType.DMA((steps, count)),
            pltpu.VMEM((others, channels, channels), jnp.float32),
            pltpu.SemaphoreType.DMA,
            pltpu.SemaphoreType.DMA((others,)),
            pltpu.SemaphoreType.DMA((others,)),
            pltpu.VMEM((count, channels, channels), jnp.float32),
            pltpu.SemaphoreType.DMA,
            pltpu.SemaphoreType.DMA((count,)),
            pltpu.SemaphoreType.DMA((count,)),
            pltpu.VMEM((channels, channels), jnp.float32),
        ],
        compiler_params=pltpu.CompilerParams(
            dimension_semantics=("arbitrary",), vmem_limit_bytes=60 * 1024 * 1024,
            collective_id=1, has_side_effects=True,
        ),
    )(hidden_pre, cotangent, xsynth, table_yt, table_z, skip_weight, skip_terms)


def y_synthesis_body(xs_ref, tyt_ref, out_ref, stage_ref):
    mz_local, channels, modes, nx = xs_ref.shape
    blocks, _, lanes = out_ref.shape
    ny = lanes // channels
    tyt = jnp.broadcast_to(tyt_ref[...][None], (channels,) + tyt_ref.shape)
    for z in range(mz_local):
        part = jnp.einsum(
            "cym,cmx->cyx", tyt, xs_ref[z], preferred_element_type=jnp.float32
        ).astype(jnp.bfloat16).astype(jnp.float32)
        for d in range(blocks):
            piece = part[:, d * ny:(d + 1) * ny, :].reshape(channels * ny, nx).T
            for q in range(lanes // 128):
                stage_ref[d * (lanes // 128) + q, pl.ds(z, nx, stride=mz_local), :] = (
                    piece[:, q * 128:(q + 1) * 128])
    for d in range(blocks):
        for q in range(lanes // 128):
            out_ref[d, :, q * 128:(q + 1) * 128] = (
                stage_ref[d * (lanes // 128) + q].astype(out_ref.dtype))


def modes_kernel(sp_ref, w_ref, gm_ref, bs_ref):
    highest = lax.Precision.HIGHEST
    channels = sp_ref.shape[1] // 2
    width = channels * channels
    sp = sp_ref[...]
    er = lax.broadcasted_iota(jnp.int32, (channels, width), 0)
    ec = lax.broadcasted_iota(jnp.int32, (channels, width), 1)
    spread = (ec // channels == er).astype(jnp.float32)
    tile = (ec % channels == er).astype(jnp.float32)
    q_rep = jnp.dot(sp[:, channels:], tile, precision=highest, preferred_element_type=jnp.float32)
    q = sp[:, channels:]
    for c in range(channels):
        gm_ref[:, c * channels:(c + 1) * channels] = sp[:, c:c + 1] * q
    weighted = w_ref[...].astype(jnp.float32) * q_rep
    back = lax.dot_general(
        weighted, spread, (((1,), (1,)), ((), ())), precision=highest,
        preferred_element_type=jnp.float32)
    bs_ref[...] = back.astype(bs_ref.dtype)


def modes_step(spectra, weights):
    rows, both = spectra.shape
    channels = both // 2
    vmem = pl.BlockSpec(memory_space=pltpu.VMEM)
    return pl.pallas_call(
        modes_kernel,
        in_specs=[vmem, vmem],
        out_specs=[vmem, vmem],
        out_shape=[
            jax.ShapeDtypeStruct((rows, channels * channels), jnp.float32),
            jax.ShapeDtypeStruct((rows, channels), jnp.bfloat16),
        ],
    )(spectra, weights)


def per_device(hidden_pre, cotangent, mode_weight, skip_weight):
    highest = lax.Precision.HIGHEST
    channels, nx, ny, nz = hidden_pre.shape
    mode_count = mode_weight.shape[2]
    n_narrow = lax.axis_size("narrow")
    n_wide = lax.axis_size("wide")
    table_x = basis_table(mode_count, NX)
    table_y = basis_table(mode_count, NY)
    table_z = basis_table(mode_count, NZ)

    zc, gram = analysis(hidden_pre, cotangent, table_z, "narrow", n_narrow)
    mz_local = mode_count // n_narrow
    zc = zc.reshape(n_narrow, mz_local, 2 * channels, nx, ny)
    ycoeffs = jnp.einsum(
        "smcxl,nsl->mcnx", zc, table_y.reshape(mode_count, n_narrow, ny),
        preferred_element_type=jnp.float32,
    ).astype(jnp.bfloat16)
    ycoeffs = lax.all_to_all(ycoeffs, "wide", split_axis=2, concat_axis=3, tiled=True)
    spectra = jnp.einsum("zcyx,kx->zykc", ycoeffs, table_x, preferred_element_type=jnp.float32)
    z_local, y_local = (spectra.shape[0], spectra.shape[1])
    grad_modes, back_spec = modes_step(
        spectra.reshape(z_local * y_local * mode_count, 2 * channels),
        mode_weight.reshape(z_local * y_local * mode_count, channels * channels),
    )
    grad_modes = grad_modes.reshape(z_local, y_local, mode_count, channels * channels)
    back_spec = jnp.transpose(
        back_spec.reshape(z_local, y_local, mode_count, channels), (0, 3, 1, 2)
    )
    xsynth = jnp.einsum(
        "zcyk,kx->zcyx", back_spec, table_x, preferred_element_type=jnp.float32
    ).astype(jnp.bfloat16)
    xsynth = lax.all_to_all(xsynth, "wide", split_axis=3, concat_axis=2, tiled=True)
    table_zp = jnp.transpose(table_z.reshape(n_narrow, mz_local, nz), (1, 0, 2)).reshape(mode_count, nz)
    grad_hidden, grad_skip = synthesis(
        hidden_pre, cotangent, xsynth, jnp.transpose(table_y), table_zp, skip_weight, gram,
        "narrow", n_narrow, "wide", n_wide)

    return (grad_hidden, grad_modes, grad_skip)


def solution(mesh):
    in_specs = (
        P(None, "wide", "narrow", None),
        P(None, "wide", "narrow", None),
        P("narrow", "wide", None, None),
        P(),
    )
    out_specs = (P(None, "wide", "narrow", None), P("narrow", "wide", None, None), P())
    return jax.shard_map(
        per_device, mesh=mesh, in_specs=in_specs, out_specs=out_specs, check_vma=False
    )
```

```python
import functools
import math

import jax
import jax.numpy as jnp
from jax import lax
from jax.experimental import pallas as pl
from jax.experimental.pallas import tpu as pltpu
from jax.sharding import PartitionSpec as P

NX = 256
NY = 256
NZ = 256
XB = 8


def basis_table(mode_count, length):
    mode_index = jnp.arange(mode_count, dtype=jnp.int32)
    halfway = mode_count // 2
    frequency = jnp.where(mode_index < halfway, mode_index, mode_index - halfway + 1)
    points = jnp.arange(length, dtype=jnp.int32)
    phases = frequency[:, None] * points[None, :] % length
    angles = phases.astype(jnp.float32) * (2.0 * math.pi / length)
    values_table = jnp.where((mode_index < halfway)[:, None], jnp.cos(angles), jnp.sin(angles))
    return (values_table * (1.0 / math.sqrt(length))).astype(jnp.bfloat16)


def _nt(a, b):
    return lax.dot_general(a, b, (((1,), (1,)), ((), ())), preferred_element_type=jnp.float32)


def analysis_kernel(axis, count, h_ref, g_ref, tz_ref, zc_ref, gram_ref, acc_ref, stage_ref,
                    slot_ref, local_sems, send_sems, recv_sems):
    mesh_ids = pl.DeviceIdType.MESH
    step = pl.program_id(0)
    steps = pl.num_programs(0)
    channels, xb, ny, nz = h_ref.shape
    width = xb * ny
    mz_local = slot_ref.shape[1] // count
    me = lax.axis_index(axis)

    def copies(at):
        slot = lax.rem(at, 2)
        cols = pl.ds(pl.multiple_of(at * width, width), width)
        local = pltpu.make_async_copy(
            slot_ref.at[slot, pl.ds(me * mz_local, mz_local)],
            zc_ref.at[me, :, :, cols],
            local_sems.at[at],
        )
        remote = []
        order = [k for pair in zip(range(1, count), range(count - 1, 0, -1)) for k in pair]
        for k in list(reversed(sorted(set(order), key=order.index))):
            peer = lax.rem(me + k, count)
            remote.append(pltpu.make_async_remote_copy(
                src_ref=slot_ref.at[slot, pl.ds(peer * mz_local, mz_local)],
                dst_ref=zc_ref.at[me, :, :, cols],
                send_sem=send_sems.at[at, k],
                recv_sem=recv_sems.at[at, k],
                device_id={axis: peer},
                device_id_type=mesh_ids,
            ))
        return local, remote

    def wait_sent(at):
        local, remote = copies(at)
        local.wait()
        for copy in remote:
            copy.wait_send()

    @pl.when(step == 0)
    def _():
        acc_ref[...] = jnp.zeros_like(acc_ref)
        barrier = pltpu.get_barrier_semaphore()
        for k in range(1, count):
            peer = lax.rem(me + k, count)
            pl.semaphore_signal(barrier, inc=1, device_id={axis: peer}, device_id_type=mesh_ids)
        pl.semaphore_wait(barrier, count - 1)

    @pl.when(step >= 2)
    def _():
        wait_sent(step - 2)

    tz = tz_ref[...]
    li = jnp.tanh(h_ref[...].astype(jnp.float32)).astype(jnp.bfloat16)
    g = g_ref[...]
    zl = _nt(tz, li.reshape(channels * width, nz))
    zg = _nt(tz, g.reshape(channels * width, nz))
    for c in range(channels):
        stage_ref[:, c, :] = zl[:, c * width:(c + 1) * width]
        stage_ref[:, channels + c, :] = zg[:, c * width:(c + 1) * width]
    slot_ref[lax.rem(step, 2)] = stage_ref[...].astype(jnp.bfloat16)
    local, remote = copies(step)
    local.start()
    for copy in remote:
        copy.start()
    for x in range(xb):
        acc_ref[...] += _nt(li[:, x].reshape(channels * ny, nz), g[:, x].reshape(channels * ny, nz))

    @pl.when(step == steps - 1)
    def _():
        rows = channels * ny
        ri = lax.broadcasted_iota(jnp.int32, (rows, rows), 0)
        ci = lax.broadcasted_iota(jnp.int32, (rows, rows), 1)
        diag = jnp.where(ri % ny == ci % ny, acc_ref[...], 0.0)
        er = lax.broadcasted_iota(jnp.int32, (channels, rows), 0)
        ec = lax.broadcasted_iota(jnp.int32, (channels, rows), 1)
        gather = (ec // ny == er).astype(jnp.float32)
        part = jnp.dot(gather, diag, precision=lax.Precision.HIGHEST, preferred_element_type=jnp.float32)
        gram_ref[...] = lax.dot_general(
            part, gather, (((1,), (1,)), ((), ())), precision=lax.Precision.HIGHEST,
            preferred_element_type=jnp.float32)
        wait_sent(step - 1)
        wait_sent(step)
        for at in range(zc_ref.shape[3] // width):
            cols = pl.ds(at * width, width)
            for k in range(1, count):
                origin = lax.rem(me + count - k, count)
                pltpu.make_async_remote_copy(
                    src_ref=slot_ref.at[0, pl.ds(me * mz_local, mz_local)],
                    dst_ref=zc_ref.at[origin, :, :, cols],
                    send_sem=send_sems.at[at, k],
                    recv_sem=recv_sems.at[at, k],
                    device_id={axis: origin},
                    device_id_type=mesh_ids,
                ).wait_recv()


def analysis(hidden_pre, cotangent, table_z, axis, count):
    channels, nx, ny, nz = hidden_pre.shape
    modes = table_z.shape[0]
    steps = nx // XB
    field_spec = pl.BlockSpec((channels, XB, ny, nz), lambda i: (0, i, 0, 0))
    return pl.pallas_call(
        functools.partial(analysis_kernel, axis, count),
        grid=(steps,),
        in_specs=[field_spec, field_spec, pl.BlockSpec((modes, nz), lambda i: (0, 0))],
        out_specs=[
            pl.BlockSpec(memory_space=pl.ANY),
            pl.BlockSpec((channels, channels), lambda i: (0, 0)),
        ],
        out_shape=[
            jax.ShapeDtypeStruct(
                (count, modes // count, 2 * channels, nx * ny), jnp.bfloat16),
            jax.ShapeDtypeStruct((channels, channels), jnp.float32),
        ],
        scratch_shapes=[
            pltpu.VMEM((channels * ny, channels * ny), jnp.float32),
            pltpu.VMEM((modes, 2 * channels, XB * ny), jnp.float32),
            pltpu.VMEM((2, modes, 2 * channels, XB * ny), jnp.bfloat16),
            pltpu.SemaphoreType.DMA((steps,)),
            pltpu.SemaphoreType.DMA((steps, count)),
            pltpu.SemaphoreType.DMA((steps, count)),
        ],
        compiler_params=pltpu.CompilerParams(
            dimension_semantics=("arbitrary",), vmem_limit_bytes=60 * 1024 * 1024,
            collective_id=0, has_side_effects=True,
        ),
    )(hidden_pre, cotangent, table_z)


def synthesis_kernel(axis, count, other, others, h_ref, g_ref, xs_ref, tyt_ref, tz_ref, sw_ref,
                     gs_ref, out_ref, skip_out_ref, ks_ref, stage_ref, send_ref, recv_ref,
                     local_sems, send_sems, recv_sems, wbuf_ref, wlocal_sem, wsend_sems,
                     wrecv_sems, nbuf_ref, nlocal_sem, nsend_sems, nrecv_sems, wstage_ref):
    mesh_ids = pl.DeviceIdType.MESH
    step = pl.program_id(0)
    steps = pl.num_programs(0)
    channels, xb, ny, nz = h_ref.shape
    rows = channels * ny
    chunk = 2 * xb
    me = lax.axis_index(axis)
    me_w = lax.axis_index(other)

    def narrow_copies():
        local = pltpu.make_async_copy(gs_ref, nbuf_ref.at[me], nlocal_sem)
        remote = []
        for k in range(1, count):
            peer = lax.rem(me + k, count)
            remote.append(pltpu.make_async_remote_copy(
                src_ref=gs_ref,
                dst_ref=nbuf_ref.at[me],
                send_sem=nsend_sems.at[k],
                recv_sem=nrecv_sems.at[k],
                device_id={axis: peer},
                device_id_type=mesh_ids,
            ))
        return local, remote

    def wide_copies():
        local = pltpu.make_async_copy(wstage_ref, wbuf_ref.at[me_w], wlocal_sem)
        remote = []
        for k in range(1, others):
            peer = lax.rem(me_w + k, others)
            remote.append(pltpu.make_async_remote_copy(
                src_ref=wstage_ref,
                dst_ref=wbuf_ref.at[me_w],
                send_sem=wsend_sems.at[k],
                recv_sem=wrecv_sems.at[k],
                device_id={other: peer},
                device_id_type=mesh_ids,
            ))
        return local, remote

    def copies(at):
        part = pl.ds(pl.multiple_of(at * chunk, chunk), chunk)
        local = pltpu.make_async_copy(
            send_ref.at[me, part], recv_ref.at[me, part], local_sems.at[at])
        remote = []
        for k in range(1, count):
            peer = lax.rem(me + k, count)
            remote.append(pltpu.make_async_remote_copy(
                src_ref=send_ref.at[peer, part],
                dst_ref=recv_ref.at[me, part],
                send_sem=send_sems.at[at, k],
                recv_sem=recv_sems.at[at, k],
                device_id={axis: peer},
                device_id_type=mesh_ids,
            ))
        return local, remote

    @pl.when(step == 0)
    def _():
        barrier = pltpu.get_barrier_semaphore()
        for k in range(1, count):
            peer = lax.rem(me + k, count)
            pl.semaphore_signal(barrier, inc=1, device_id={axis: peer}, device_id_type=mesh_ids)
        for k in range(1, others):
            peer = lax.rem(me_w + k, others)
            pl.semaphore_signal(barrier, inc=1, device_id={other: peer}, device_id_type=mesh_ids)
        pl.semaphore_wait(barrier, count - 1 + others - 1)
        nlocal, nremote = narrow_copies()
        nlocal.start()
        for copy in nremote:
            copy.start()
        y_synthesis_body(xs_ref, tyt_ref, send_ref, stage_ref)
        for at in range(recv_ref.shape[1] // chunk):
            local, remote = copies(at)
            local.start()
            for copy in remote:
                copy.start()
        r = lax.broadcasted_iota(jnp.int32, (rows, channels), 0)
        k = lax.broadcasted_iota(jnp.int32, (rows, channels), 1)
        expand = (r // ny == k).astype(jnp.float32)
        spread = jnp.dot(expand, sw_ref[...].astype(jnp.float32), preferred_element_type=jnp.float32)
        kr = lax.broadcasted_iota(jnp.int32, (channels, rows), 0)
        kc = lax.broadcasted_iota(jnp.int32, (channels, rows), 1)
        expand_t = (kc // ny == kr).astype(jnp.float32)
        full = jnp.dot(spread, expand_t, preferred_element_type=jnp.float32)
        ri = lax.broadcasted_iota(jnp.int32, (rows, rows), 0)
        ci = lax.broadcasted_iota(jnp.int32, (rows, rows), 1)
        ks_ref[...] = jnp.where(ri % ny == ci % ny, full, 0.0).astype(ks_ref.dtype)

    @pl.when(step == 1)
    def _():
        nlocal, nremote = narrow_copies()
        nlocal.wait()
        for k in range(1, count):
            nremote[k - 1].wait_send()
            origin = lax.rem(me + count - k, count)
            pltpu.make_async_remote_copy(
                src_ref=gs_ref,
                dst_ref=nbuf_ref.at[origin],
                send_sem=nsend_sems.at[k],
                recv_sem=nrecv_sems.at[k],
                device_id={axis: origin},
                device_id_type=mesh_ids,
            ).wait_recv()
        total = nbuf_ref[0]
        for src in range(1, count):
            total = total + nbuf_ref[src]
        wstage_ref[...] = total
        wlocal, wremote = wide_copies()
        wlocal.start()
        for copy in wremote:
            copy.start()

    local, _ = copies(step)
    local.wait()
    part = pl.ds(pl.multiple_of(step * chunk, chunk), chunk)
    for k in range(1, count):
        origin = lax.rem(me + count - k, count)
        pltpu.make_async_remote_copy(
            src_ref=send_ref.at[me, part],
            dst_ref=recv_ref.at[origin, part],
            send_sem=send_sems.at[step, k],
            recv_sem=recv_sems.at[step, k],
            device_id={axis: origin},
            device_id_type=mesh_ids,
        ).wait_recv()

    tz = tz_ref[...]
    ks = ks_ref[...]
    ys = recv_ref[:, part, :].astype(jnp.float32)
    for x in range(xb):
        lo = ys[:, 2 * x, :]
        hi = ys[:, 2 * x + 1, :]
        lhs = jnp.concatenate([lo, hi], axis=0).T.astype(jnp.bfloat16)
        spec = jnp.dot(lhs, tz, preferred_element_type=jnp.float32)
        spec = spec.astype(jnp.bfloat16).astype(jnp.float32)
        skip = jnp.dot(ks, g_ref[:, x].reshape(channels * ny, nz), preferred_element_type=jnp.float32)
        activ = jnp.tanh(h_ref[:, x].astype(jnp.float32)).reshape(channels * ny, nz)
        grad = (spec + skip) * (1.0 - activ * activ)
        out_ref[:, x] = grad.astype(jnp.bfloat16).reshape(channels, ny, nz)

    @pl.when(step == steps - 1)
    def _():
        for at in range(recv_ref.shape[1] // chunk):
            _, remote = copies(at)
            for copy in remote:
                copy.wait_send()
        wlocal, wremote = wide_copies()
        wlocal.wait()
        for k in range(1, others):
            wremote[k - 1].wait_send()
            origin = lax.rem(me_w + others - k, others)
            pltpu.make_async_remote_copy(
                src_ref=wstage_ref,
                dst_ref=wbuf_ref.at[origin],
                send_sem=wsend_sems.at[k],
                recv_sem=wrecv_sems.at[k],
                device_id={other: origin},
                device_id_type=mesh_ids,
            ).wait_recv()
        total = wbuf_ref[0]
        for src in range(1, others):
            total = total + wbuf_ref[src]
        skip_out_ref[...] = total * (1.0 / math.sqrt(NX * NY * NZ))


def synthesis(hidden_pre, cotangent, xsynth, table_yt, table_z, skip_weight, skip_terms, axis,
              count, other, others):
    channels, nx, ny, nz = hidden_pre.shape
    modes = table_z.shape[0]
    mz_local = xsynth.shape[0]
    steps = nx // XB
    field_spec = pl.BlockSpec((channels, XB, ny, nz), lambda i: (0, i, 0, 0))
    whole = pl.BlockSpec(memory_space=pltpu.VMEM)
    lanes = channels * ny
    return pl.pallas_call(
        functools.partial(synthesis_kernel, axis, count, other, others),
        grid=(steps,),
        in_specs=[
            field_spec,
            field_spec,
            whole,
            whole,
            pl.BlockSpec((modes, nz), lambda i: (0, 0)),
            pl.BlockSpec((channels, channels), lambda i: (0, 0)),
            whole,
        ],
        out_specs=[field_spec, pl.BlockSpec((channels, channels), lambda i: (0, 0))],
        out_shape=[
            jax.ShapeDtypeStruct(hidden_pre.shape, jnp.bfloat16),
            jax.ShapeDtypeStruct((channels, channels), jnp.float32),
        ],
        scratch_shapes=[
            pltpu.VMEM((lanes, lanes), jnp.bfloat16),
            pltpu.VMEM((count * lanes // 128, nx * mz_local, 128), jnp.float32),
            pltpu.VMEM((count, nx * mz_local, lanes), jnp.bfloat16),
            pltpu.VMEM((count, nx * mz_local, lanes), jnp.bfloat16),
            pltpu.SemaphoreType.DMA((steps,)),
            pltpu.SemaphoreType.DMA((steps, count)),
            pltpu.SemaphoreType.DMA((steps, count)),
            pltpu.VMEM((others, channels, channels), jnp.float32),
            pltpu.SemaphoreType.DMA,
            pltpu.SemaphoreType.DMA((others,)),
            pltpu.SemaphoreType.DMA((others,)),
            pltpu.VMEM((count, channels, channels), jnp.float32),
            pltpu.SemaphoreType.DMA,
            pltpu.SemaphoreType.DMA((count,)),
            pltpu.SemaphoreType.DMA((count,)),
            pltpu.VMEM((channels, channels), jnp.float32),
        ],
        compiler_params=pltpu.CompilerParams(
            dimension_semantics=("arbitrary",), vmem_limit_bytes=60 * 1024 * 1024,
            collective_id=1, has_side_effects=True,
        ),
    )(hidden_pre, cotangent, xsynth, table_yt, table_z, skip_weight, skip_terms)


def y_synthesis_body(xs_ref, tyt_ref, out_ref, stage_ref):
    mz_local, channels, modes, nx = xs_ref.shape
    blocks, _, lanes = out_ref.shape
    ny = lanes // channels
    tyt = jnp.broadcast_to(tyt_ref[...][None], (channels,) + tyt_ref.shape)
    for z in range(mz_local):
        part = jnp.einsum(
            "cym,cmx->cyx", tyt, xs_ref[z], preferred_element_type=jnp.float32
        ).astype(jnp.bfloat16).astype(jnp.float32)
        for d in range(blocks):
            piece = part[:, d * ny:(d + 1) * ny, :].reshape(channels * ny, nx).T
            for q in range(lanes // 128):
                stage_ref[d * (lanes // 128) + q, pl.ds(z, nx, stride=mz_local), :] = (
                    piece[:, q * 128:(q + 1) * 128])
    for d in range(blocks):
        for q in range(lanes // 128):
            out_ref[d, :, q * 128:(q + 1) * 128] = (
                stage_ref[d * (lanes // 128) + q].astype(out_ref.dtype))


def modes_kernel(sp_ref, w_ref, gm_ref, bs_ref):
    highest = lax.Precision.HIGHEST
    channels = sp_ref.shape[1] // 2
    width = channels * channels
    sp = sp_ref[...]
    er = lax.broadcasted_iota(jnp.int32, (channels, width), 0)
    ec = lax.broadcasted_iota(jnp.int32, (channels, width), 1)
    spread = (ec // channels == er).astype(jnp.float32)
    tile = (ec % channels == er).astype(jnp.float32)
    q_rep = jnp.dot(sp[:, channels:], tile, precision=highest, preferred_element_type=jnp.float32)
    q = sp[:, channels:]
    for c in range(channels):
        gm_ref[:, c * channels:(c + 1) * channels] = sp[:, c:c + 1] * q
    weighted = w_ref[...].astype(jnp.float32) * q_rep
    back = lax.dot_general(
        weighted, spread, (((1,), (1,)), ((), ())), precision=highest,
        preferred_element_type=jnp.float32)
    bs_ref[...] = back.astype(bs_ref.dtype)


def modes_step(spectra, weights):
    rows, both = spectra.shape
    channels = both // 2
    vmem = pl.BlockSpec(memory_space=pltpu.VMEM)
    return pl.pallas_call(
        modes_kernel,
        in_specs=[vmem, vmem],
        out_specs=[vmem, vmem],
        out_shape=[
            jax.ShapeDtypeStruct((rows, channels * channels), jnp.float32),
            jax.ShapeDtypeStruct((rows, channels), jnp.bfloat16),
        ],
    )(spectra, weights)


def per_device(hidden_pre, cotangent, mode_weight, skip_weight):
    highest = lax.Precision.HIGHEST
    channels, nx, ny, nz = hidden_pre.shape
    mode_count = mode_weight.shape[2]
    n_narrow = lax.axis_size("narrow")
    n_wide = lax.axis_size("wide")
    table_x = basis_table(mode_count, NX)
    table_y = basis_table(mode_count, NY)
    table_z = basis_table(mode_count, NZ)

    zc, gram = analysis(hidden_pre, cotangent, table_z, "narrow", n_narrow)
    mz_local = mode_count // n_narrow
    zc = zc.reshape(n_narrow, mz_local, 2 * channels, nx, ny)
    ycoeffs = jnp.einsum(
        "smcxl,nsl->mcnx", zc, table_y.reshape(mode_count, n_narrow, ny),
        preferred_element_type=jnp.float32,
    ).astype(jnp.bfloat16)
    ycoeffs = lax.all_to_all(ycoeffs, "wide", split_axis=2, concat_axis=3, tiled=True)
    spectra = jnp.einsum("zcyx,kx->zykc", ycoeffs, table_x, preferred_element_type=jnp.float32)
    z_local, y_local = (spectra.shape[0], spectra.shape[1])
    grad_modes, back_spec = modes_step(
        spectra.reshape(z_local * y_local * mode_count, 2 * channels),
        mode_weight.reshape(z_local * y_local * mode_count, channels * channels),
    )
    grad_modes = grad_modes.reshape(z_local, y_local, mode_count, channels * channels)
    back_spec = jnp.transpose(
        back_spec.reshape(z_local, y_local, mode_count, channels), (0, 3, 1, 2)
    )
    xsynth = jnp.einsum(
        "zcyk,kx->zcyx", back_spec, table_x, preferred_element_type=jnp.float32
    ).astype(jnp.bfloat16)
    xsynth = lax.all_to_all(xsynth, "wide", split_axis=3, concat_axis=2, tiled=True)
    table_zp = jnp.transpose(table_z.reshape(n_narrow, mz_local, nz), (1, 0, 2)).reshape(mode_count, nz)
    grad_hidden, grad_skip = synthesis(
        hidden_pre, cotangent, xsynth, jnp.transpose(table_y), table_zp, skip_weight, gram,
        "narrow", n_narrow, "wide", n_wide)

    return (grad_hidden, grad_modes, grad_skip)


def solution(mesh):
    in_specs = (
        P(None, "wide", "narrow", None),
        P(None, "wide", "narrow", None),
        P("narrow", "wide", None, None),
        P(),
    )
    out_specs = (P(None, "wide", "narrow", None), P("narrow", "wide", None, None), P())
    return jax.shard_map(
        per_device, mesh=mesh, in_specs=in_specs, out_specs=out_specs, check_vma=False
    )
```

```python
import functools
import math

import jax
import ml_dtypes
import numpy as np
import jax.numpy as jnp
from jax import lax
from jax.experimental import pallas as pl
from jax.experimental.pallas import tpu as pltpu
from jax.sharding import PartitionSpec as P

NX = 256
NY = 256
NZ = 256
XB = 8


def basis_table(mode_count, length):
    mode_index = np.arange(mode_count, dtype=np.int32)
    halfway = mode_count // 2
    frequency = np.where(mode_index < halfway, mode_index, mode_index - halfway + 1)
    points = np.arange(length, dtype=np.int32)
    phases = frequency[:, None] * points[None, :] % length
    angles = phases.astype(np.float32) * np.float32(2.0 * math.pi / length)
    values_table = np.where((mode_index < halfway)[:, None], np.cos(angles), np.sin(angles))
    values_table = values_table.astype(np.float32) * np.float32(1.0 / math.sqrt(length))
    return jnp.asarray(values_table.astype(ml_dtypes.bfloat16))


def _nt(a, b):
    return lax.dot_general(a, b, (((1,), (1,)), ((), ())), preferred_element_type=jnp.float32)


def analysis_kernel(axis, count, h_ref, g_ref, tz_ref, zc_ref, gram_ref, acc_ref, stage_ref,
                    slot_ref, local_sems, send_sems, recv_sems):
    mesh_ids = pl.DeviceIdType.MESH
    step = pl.program_id(0)
    steps = pl.num_programs(0)
    channels, xb, ny, nz = h_ref.shape
    width = xb * ny
    mz_local = slot_ref.shape[1] // count
    me = lax.axis_index(axis)

    def copies(at):
        slot = lax.rem(at, 2)
        cols = pl.ds(pl.multiple_of(at * width, width), width)
        local = pltpu.make_async_copy(
            slot_ref.at[slot, pl.ds(me * mz_local, mz_local)],
            zc_ref.at[me, :, :, cols],
            local_sems.at[at],
        )
        remote = []
        order = [k for pair in zip(range(1, count), range(count - 1, 0, -1)) for k in pair]
        for k in sorted(set(order), key=order.index):
            peer = lax.rem(me + k, count)
            remote.append(pltpu.make_async_remote_copy(
                src_ref=slot_ref.at[slot, pl.ds(peer * mz_local, mz_local)],
                dst_ref=zc_ref.at[me, :, :, cols],
                send_sem=send_sems.at[at, k],
                recv_sem=recv_sems.at[at, k],
                device_id={axis: peer},
                device_id_type=mesh_ids,
            ))
        return local, remote

    def wait_sent(at):
        local, remote = copies(at)
        local.wait()
        for copy in remote:
            copy.wait_send()

    @pl.when(step == 0)
    def _():
        acc_ref[...] = jnp.zeros_like(acc_ref)
        barrier = pltpu.get_barrier_semaphore()
        for k in range(1, count):
            peer = lax.rem(me + k, count)
            pl.semaphore_signal(barrier, inc=1, device_id={axis: peer}, device_id_type=mesh_ids)
        pl.semaphore_wait(barrier, count - 1)

    @pl.when(step >= 2)
    def _():
        wait_sent(step - 2)

    tz = tz_ref[...]
    li = jnp.tanh(h_ref[...].astype(jnp.float32)).astype(jnp.bfloat16)
    g = g_ref[...]
    zl = _nt(tz, li.reshape(channels * width, nz))
    zg = _nt(tz, g.reshape(channels * width, nz))
    for c in range(channels):
        stage_ref[:, c, :] = zl[:, c * width:(c + 1) * width]
        stage_ref[:, channels + c, :] = zg[:, c * width:(c + 1) * width]
    slot_ref[lax.rem(step, 2)] = stage_ref[...].astype(jnp.bfloat16)
    local, remote = copies(step)
    local.start()
    for copy in remote:
        copy.start()
    for x in range(xb):
        acc_ref[...] += _nt(li[:, x].reshape(channels * ny, nz), g[:, x].reshape(channels * ny, nz))

    @pl.when(step == steps - 1)
    def _():
        rows = channels * ny
        ri = lax.broadcasted_iota(jnp.int32, (rows, rows), 0)
        ci = lax.broadcasted_iota(jnp.int32, (rows, rows), 1)
        diag = jnp.where(ri % ny == ci % ny, acc_ref[...], 0.0)
        er = lax.broadcasted_iota(jnp.int32, (channels, rows), 0)
        ec = lax.broadcasted_iota(jnp.int32, (channels, rows), 1)
        gather = (ec // ny == er).astype(jnp.float32)
        part = jnp.dot(gather, diag, precision=lax.Precision.HIGHEST, preferred_element_type=jnp.float32)
        gram_ref[...] = lax.dot_general(
            part, gather, (((1,), (1,)), ((), ())), precision=lax.Precision.HIGHEST,
            preferred_element_type=jnp.float32)
        wait_sent(step - 1)
        wait_sent(step)
        for at in range(zc_ref.shape[3] // width):
            cols = pl.ds(at * width, width)
            for k in range(1, count):
                origin = lax.rem(me + count - k, count)
                pltpu.make_async_remote_copy(
                    src_ref=slot_ref.at[0, pl.ds(me * mz_local, mz_local)],
                    dst_ref=zc_ref.at[origin, :, :, cols],
                    send_sem=send_sems.at[at, k],
                    recv_sem=recv_sems.at[at, k],
                    device_id={axis: origin},
                    device_id_type=mesh_ids,
                ).wait_recv()


def analysis(hidden_pre, cotangent, table_z, axis, count):
    channels, nx, ny, nz = hidden_pre.shape
    modes = table_z.shape[0]
    steps = nx // XB
    field_spec = pl.BlockSpec((channels, XB, ny, nz), lambda i: (0, i, 0, 0))
    return pl.pallas_call(
        functools.partial(analysis_kernel, axis, count),
        grid=(steps,),
        in_specs=[field_spec, field_spec, pl.BlockSpec((modes, nz), lambda i: (0, 0))],
        out_specs=[
            pl.BlockSpec(memory_space=pl.ANY),
            pl.BlockSpec((channels, channels), lambda i: (0, 0)),
        ],
        out_shape=[
            jax.ShapeDtypeStruct(
                (count, modes // count, 2 * channels, nx * ny), jnp.bfloat16),
            jax.ShapeDtypeStruct((channels, channels), jnp.float32),
        ],
        scratch_shapes=[
            pltpu.VMEM((channels * ny, channels * ny), jnp.float32),
            pltpu.VMEM((modes, 2 * channels, XB * ny), jnp.float32),
            pltpu.VMEM((2, modes, 2 * channels, XB * ny), jnp.bfloat16),
            pltpu.SemaphoreType.DMA((steps,)),
            pltpu.SemaphoreType.DMA((steps, count)),
            pltpu.SemaphoreType.DMA((steps, count)),
        ],
        compiler_params=pltpu.CompilerParams(
            dimension_semantics=("arbitrary",), vmem_limit_bytes=60 * 1024 * 1024,
            collective_id=0, has_side_effects=True,
        ),
    )(hidden_pre, cotangent, table_z)


def synthesis_kernel(axis, count, other, others, h_ref, g_ref, xs_ref, tyt_ref, tz_ref, sw_ref,
                     gs_ref, out_ref, skip_out_ref, ks_ref, stage_ref, send_ref, recv_ref,
                     local_sems, send_sems, recv_sems, wbuf_ref, wlocal_sem, wsend_sems,
                     wrecv_sems, nbuf_ref, nlocal_sem, nsend_sems, nrecv_sems, wstage_ref):
    mesh_ids = pl.DeviceIdType.MESH
    step = pl.program_id(0)
    steps = pl.num_programs(0)
    channels, xb, ny, nz = h_ref.shape
    rows = channels * ny
    chunk = 2 * xb
    me = lax.axis_index(axis)
    me_w = lax.axis_index(other)

    def narrow_copies():
        local = pltpu.make_async_copy(gs_ref, nbuf_ref.at[me], nlocal_sem)
        remote = []
        for k in range(1, count):
            peer = lax.rem(me + k, count)
            remote.append(pltpu.make_async_remote_copy(
                src_ref=gs_ref,
                dst_ref=nbuf_ref.at[me],
                send_sem=nsend_sems.at[k],
                recv_sem=nrecv_sems.at[k],
                device_id={axis: peer},
                device_id_type=mesh_ids,
            ))
        return local, remote

    def wide_copies():
        local = pltpu.make_async_copy(wstage_ref, wbuf_ref.at[me_w], wlocal_sem)
        remote = []
        for k in range(1, others):
            peer = lax.rem(me_w + k, others)
            remote.append(pltpu.make_async_remote_copy(
                src_ref=wstage_ref,
                dst_ref=wbuf_ref.at[me_w],
                send_sem=wsend_sems.at[k],
                recv_sem=wrecv_sems.at[k],
                device_id={other: peer},
                device_id_type=mesh_ids,
            ))
        return local, remote

    def copies(at):
        part = pl.ds(pl.multiple_of(at * chunk, chunk), chunk)
        local = pltpu.make_async_copy(
            send_ref.at[me, part], recv_ref.at[me, part], local_sems.at[at])
        remote = []
        for k in range(1, count):
            peer = lax.rem(me + k, count)
            remote.append(pltpu.make_async_remote_copy(
                src_ref=send_ref.at[peer, part],
                dst_ref=recv_ref.at[me, part],
                send_sem=send_sems.at[at, k],
                recv_sem=recv_sems.at[at, k],
                device_id={axis: peer},
                device_id_type=mesh_ids,
            ))
        return local, remote

    @pl.when(step == 0)
    def _():
        barrier = pltpu.get_barrier_semaphore()
        for k in range(1, count):
            peer = lax.rem(me + k, count)
            pl.semaphore_signal(barrier, inc=1, device_id={axis: peer}, device_id_type=mesh_ids)
        for k in range(1, others):
            peer = lax.rem(me_w + k, others)
            pl.semaphore_signal(barrier, inc=1, device_id={other: peer}, device_id_type=mesh_ids)
        pl.semaphore_wait(barrier, count - 1 + others - 1)
        nlocal, nremote = narrow_copies()
        nlocal.start()
        for copy in nremote:
            copy.start()
        y_synthesis_body(xs_ref, tyt_ref, send_ref, stage_ref)
        for at in range(recv_ref.shape[1] // chunk):
            local, remote = copies(at)
            local.start()
            for copy in remote:
                copy.start()
        r = lax.broadcasted_iota(jnp.int32, (rows, channels), 0)
        k = lax.broadcasted_iota(jnp.int32, (rows, channels), 1)
        expand = (r // ny == k).astype(jnp.float32)
        spread = jnp.dot(expand, sw_ref[...].astype(jnp.float32), preferred_element_type=jnp.float32)
        kr = lax.broadcasted_iota(jnp.int32, (channels, rows), 0)
        kc = lax.broadcasted_iota(jnp.int32, (channels, rows), 1)
        expand_t = (kc // ny == kr).astype(jnp.float32)
        full = jnp.dot(spread, expand_t, preferred_element_type=jnp.float32)
        ri = lax.broadcasted_iota(jnp.int32, (rows, rows), 0)
        ci = lax.broadcasted_iota(jnp.int32, (rows, rows), 1)
        ks_ref[...] = jnp.where(ri % ny == ci % ny, full, 0.0).astype(ks_ref.dtype)

    @pl.when(step == 1)
    def _():
        nlocal, nremote = narrow_copies()
        nlocal.wait()
        for k in range(1, count):
            nremote[k - 1].wait_send()
            origin = lax.rem(me + count - k, count)
            pltpu.make_async_remote_copy(
                src_ref=gs_ref,
                dst_ref=nbuf_ref.at[origin],
                send_sem=nsend_sems.at[k],
                recv_sem=nrecv_sems.at[k],
                device_id={axis: origin},
                device_id_type=mesh_ids,
            ).wait_recv()
        total = nbuf_ref[0]
        for src in range(1, count):
            total = total + nbuf_ref[src]
        wstage_ref[...] = total
        wlocal, wremote = wide_copies()
        wlocal.start()
        for copy in wremote:
            copy.start()

    local, _ = copies(step)
    local.wait()
    part = pl.ds(pl.multiple_of(step * chunk, chunk), chunk)
    for k in range(1, count):
        origin = lax.rem(me + count - k, count)
        pltpu.make_async_remote_copy(
            src_ref=send_ref.at[me, part],
            dst_ref=recv_ref.at[origin, part],
            send_sem=send_sems.at[step, k],
            recv_sem=recv_sems.at[step, k],
            device_id={axis: origin},
            device_id_type=mesh_ids,
        ).wait_recv()

    tz = tz_ref[...]
    ks = ks_ref[...]
    ys = recv_ref[:, part, :].astype(jnp.float32)
    for x in range(xb):
        lo = ys[:, 2 * x, :]
        hi = ys[:, 2 * x + 1, :]
        lhs = jnp.concatenate([lo, hi], axis=0).T.astype(jnp.bfloat16)
        spec = jnp.dot(lhs, tz, preferred_element_type=jnp.float32)
        spec = spec.astype(jnp.bfloat16).astype(jnp.float32)
        skip = jnp.dot(ks, g_ref[:, x].reshape(channels * ny, nz), preferred_element_type=jnp.float32)
        activ = jnp.tanh(h_ref[:, x].astype(jnp.float32)).reshape(channels * ny, nz)
        grad = (spec + skip) * (1.0 - activ * activ)
        out_ref[:, x] = grad.astype(jnp.bfloat16).reshape(channels, ny, nz)

    @pl.when(step == steps - 1)
    def _():
        for at in range(recv_ref.shape[1] // chunk):
            _, remote = copies(at)
            for copy in remote:
                copy.wait_send()
        wlocal, wremote = wide_copies()
        wlocal.wait()
        for k in range(1, others):
            wremote[k - 1].wait_send()
            origin = lax.rem(me_w + others - k, others)
            pltpu.make_async_remote_copy(
                src_ref=wstage_ref,
                dst_ref=wbuf_ref.at[origin],
                send_sem=wsend_sems.at[k],
                recv_sem=wrecv_sems.at[k],
                device_id={other: origin},
                device_id_type=mesh_ids,
            ).wait_recv()
        total = wbuf_ref[0]
        for src in range(1, others):
            total = total + wbuf_ref[src]
        skip_out_ref[...] = total * (1.0 / math.sqrt(NX * NY * NZ))


def synthesis(hidden_pre, cotangent, xsynth, table_yt, table_z, skip_weight, skip_terms, axis,
              count, other, others):
    channels, nx, ny, nz = hidden_pre.shape
    modes = table_z.shape[0]
    mz_local = xsynth.shape[0]
    steps = nx // XB
    field_spec = pl.BlockSpec((channels, XB, ny, nz), lambda i: (0, i, 0, 0))
    whole = pl.BlockSpec(memory_space=pltpu.VMEM)
    lanes = channels * ny
    return pl.pallas_call(
        functools.partial(synthesis_kernel, axis, count, other, others),
        grid=(steps,),
        in_specs=[
            field_spec,
            field_spec,
            whole,
            whole,
            pl.BlockSpec((modes, nz), lambda i: (0, 0)),
            pl.BlockSpec((channels, channels), lambda i: (0, 0)),
            whole,
        ],
        out_specs=[field_spec, pl.BlockSpec((channels, channels), lambda i: (0, 0))],
        out_shape=[
            jax.ShapeDtypeStruct(hidden_pre.shape, jnp.bfloat16),
            jax.ShapeDtypeStruct((channels, channels), jnp.float32),
        ],
        scratch_shapes=[
            pltpu.VMEM((lanes, lanes), jnp.bfloat16),
            pltpu.VMEM((count * lanes // 128, nx * mz_local, 128), jnp.float32),
            pltpu.VMEM((count, nx * mz_local, lanes), jnp.bfloat16),
            pltpu.VMEM((count, nx * mz_local, lanes), jnp.bfloat16),
            pltpu.SemaphoreType.DMA((steps,)),
            pltpu.SemaphoreType.DMA((steps, count)),
            pltpu.SemaphoreType.DMA((steps, count)),
            pltpu.VMEM((others, channels, channels), jnp.float32),
            pltpu.SemaphoreType.DMA,
            pltpu.SemaphoreType.DMA((others,)),
            pltpu.SemaphoreType.DMA((others,)),
            pltpu.VMEM((count, channels, channels), jnp.float32),
            pltpu.SemaphoreType.DMA,
            pltpu.SemaphoreType.DMA((count,)),
            pltpu.SemaphoreType.DMA((count,)),
            pltpu.VMEM((channels, channels), jnp.float32),
        ],
        compiler_params=pltpu.CompilerParams(
            dimension_semantics=("arbitrary",), vmem_limit_bytes=60 * 1024 * 1024,
            collective_id=1, has_side_effects=True,
        ),
    )(hidden_pre, cotangent, xsynth, table_yt, table_z, skip_weight, skip_terms)


def y_synthesis_body(xs_ref, tyt_ref, out_ref, stage_ref):
    mz_local, channels, modes, nx = xs_ref.shape
    blocks, _, lanes = out_ref.shape
    ny = lanes // channels
    tyt = jnp.broadcast_to(tyt_ref[...][None], (channels,) + tyt_ref.shape)
    for z in range(mz_local):
        part = jnp.einsum(
            "cym,cmx->cyx", tyt, xs_ref[z], preferred_element_type=jnp.float32
        ).astype(jnp.bfloat16).astype(jnp.float32)
        for d in range(blocks):
            piece = part[:, d * ny:(d + 1) * ny, :].reshape(channels * ny, nx).T
            for q in range(lanes // 128):
                stage_ref[d * (lanes // 128) + q, pl.ds(z, nx, stride=mz_local), :] = (
                    piece[:, q * 128:(q + 1) * 128])
    for d in range(blocks):
        for q in range(lanes // 128):
            out_ref[d, :, q * 128:(q + 1) * 128] = (
                stage_ref[d * (lanes // 128) + q].astype(out_ref.dtype))


def modes_kernel(sp_ref, w_ref, gm_ref, bs_ref):
    highest = lax.Precision.HIGHEST
    channels = sp_ref.shape[1] // 2
    width = channels * channels
    sp = sp_ref[...]
    er = lax.broadcasted_iota(jnp.int32, (channels, width), 0)
    ec = lax.broadcasted_iota(jnp.int32, (channels, width), 1)
    spread = (ec // channels == er).astype(jnp.float32)
    tile = (ec % channels == er).astype(jnp.float32)
    q_rep = jnp.dot(sp[:, channels:], tile, precision=highest, preferred_element_type=jnp.float32)
    q = sp[:, channels:]
    for c in range(channels):
        gm_ref[:, c * channels:(c + 1) * channels] = sp[:, c:c + 1] * q
    weighted = w_ref[...].astype(jnp.float32) * q_rep
    back = lax.dot_general(
        weighted, spread, (((1,), (1,)), ((), ())), precision=highest,
        preferred_element_type=jnp.float32)
    bs_ref[...] = back.astype(bs_ref.dtype)


def modes_step(spectra, weights):
    rows, both = spectra.shape
    channels = both // 2
    vmem = pl.BlockSpec(memory_space=pltpu.VMEM)
    return pl.pallas_call(
        modes_kernel,
        in_specs=[vmem, vmem],
        out_specs=[vmem, vmem],
        out_shape=[
            jax.ShapeDtypeStruct((rows, channels * channels), jnp.float32),
            jax.ShapeDtypeStruct((rows, channels), jnp.bfloat16),
        ],
    )(spectra, weights)


def per_device(hidden_pre, cotangent, mode_weight, skip_weight):
    highest = lax.Precision.HIGHEST
    channels, nx, ny, nz = hidden_pre.shape
    mode_count = mode_weight.shape[2]
    n_narrow = lax.axis_size("narrow")
    n_wide = lax.axis_size("wide")
    table_x = basis_table(mode_count, NX)
    table_y = basis_table(mode_count, NY)
    table_z = basis_table(mode_count, NZ)

    zc, gram = analysis(hidden_pre, cotangent, table_z, "narrow", n_narrow)
    mz_local = mode_count // n_narrow
    zc = zc.reshape(n_narrow, mz_local, 2 * channels, nx, ny)
    ycoeffs = jnp.einsum(
        "smcxl,nsl->mcnx", zc, table_y.reshape(mode_count, n_narrow, ny),
        preferred_element_type=jnp.float32,
    ).astype(jnp.bfloat16)
    ycoeffs = lax.all_to_all(ycoeffs, "wide", split_axis=2, concat_axis=3, tiled=True)
    spectra = jnp.einsum("zcyx,kx->zykc", ycoeffs, table_x, preferred_element_type=jnp.float32)
    z_local, y_local = (spectra.shape[0], spectra.shape[1])
    grad_modes, back_spec = modes_step(
        spectra.reshape(z_local * y_local * mode_count, 2 * channels),
        mode_weight.reshape(z_local * y_local * mode_count, channels * channels),
    )
    grad_modes = grad_modes.reshape(z_local, y_local, mode_count, channels * channels)
    back_spec = jnp.transpose(
        back_spec.reshape(z_local, y_local, mode_count, channels), (0, 3, 1, 2)
    )
    xsynth = jnp.einsum(
        "zcyk,kx->zcyx", back_spec, table_x, preferred_element_type=jnp.float32
    ).astype(jnp.bfloat16)
    xsynth = lax.all_to_all(xsynth, "wide", split_axis=3, concat_axis=2, tiled=True)
    table_zp = jnp.transpose(table_z.reshape(n_narrow, mz_local, nz), (1, 0, 2)).reshape(mode_count, nz)
    grad_hidden, grad_skip = synthesis(
        hidden_pre, cotangent, xsynth, jnp.transpose(table_y), table_zp, skip_weight, gram,
        "narrow", n_narrow, "wide", n_wide)

    return (grad_hidden, grad_modes, grad_skip)


def solution(mesh):
    in_specs = (
        P(None, "wide", "narrow", None),
        P(None, "wide", "narrow", None),
        P("narrow", "wide", None, None),
        P(),
    )
    out_specs = (P(None, "wide", "narrow", None), P("narrow", "wide", None, None), P())
    return jax.shard_map(
        per_device, mesh=mesh, in_specs=in_specs, out_specs=out_specs, check_vma=False
    )
```
